256 devices in a mesh: comp: 2 (over y_hi), lon: 64 (over z, x, core), ch: 2 (over y_lo).
Axes of the slice: x: 4, y: 4 (y_hi: 2, y_lo: 2; y = y_hi * 2 + y_lo), z: 8, core: 2. Of those that a mesh axis runs over, the one named last changes fastest.
Arguments:
- ocean_state: bfloat16 [3, 128, 512, 256], P(None, 'ch', ('comp', 'lon')), may hold values from -6 to 6
- ocean_mask: int32 [512, 256], P(('comp', 'lon')), may hold values 0 or 1
- air_state: bfloat16 [2, 192, 256, 2, 256], P(None, 'ch', 'lon', None, 'comp'), may hold values from -6 to 6
- surface_temp: float32 [512, 256], P(('comp', 'lon')), may hold values from -6 to 6
- air_fluxes: float32 [4, 256, 2, 256], P(None, 'lon', None, 'comp'), may hold values from -6 to 6
- ocean_kernel: float32 [128, 3, 7, 7], P('ch'), may hold values from -0.5 to 0.5
- ocean_gain: float32 [128], replicated, may hold values from 0.5 to 1.5
- ocean_up: bfloat16 [128, 512], replicated, may hold values from -0.5 to 0.5
- ocean_down: bfloat16 [512, 128], replicated, may hold values from -0.25 to 0.25
- air_kernel: float32 [192, 3, 7, 7], P('ch'), may hold values from -0.5 to 0.5
- air_gain: float32 [192], replicated, may hold values from 0.5 to 1.5
- air_up: bfloat16 [192, 768], replicated, may hold values from -0.4375 to 0.4375
- air_down: bfloat16 [768, 192], replicated, may hold values from -0.21875 to 0.21875
- flux_weight: float32 [4, 128], P(None, 'ch'), may hold values from -3 to 3
- temp_weight: float32 [192], P('ch'), may hold values from -1 to 1
Outputs:
- ocean_next: bfloat16 [3, 128, 512, 256], P(None, 'ch', ('comp', 'lon'))
- air_next: bfloat16 [2, 192, 256, 2, 256], P(None, 'ch', 'lon', None, 'comp')
The draws below stay inside these ranges and needn't reach their ends.
All inputs are finite; a program needn't handle non-finite values. No bound on the sum of `ocean_mask` on one device may be relied on, other than what follows from the above.
Results may differ from the reference program's by a relative error of at most 0.007.
Values may be sent and summed in bfloat16 or wider, within the bound.
No kernel may reach another device: no remote copies, remote signals or barrier semaphores. Data moves between devices by JAX's collectives and lax.ppermute only.
A program may use at most 64 MiB of HBM per device.

```python
import jax
import jax.numpy as jnp
from jax import lax

OCEAN_LEV = 3
AIR_LEV = 2
OCEAN_CH = 128
OCEAN_HID = 512
AIR_CH = 192
AIR_HID = 768
NFLUX = 4
BAND = 4
NLAT = 256
NLON = 512
N_COMP = 2


def place_ends(array, key, least, high):
    index_at = [jax.random.randint(jax.random.fold_in(key, axis), (), 0, length) for axis, length in enumerate(array.shape)]
    longest = array.shape.index(max(array.shape))
    beside = index_at[:longest] + [(index_at[longest] + 1) % array.shape[longest]] + index_at[longest + 1:]
    return array.at[tuple(index_at)].set(least).at[tuple(beside)].set(high)


def steps_of(key, dims, cuts, low, top_value):
    level = 1.0
    for axis_at, blocks in cuts:
        heights = jax.random.uniform(jax.random.fold_in(jax.random.fold_in(key, 6), axis_at), (blocks,), jnp.float32, low / len(cuts), top_value / len(cuts))
        level = level * jnp.repeat(jnp.exp(heights), dims[axis_at] // blocks).reshape((-1,) + (1,) * (len(dims) - 1 - axis_at))
    return level


def centred(rng, dims, width, bound, pieces=(), kind=jnp.bfloat16):
    result = width * jax.random.normal(rng, dims, jnp.float32)
    if pieces:
        result = result * steps_of(rng, dims, pieces, -0.22, 0.18)
    return jnp.clip(result, -bound, bound).astype(kind)


def setup_inputs(seed: int = 0) -> dict:
    arg_keys = jax.random.split(jax.random.key(seed), 16)
    ocean_state = centred(arg_keys[0], (OCEAN_LEV, OCEAN_CH, NLON, NLAT), 1.0, 6.0, ((1, 2), (2, 128)))
    ocean_mask = place_ends((jax.random.randint(arg_keys[1], (NLON, NLAT), 0, 10) < 7).astype(jnp.int32), jax.random.fold_in(arg_keys[1], 1), 0, 1)
    air_state = centred(arg_keys[2], (AIR_LEV, AIR_CH, NLON // N_COMP, N_COMP, NLAT), 1.0, 6.0, ((1, 2), (2, 64), (4, 2)))
    surface_temp = centred(arg_keys[3], (NLON, NLAT), 1.0, 6.0, ((0, 128),), jnp.float32)
    air_fluxes = centred(arg_keys[4], (NFLUX, NLON // N_COMP, N_COMP, NLAT), 1.0, 6.0, ((1, 64), (3, 2)), jnp.float32)
    ocean_kernel = centred(arg_keys[5], (OCEAN_CH, 3, 7, 7), 147 ** -0.5, 0.5, ((0, 2),), jnp.float32)
    ocean_gain = jnp.clip(jax.random.uniform(arg_keys[6], (OCEAN_CH,), jnp.float32, 0.5, 1.5), 0.5, 1.5)
    ocean_up = centred(arg_keys[7], (OCEAN_CH, OCEAN_HID), OCEAN_CH ** -0.5, 0.5)
    ocean_down = centred(arg_keys[8], (OCEAN_HID, OCEAN_CH), OCEAN_HID ** -0.5, 0.25)
    air_kernel = centred(arg_keys[9], (AIR_CH, 3, 7, 7), 147 ** -0.5, 0.5, ((0, 2),), jnp.float32)
    air_gain = jnp.clip(jax.random.uniform(arg_keys[10], (AIR_CH,), jnp.float32, 0.5, 1.5), 0.5, 1.5)
    air_up = centred(arg_keys[11], (AIR_CH, AIR_HID), AIR_CH ** -0.5, 0.4375)
    air_down = centred(arg_keys[12], (AIR_HID, AIR_CH), AIR_HID ** -0.5, 0.21875)
    flux_weight = centred(arg_keys[13], (NFLUX, OCEAN_CH), NFLUX ** -0.5, 3.0, ((1, 2),), jnp.float32)
    temp_weight = jnp.clip(jax.random.uniform(arg_keys[14], (AIR_CH,), jnp.float32, -1.0, 1.0) * steps_of(arg_keys[14], (AIR_CH,), ((0, 2),), -0.4, 0.0), -1.0, 1.0)
    return {"ocean_state": ocean_state, "ocean_mask": ocean_mask, "air_state": air_state, "surface_temp": surface_temp, "air_fluxes": air_fluxes, "ocean_kernel": ocean_kernel, "ocean_gain": ocean_gain, "ocean_up": ocean_up, "ocean_down": ocean_down, "air_kernel": air_kernel, "air_gain": air_gain, "air_up": air_up, "air_down": air_down, "flux_weight": flux_weight, "temp_weight": temp_weight}


def periodic_conv(forced, kernel):
    channels = forced.shape[1]
    wrapped = jnp.concatenate([forced[:, :, -3:], forced, forced[:, :, :3]], axis=2)
    inputs = jnp.transpose(wrapped, (1, 0, 2, 3))[None]
    filters = kernel[:, None]
    output = lax.conv_general_dilated(inputs, filters, (1, 1, 1), ((1, 1), (0, 0), (3, 3)), dimension_numbers=('NCDHW', 'OIDHW', 'NCDHW'), feature_group_count=channels, precision=lax.Precision.HIGHEST)
    return jnp.transpose(output[0], (1, 0, 2, 3))

def channel_norm(conv_out, gain_vec):
    values = conv_out.astype(jnp.float32)
    center = lax.optimization_barrier(jnp.mean(values, axis=1, keepdims=True))
    spread = lax.optimization_barrier(jnp.mean(jnp.square(values - center), axis=1, keepdims=True))
    scaled = gain_vec.reshape((1, gain_vec.shape[0]) + (1,) * (values.ndim - 2))
    return ((values - center) * lax.rsqrt(spread + 1e-06) * scaled).astype(jnp.bfloat16)

def feed_forward(normed, up_proj, down_proj):
    hidden = jax.nn.gelu(jnp.einsum('ch,lcxy->lhxy', up_proj.astype(jnp.float32), normed.astype(jnp.float32), precision=lax.Precision.HIGHEST)).astype(jnp.bfloat16)
    return jnp.einsum('hc,lhxy->lcxy', down_proj.astype(jnp.float32), hidden.astype(jnp.float32), precision=lax.Precision.HIGHEST)

def block_update(conv_out, gain_vec, up_proj, down_proj):
    levels = conv_out.shape[0]
    channels = conv_out.shape[1]
    blocks = NLON // BAND
    tiled = jnp.transpose(conv_out.reshape(levels, channels, blocks, BAND, NLAT), (2, 0, 1, 3, 4))

    def one_block(piece):
        return feed_forward(channel_norm(piece, gain_vec), up_proj, down_proj).astype(jnp.bfloat16)
    updated = lax.map(one_block, tiled)
    return jnp.transpose(updated, (1, 2, 0, 3, 4)).reshape(levels, channels, NLON, NLAT)

def reference(ocean_state, ocean_mask, air_state, surface_temp, air_fluxes, ocean_kernel, ocean_gain, ocean_up, ocean_down, air_kernel, air_gain, air_up, air_down, flux_weight, temp_weight):
    sea_mask = ocean_mask.astype(jnp.float32)
    flux_grid = jnp.transpose(air_fluxes, (0, 2, 1, 3)).reshape(NFLUX, NLON, NLAT)
    inject = jnp.einsum('kc,kxy->cxy', flux_weight, flux_grid, precision=lax.Precision.HIGHEST)
    ocean_states = ocean_state.astype(jnp.float32)
    ocean_forced = jnp.concatenate([ocean_states[:1] + inject[None], ocean_states[1:]], axis=0) * sea_mask
    ocean_conv = periodic_conv(ocean_forced, ocean_kernel).astype(jnp.bfloat16)
    ocean_update = block_update(ocean_conv, ocean_gain, ocean_up, ocean_down)
    ocean_next = ((ocean_forced + ocean_update.astype(jnp.float32)) * sea_mask).astype(jnp.bfloat16)
    air_grid = jnp.transpose(air_state, (0, 1, 3, 2, 4)).reshape(AIR_LEV, AIR_CH, NLON, NLAT).astype(jnp.float32)
    heating = temp_weight[:, None, None] * (surface_temp * sea_mask)[None]
    air_forced = jnp.concatenate([air_grid[:1] + heating[None], air_grid[1:]], axis=0)
    air_conv = periodic_conv(air_forced, air_kernel).astype(jnp.bfloat16)
    air_update = block_update(air_conv, air_gain, air_up, air_down)
    air_final = (air_forced + air_update.astype(jnp.float32)).astype(jnp.bfloat16)
    air_next = jnp.transpose(air_final.reshape(AIR_LEV, AIR_CH, N_COMP, NLON // N_COMP, NLAT), (0, 1, 3, 2, 4))
    return (ocean_next, air_next)
```

```python
import functools

import jax
import jax.numpy as jnp
from jax import lax
from jax.experimental import pallas as pl
from jax.experimental.pallas import tpu as pltpu
from jax.sharding import PartitionSpec as P

F32 = jnp.float32
BF16 = jnp.bfloat16
LANES = 128
VMEM = pl.BlockSpec(memory_space=pltpu.VMEM)


def lane_ids(rows):
    return lax.broadcasted_iota(jnp.int32, (rows, LANES), 1)


def call(kernel, out_shape, scratch, name, flops, moved, *args):
    return pl.pallas_call(
        kernel,
        out_shape=out_shape,
        in_specs=[VMEM] * len(args),
        out_specs=jax.tree.map(lambda _: VMEM, out_shape),
        scratch_shapes=scratch,
        name=name,
        cost_estimate=pl.CostEstimate(flops=flops, bytes_accessed=moved, transcendentals=0),
    )(*args)


def pack_kernel(mask_ref, temp_ref, flux_ref, air_ref, out_ref):
    comp = lax.axis_index("comp")
    band = mask_ref.shape[0]
    fields = flux_ref.shape[0]
    for k in range(fields):
        for j in range(band):
            out_ref[k * band + j : k * band + j + 1, :] = flux_ref[k, j, pl.ds(1 - comp, 1), :]
    temp = temp_ref[...] * mask_ref[...].astype(F32)
    base = fields * band
    for s in range(2):
        out_ref[base + s * band : base + (s + 1) * band, :] = temp[:, s * LANES : (s + 1) * LANES]
    base += 2 * band
    levels, channels = air_ref.shape[1], air_ref.shape[3]
    start = jnp.where(comp == 0, LANES - 8, 0)
    lane = lane_ids(channels)
    packed = jnp.zeros((channels, LANES), F32)
    for level in range(levels):
        for h in range(2):
            for j in range(band):
                idx = (level * 2 + h) * band + j
                rolled = pltpu.roll(
                    air_ref[h, level, j].astype(F32), lax.rem(8 * idx - start + LANES, LANES), 1
                )
                packed = jnp.where(lane // 8 == idx, rolled, packed)
    out_ref[base : base + channels, :] = packed


def force_kernel(
    mask_ref, temp_ref, flux_ref, got_ref, ocean_ref, air_ref, fw_ref, tw_ref,
    fo_ref, fa_ref, edge_ref, ow_ref, oe_ref, aw_ref, ae_ref,
):
    comp = lax.axis_index("comp")
    band = mask_ref.shape[0]
    fields = flux_ref.shape[0]
    o_levels, a_levels = ocean_ref.shape[1], air_ref.shape[1]
    channels = air_ref.shape[3]
    sea = mask_ref[...].astype(F32)
    temp = temp_ref[...] * sea
    weights = fw_ref[...]
    for s in range(2):
        for i in range(band):
            sea_row = sea[i : i + 1, s * LANES : (s + 1) * LANES]
            inject = None
            for k in range(fields):
                mine = flux_ref[k, i, pl.ds(comp, 1), :]
                row = jnp.where(comp == s, mine, got_ref[k * band + i : k * band + i + 1, :])
                term = weights[:, k : k + 1] * row
                inject = term if inject is None else inject + term
            for level in range(o_levels):
                value = ocean_ref[s, level, i].astype(F32)
                if level == 0:
                    value = value + inject
                value = value * sea_row
                fo_ref[s, level, i] = value
                small = value.astype(BF16)
                at = (s * o_levels + level) * (band - 1)
                if i < band - 1:
                    ow_ref[at + i] = small
                if i > 0:
                    oe_ref[at + i - 1] = small
    base = fields * band
    heat = tw_ref[...]
    start = jnp.where(comp == 0, 0, LANES - 8)
    lane = lane_ids(8)
    edge_temp = jnp.zeros((8, LANES), F32)
    for h in range(2):
        for j in range(band):
            mine = [temp[j : j + 1, s * LANES : (s + 1) * LANES] for s in range(2)]
            here = jnp.where(comp == 0, mine[0], mine[1])
            there = jnp.where(comp == 0, mine[1], mine[0])
            got_here = got_ref[pl.ds(base + comp * band + j, 1), :]
            got_there = got_ref[pl.ds(base + (1 - comp) * band + j, 1), :]
            row = jnp.where(comp == h, here, got_here)
            beyond = jnp.where(comp == h, there, got_there)
            idx = h * band + j
            rolled = pltpu.roll(
                jnp.broadcast_to(beyond, (8, LANES)), lax.rem(8 * idx - start + LANES, LANES), 1
            )
            edge_temp = jnp.where(lane // 8 == idx, rolled, edge_temp)
            for level in range(a_levels):
                value = air_ref[h, level, j].astype(F32)
                if level == 0:
                    value = value + heat * row
                fa_ref[h, level, j] = value
                small = value.astype(BF16)
                at = (h * a_levels + level) * (band - 1)
                if j < band - 1:
                    aw_ref[at + j] = small
                if j > 0:
                    ae_ref[at + j - 1] = small
    base += 2 * band
    edge = got_ref[base : base + channels, :] + heat * edge_temp[0:1, :]
    edge_ref[...] = edge
    last = 2 * a_levels * (band - 1)
    aw_ref[last] = edge.astype(BF16)
    ae_ref[last] = edge.astype(BF16)


def lat_swap(data_ref, edge_ref, count):
    levels, channels = data_ref.shape[1], data_ref.shape[3]
    lane = lane_ids(channels)
    for level in range(levels):
        for i in range(count):
            edge_ref[0, level, i] = jnp.where(lane < 64, data_ref[1, level, i], 0.0)
            edge_ref[1, level, i] = jnp.where(lane >= 64, data_ref[0, level, i], 0.0)


def unpack_edge(packed, idx, channels):
    comp = lax.axis_index("comp")
    start = jnp.where(comp == 0, 0, LANES - 8)
    rolled = pltpu.roll(packed, lax.rem(start - 8 * idx + 2 * LANES, LANES), 1)
    return jnp.where(lane_ids(channels) // 8 == start // 8, rolled, 0.0)


def convolve(data_ref, edge_ref, weight_ref, start_ref, out_ref, columns, band):
    levels, channels = data_ref.shape[1], data_ref.shape[3]
    lane = lane_ids(8)

    def step(at, carry):
        half = lax.rem(at, 2)
        rows = pl.ds(pl.multiple_of(at // 2 * 8, 8), 8)
        weight = weight_ref[rows, :]
        acc = [
            [None if start_ref is None else start_ref[half, level, i, rows] for i in range(band)]
            for level in range(levels)
        ]
        for d in range(7):
            off = d - 3
            shifted = {}
            for level in range(levels):
                for slot, x in enumerate(columns):
                    value = data_ref[half, level, slot, rows]
                    if off > 0:
                        beyond = edge_ref[half, level, slot, rows]
                        value = pltpu.roll(jnp.where(lane < off, beyond, value), LANES - off, 1)
                    elif off < 0:
                        beyond = edge_ref[half, level, slot, rows]
                        value = pltpu.roll(
                            jnp.where(lane >= LANES + off, beyond, value), -off, 1
                        )
                    shifted[level, x] = value
            for a in range(3):
                for b in range(7):
                    pairs = [
                        (level, i)
                        for level in range(levels)
                        for i in range(band)
                        if (level + a - 1, i + b - 3) in shifted
                    ]
                    if not pairs:
                        continue
                    tap = a * 49 + b * 7 + d
                    scale = jnp.broadcast_to(weight[:, tap : tap + 1], (8, LANES))
                    for level, i in pairs:
                        term = scale * shifted[level + a - 1, i + b - 3]
                        old = acc[level][i]
                        acc[level][i] = term if old is None else old + term
        for level in range(levels):
            for i in range(band):
                out_ref[half, level, i, rows] = acc[level][i]
        return carry

    lax.fori_loop(0, channels // 8 * 2, step, 0)


def own_ocean_kernel(data_ref, weight_ref, out_ref, edge_ref):
    band = data_ref.shape[2]
    lat_swap(data_ref, edge_ref, band)
    convolve(data_ref, edge_ref, weight_ref, None, out_ref, range(band), band)


def own_air_kernel(data_ref, packed_ref, weight_ref, out_ref, edge_ref):
    _, levels, band, channels, _ = data_ref.shape
    for h in range(2):
        for level in range(levels):
            for j in range(band):
                idx = (level * 2 + h) * band + j
                edge_ref[h, level, j] = unpack_edge(packed_ref[...], idx, channels)
    convolve(data_ref, edge_ref, weight_ref, None, out_ref, range(band), band)


def halo_columns(band):
    return [-3, -2, -1] + [band, band + 1, band + 2]


def halo_ocean_kernel(west_ref, east_ref, weight_ref, start_ref, out_ref, data_ref, edge_ref, acc_ref):
    _, levels, band, _, _ = start_ref.shape
    for s in range(2):
        for level in range(levels):
            for i in range(3):
                at = (s * levels + level) * 3 + i
                data_ref[s, level, i] = west_ref[at].astype(F32)
                data_ref[s, level, 3 + i] = east_ref[at].astype(F32)
    lat_swap(data_ref, edge_ref, 6)
    convolve(data_ref, edge_ref, weight_ref, start_ref, acc_ref, halo_columns(band), band)
    out_ref[...] = acc_ref[...].astype(BF16)


def halo_air_kernel(west_ref, east_ref, weight_ref, start_ref, out_ref, data_ref, edge_ref, acc_ref):
    _, levels, band, channels, _ = start_ref.shape
    lon = lax.axis_index("lon")
    swap_west = jnp.where(lon == 0, 1, 0)
    swap_east = jnp.where(lon == lax.axis_size("lon") - 1, 1, 0)
    last = 2 * levels * 3
    west_edge = west_ref[last].astype(F32)
    east_edge = east_ref[last].astype(F32)
    for h in range(2):
        west_h = jnp.abs(h - swap_west)
        east_h = jnp.abs(h - swap_east)
        for level in range(levels):
            for i in range(3):
                data_ref[h, level, i] = west_ref[(west_h * levels + level) * 3 + i].astype(F32)
                data_ref[h, level, 3 + i] = east_ref[(east_h * levels + level) * 3 + i].astype(F32)
                edge_ref[h, level, i] = unpack_edge(
                    west_edge, (level * 2 + west_h) * band + i + band - 3, channels
                )
                edge_ref[h, level, 3 + i] = unpack_edge(
                    east_edge, (level * 2 + east_h) * band + i, channels
                )
    convolve(data_ref, edge_ref, weight_ref, start_ref, acc_ref, halo_columns(band), band)
    out_ref[...] = acc_ref[...].astype(BF16)


def mlp_kernel(masked, *refs):
    own_ref, other_ref, gain_ref, up_ref, down_ref, forced_ref = refs[:6]
    mask_ref = refs[6] if masked else None
    out_ref, values_ref = refs[-2:]
    _, levels, band, channels, _ = own_ref.shape
    ch = lax.axis_index("ch")
    total = 2 * channels

    def step(at, carry):
        level = at // band
        i = lax.rem(at, band)
        mine = pl.ds(pl.multiple_of(ch * channels, channels), channels)
        theirs = pl.ds(pl.multiple_of((1 - ch) * channels, channels), channels)
        for s in range(2):
            lanes = slice(s * LANES, (s + 1) * LANES)
            values_ref[mine, lanes] = own_ref[s, level, i].astype(F32)
            values_ref[theirs, lanes] = other_ref[s, level, i].astype(F32)
        values = values_ref[...]
        center = jnp.sum(values, axis=0, keepdims=True) * (1.0 / total)
        values = values - center
        spread = jnp.sum(values * values, axis=0, keepdims=True) * (1.0 / total)
        normed = (values * lax.rsqrt(spread + 1e-06) * gain_ref[...]).astype(BF16)
        raw = jnp.dot(up_ref[...], normed, preferred_element_type=F32)
        inner = raw * (0.7978845608028654 + 0.035677408136300125 * (raw * raw))
        half = 0.5 * raw
        hidden = (half + half * jnp.tanh(inner)).astype(BF16)
        down = down_ref[mine, :]
        if masked:
            mask = mask_ref[...]
            picked = lax.broadcasted_iota(jnp.int32, mask.shape, 0) == i
            sea = jnp.sum(jnp.where(picked, mask.astype(F32), 0.0), axis=0, keepdims=True)
        update = jnp.dot(down, hidden, preferred_element_type=F32).astype(BF16).astype(F32)
        for s in range(2):
            lanes = slice(s * LANES, (s + 1) * LANES)
            result = forced_ref[s, level, i] + update[:, lanes]
            if masked:
                result = result * sea[:, lanes]
            out_ref[s, level, i] = result.astype(BF16)
        return carry

    lax.fori_loop(0, levels * band, step, 0)


def ring(count, step):
    return [(i, (i + step) % count) for i in range(count)]


def per_device(
    ocean_state, ocean_mask, air_state, surface_temp, air_fluxes, ocean_kernel, ocean_gain, ocean_up,
    ocean_down, air_kernel, air_gain, air_up, air_down, flux_weight, temp_weight,
):
    o_levels, o_ch, band, lats = ocean_state.shape
    a_levels, a_ch = air_state.shape[:2]
    fields = air_fluxes.shape[0]
    shape = jax.ShapeDtypeStruct

    ocean_grid = jnp.transpose(
        ocean_state.reshape(o_levels, o_ch, band, 2, LANES), (3, 0, 2, 1, 4)
    )
    air_grid = jnp.transpose(air_state, (3, 0, 2, 1, 4))
    o_grid = (2, o_levels, band, o_ch, LANES)
    a_grid = (2, a_levels, band, a_ch, LANES)

    rows = fields * band + 2 * band + a_ch
    packed = call(
        pack_kernel, shape((rows, LANES), F32), [], "pack", 10**5, 10**6,
        ocean_mask, surface_temp, air_fluxes, air_grid,
    )
    got = lax.ppermute(packed, "comp", ring(2, 1))
    o_rim = (2 * o_levels * 3, o_ch, LANES)
    a_rim = (2 * a_levels * 3 + 1, a_ch, LANES)
    ocean_forced, air_forced, edge, o_west, o_east, a_west, a_east = call(
        force_kernel,
        (
            shape(o_grid, F32), shape(a_grid, F32), shape((a_ch, LANES), F32),
            shape(o_rim, BF16), shape(o_rim, BF16), shape(a_rim, BF16), shape(a_rim, BF16),
        ),
        [], "force", 10**6, 4 * 10**6,
        ocean_mask, surface_temp, air_fluxes, got, ocean_grid, air_grid,
        flux_weight.T, temp_weight[:, None],
    )
    bands = lax.axis_size("comp") * lax.axis_size("lon")
    lons = lax.axis_size("lon")
    from_west_o = lax.ppermute(o_east, ("comp", "lon"), ring(bands, 1))
    from_east_o = lax.ppermute(o_west, ("comp", "lon"), ring(bands, -1))
    from_west_a = lax.ppermute(a_east, "lon", ring(lons, 1))
    from_east_a = lax.ppermute(a_west, "lon", ring(lons, -1))

    o_weight = ocean_kernel.reshape(o_ch, -1)
    a_weight = air_kernel.reshape(a_ch, -1)
    o_own = call(
        own_ocean_kernel, shape(o_grid, F32), [pltpu.VMEM(o_grid, F32)], "own_ocean",
        3 * 10**9, 10**6, ocean_forced, o_weight,
    )
    a_own = call(
        own_air_kernel, shape(a_grid, F32), [pltpu.VMEM(a_grid, F32)], "own_air",
        3 * 10**9, 10**6, air_forced, edge, a_weight,
    )
    o_six = (2, o_levels, 6, o_ch, LANES)
    a_six = (2, a_levels, 6, a_ch, LANES)
    o_conv = call(
        halo_ocean_kernel, shape(o_grid, BF16),
        [pltpu.VMEM(o_six, F32), pltpu.VMEM(o_six, F32), pltpu.VMEM(o_grid, F32)], "halo_ocean",
        2 * 10**9, 10**6, from_west_o, from_east_o, o_weight, o_own,
    )
    o_other = lax.ppermute(o_conv, "ch", ring(2, 1))
    a_conv = call(
        halo_air_kernel, shape(a_grid, BF16),
        [pltpu.VMEM(a_six, F32), pltpu.VMEM(a_six, F32), pltpu.VMEM(a_grid, F32)], "halo_air",
        2 * 10**9, 10**6, from_west_a, from_east_a, a_weight, a_own,
    )
    a_other = lax.ppermute(a_conv, "ch", ring(2, 1))

    o_next = call(
        functools.partial(mlp_kernel, True), shape(o_grid, BF16),
        [pltpu.VMEM((2 * o_ch, 2 * LANES), F32)], "mlp_ocean", 10**9, 3 * 10**6,
        o_conv, o_other, ocean_gain[:, None], ocean_up.T, ocean_down.T, ocean_forced, ocean_mask,
    )
    a_next = call(
        functools.partial(mlp_kernel, False), shape(a_grid, BF16),
        [pltpu.VMEM((2 * a_ch, 2 * LANES), F32)], "mlp_air", 10**9, 3 * 10**6,
        a_conv, a_other, air_gain[:, None], air_up.T, air_down.T, air_forced,
    )
    ocean_next = jnp.transpose(o_next, (1, 3, 2, 0, 4)).reshape(ocean_state.shape)
    air_next = jnp.transpose(a_next, (1, 3, 2, 0, 4))
    return (ocean_next, air_next)


def solution(mesh):
    in_specs = (
        P(None, "ch", ("comp", "lon"), None),
        P(("comp", "lon"), None),
        P(None, "ch", "lon", None, "comp"),
        P(("comp", "lon"), None),
        P(None, "lon", None, "comp"),
        P("ch", None, None, None),
        P(),
        P(),
        P(),
        P("ch", None, None, None),
        P(),
        P(),
        P(),
        P(None, "ch"),
        P("ch"),
    )
    out_specs = (P(None, "ch", ("comp", "lon"), None), P(None, "ch", "lon", None, "comp"))
    return jax.shard_map(
        per_device, mesh=mesh, in_specs=in_specs, out_specs=out_specs, check_vma=False
    )
```

```python
import functools

import jax
import jax.numpy as jnp
from jax import lax
from jax.experimental import pallas as pl
from jax.experimental.pallas import tpu as pltpu
from jax.sharding import PartitionSpec as P

F32 = jnp.float32
BF16 = jnp.bfloat16
LANES = 128
VMEM = pl.BlockSpec(memory_space=pltpu.VMEM)


def lane_ids(rows):
    return lax.broadcasted_iota(jnp.int32, (rows, LANES), 1)


def call(kernel, out_shape, scratch, name, flops, moved, *args):
    return pl.pallas_call(
        kernel,
        out_shape=out_shape,
        in_specs=[VMEM] * len(args),
        out_specs=jax.tree.map(lambda _: VMEM, out_shape),
        scratch_shapes=scratch,
        name=name,
        cost_estimate=pl.CostEstimate(flops=flops, bytes_accessed=moved, transcendentals=0),
    )(*args)


def pack_kernel(mask_ref, temp_ref, flux_ref, air_ref, out_ref):
    comp = lax.axis_index("comp")
    band = mask_ref.shape[0]
    fields = flux_ref.shape[0]
    for k in range(fields):
        for j in range(band):
            out_ref[k * band + j : k * band + j + 1, :] = flux_ref[k, j, pl.ds(1 - comp, 1), :]
    temp = temp_ref[...] * mask_ref[...].astype(F32)
    base = fields * band
    for s in range(2):
        out_ref[base + s * band : base + (s + 1) * band, :] = temp[:, s * LANES : (s + 1) * LANES]
    base += 2 * band
    levels, channels = air_ref.shape[1], air_ref.shape[3]
    start = jnp.where(comp == 0, LANES - 8, 0)
    lane = lane_ids(channels)
    packed = jnp.zeros((channels, LANES), F32)
    for level in range(levels):
        for h in range(2):
            for j in range(band):
                idx = (level * 2 + h) * band + j
                rolled = pltpu.roll(
                    air_ref[h, level, j].astype(F32), lax.rem(8 * idx - start + LANES, LANES), 1
                )
                packed = jnp.where(lane // 8 == idx, rolled, packed)
    out_ref[base : base + channels, :] = packed


def force_kernel(
    mask_ref, temp_ref, flux_ref, got_ref, ocean_ref, air_ref, fw_ref, tw_ref,
    fo_ref, fa_ref, ob_ref, ab_ref, edge_ref, ow_ref, oe_ref, aw_ref, ae_ref,
):
    comp = lax.axis_index("comp")
    band = mask_ref.shape[0]
    fields = flux_ref.shape[0]
    o_levels, a_levels = ocean_ref.shape[1], air_ref.shape[1]
    channels = air_ref.shape[3]
    sea = mask_ref[...].astype(F32)
    temp = temp_ref[...] * sea
    weights = fw_ref[...]
    for s in range(2):
        for i in range(band):
            sea_row = sea[i : i + 1, s * LANES : (s + 1) * LANES]
            inject = None
            for k in range(fields):
                mine = flux_ref[k, i, pl.ds(comp, 1), :]
                row = jnp.where(comp == s, mine, got_ref[k * band + i : k * band + i + 1, :])
                term = weights[:, k : k + 1] * row
                inject = term if inject is None else inject + term
            for level in range(o_levels):
                value = ocean_ref[s, level, i].astype(F32)
                if level == 0:
                    value = value + inject
                value = value * sea_row
                if level == 0:
                    fo_ref[s, i] = value
                small = value.astype(BF16)
                ob_ref[s, level, i] = small
                at = (s * o_levels + level) * (band - 1)
                if i < band - 1:
                    ow_ref[at + i] = small
                if i > 0:
                    oe_ref[at + i - 1] = small
    base = fields * band
    heat = tw_ref[...]
    start = jnp.where(comp == 0, 0, LANES - 8)
    lane = lane_ids(8)
    edge_temp = jnp.zeros((8, LANES), F32)
    for h in range(2):
        for j in range(band):
            mine = [temp[j : j + 1, s * LANES : (s + 1) * LANES] for s in range(2)]
            here = jnp.where(comp == 0, mine[0], mine[1])
            there = jnp.where(comp == 0, mine[1], mine[0])
            got_here = got_ref[pl.ds(base + comp * band + j, 1), :]
            got_there = got_ref[pl.ds(base + (1 - comp) * band + j, 1), :]
            row = jnp.where(comp == h, here, got_here)
            beyond = jnp.where(comp == h, there, got_there)
            idx = h * band + j
            rolled = pltpu.roll(
                jnp.broadcast_to(beyond, (8, LANES)), lax.rem(8 * idx - start + LANES, LANES), 1
            )
            edge_temp = jnp.where(lane // 8 == idx, rolled, edge_temp)
            for level in range(a_levels):
                value = air_ref[h, level, j].astype(F32)
                if level == 0:
                    value = value + heat * row
                if level == 0:
                    fa_ref[h, j] = value
                small = value.astype(BF16)
                ab_ref[h, level, j] = small
                at = (h * a_levels + level) * (band - 1)
                if j < band - 1:
                    aw_ref[at + j] = small
                if j > 0:
                    ae_ref[at + j - 1] = small
    base += 2 * band
    edge = got_ref[base : base + channels, :] + heat * edge_temp[0:1, :]
    edge_ref[...] = edge
    last = 2 * a_levels * (band - 1)
    aw_ref[last] = edge.astype(BF16)
    ae_ref[last] = edge.astype(BF16)


def unpack_edge(packed, idx, shift, lane):
    comp = lax.axis_index("comp")
    start = lax.rem(jnp.where(comp == 0, 0, LANES - 8) + shift, LANES)
    rolled = pltpu.roll(packed, lax.rem(start - 8 * idx + 2 * LANES, LANES), 1)
    return jnp.where(lane // 8 == start // 8, rolled, 0.0)


TAPS = 7


def toeplitz_kernel(taps_ref, out_ref):
    groups, pairs, rows, depth = out_ref.shape
    channels = groups * 8
    levels = pairs // 2
    window = taps_ref.shape[1]
    taps = taps_ref[...].astype(BF16)
    row = lax.broadcasted_iota(jnp.int32, (window, depth), 0)
    lane = lax.broadcasted_iota(jnp.int32, (window, depth), 1)
    from_level = lane // 80
    from_lon = lane // 8 - from_level * 10
    same = (lax.broadcasted_iota(jnp.int32, (8, depth), 1) & 7) == lax.broadcasted_iota(
        jnp.int32, (8, depth), 0
    )

    def step(pair, carry):
        level = pair // 2
        parts = []
        for side in range(2):
            a = from_level - level + 1
            b = from_lon - (lax.rem(pair, 2) * 2 + side)
            hit = (
                (from_level < levels)
                & (a >= 0) & (a <= 2) & (b >= 0) & (b < TAPS) & (a * TAPS + b == row)
            )
            choose = jnp.where(hit, 1.0, 0.0).astype(BF16)
            parts.append(jnp.dot(taps, choose, preferred_element_type=F32))
        for g in range(groups):
            tiles = [
                jnp.where(same, part[d * channels + g * 8 : d * channels + g * 8 + 8], 0.0)
                for part in parts
                for d in range(TAPS)
            ]
            out_ref[g, pair] = jnp.concatenate(tiles, axis=0).astype(BF16)
        return carry

    lax.fori_loop(0, pairs, step, 0)


def conv_ocean_kernel(own_ref, west_ref, east_ref, matrix_ref, out_ref, product_ref):
    _, levels, band, count, _ = own_ref.shape
    depth = matrix_ref.shape[-1]
    lane = lane_ids(8)
    for sub in range(count // 8):
        rows = slice(sub * 8, sub * 8 + 8)
        halves = []
        for s in range(2):
            tiles = []
            for level in range(levels):
                at = (s * levels + level) * 3
                tiles += [west_ref[at + i, rows].astype(F32) for i in range(3)]
                tiles += [own_ref[s, level, i, rows].astype(F32) for i in range(band)]
                tiles += [east_ref[at + i, rows].astype(F32) for i in range(3)]
            if depth > len(tiles) * 8:
                tiles.append(jnp.zeros((depth - len(tiles) * 8, LANES), F32))
            halves.append(jnp.concatenate(tiles, axis=0))
        data = jnp.concatenate(halves, axis=1).astype(BF16)
        matrix = matrix_ref[sub].reshape(-1, depth)
        product_ref[...] = jnp.dot(matrix, data, preferred_element_type=F32)
        for level in range(levels):
            for i in range(band):
                base = (level * band + i) * TAPS
                sums = [None, None]
                for d in range(TAPS):
                    at = slice((base + d) * 8, (base + d) * 8 + 8)
                    first = product_ref[at, :LANES]
                    second = product_ref[at, LANES:]
                    off = d - 3
                    if off > 0:
                        first, second = (
                            pltpu.roll(jnp.where(lane < off, second, first), LANES - off, 1),
                            pltpu.roll(jnp.where(lane < off, 0.0, second), LANES - off, 1),
                        )
                    elif off < 0:
                        first, second = (
                            pltpu.roll(jnp.where(lane >= LANES + off, 0.0, first), -off, 1),
                            pltpu.roll(jnp.where(lane >= LANES + off, first, second), -off, 1),
                        )
                    sums = [
                        part if old is None else old + part
                        for old, part in zip(sums, (first, second))
                    ]
                for s in range(2):
                    out_ref[s, level, i, rows] = sums[s].astype(BF16)


def conv_air_kernel(own_ref, west_ref, east_ref, packed_ref, matrix_ref, out_ref, product_ref):
    _, levels, band, count, _ = own_ref.shape
    depth = matrix_ref.shape[-1]
    lon = lax.axis_index("lon")
    swap_west = jnp.where(lon == 0, 1, 0)
    swap_east = jnp.where(lon == lax.axis_size("lon") - 1, 1, 0)
    last = 2 * levels * 3
    lane = lane_ids(8)
    for sub in range(count // 8):
        rows = slice(sub * 8, sub * 8 + 8)
        packed = [packed_ref[rows], west_ref[last, rows].astype(F32), east_ref[last, rows].astype(F32)]
        columns = []
        edges = []
        for h in range(2):
            west_h = jnp.abs(h - swap_west)
            east_h = jnp.abs(h - swap_east)
            tiles = []
            beyond = []
            for level in range(levels):
                for i in range(3):
                    tiles.append(west_ref[(west_h * levels + level) * 3 + i, rows].astype(F32))
                    beyond.append((1, (level * 2 + west_h) * band + i + band - 3))
                for i in range(band):
                    tiles.append(own_ref[h, level, i, rows].astype(F32))
                    beyond.append((0, (level * 2 + h) * band + i))
                for i in range(3):
                    tiles.append(east_ref[(east_h * levels + level) * 3 + i, rows].astype(F32))
                    beyond.append((2, (level * 2 + east_h) * band + i))
            edges.append([unpack_edge(packed[who], idx, h * 64, lane) for who, idx in beyond])
            columns.append(tiles)
        columns.append([first + second for first, second in zip(*edges)])
        pad = depth - len(columns[0]) * 8
        if pad:
            columns = [tiles + [jnp.zeros((pad, LANES), F32)] for tiles in columns]
        data = jnp.concatenate(
            [jnp.concatenate(tiles, axis=0) for tiles in columns], axis=1
        ).astype(BF16)
        matrix = matrix_ref[sub].reshape(-1, depth)
        product_ref[...] = jnp.dot(matrix, data, preferred_element_type=F32)
        for level in range(levels):
            for i in range(band):
                base = (level * band + i) * TAPS
                sums = [None, None]
                for d in range(TAPS):
                    at = slice((base + d) * 8, (base + d) * 8 + 8)
                    off = d - 3
                    edge = product_ref[at, 2 * LANES :] if off else None
                    for h in range(2):
                        part = product_ref[at, h * LANES : (h + 1) * LANES]
                        if off:
                            here = edge if h == 0 else pltpu.roll(edge, 64, 1)
                            inside = lane < off if off > 0 else lane >= LANES + off
                            part = pltpu.roll(jnp.where(inside, here, part), (LANES - off) % LANES, 1)
                        sums[h] = part if sums[h] is None else sums[h] + part
                for h in range(2):
                    out_ref[h, level, i, rows] = sums[h].astype(BF16)


def convolution(kernel, name, own, west, east, packed, matrix):
    _, levels, band, channels, _ = own.shape
    groups, pairs, rows, depth = matrix.shape
    count = 16
    lane_tiles = 2 if packed is None else 3
    grid_spec = pl.BlockSpec((2, levels, band, count, LANES), lambda g: (0, 0, 0, g, 0))
    rim_spec = pl.BlockSpec((west.shape[0], count, LANES), lambda g: (0, g, 0))
    args = [own, west, east]
    specs = [grid_spec, rim_spec, rim_spec]
    if packed is not None:
        args.append(packed)
        specs.append(pl.BlockSpec((count, LANES), lambda g: (g, 0)))
    args.append(matrix)
    specs.append(pl.BlockSpec((count // 8, pairs, rows, depth), lambda g: (g, 0, 0, 0)))
    return pl.pallas_call(
        kernel,
        grid=(channels // count,),
        out_shape=jax.ShapeDtypeStruct(own.shape, BF16),
        in_specs=specs,
        out_specs=grid_spec,
        scratch_shapes=[pltpu.VMEM((pairs * rows, lane_tiles * LANES), F32)],
        name=name,
        cost_estimate=pl.CostEstimate(flops=2 * 10**9, bytes_accessed=4 * 10**6, transcendentals=0),
    )(*args)


def mlp_kernel(masked, *refs):
    own_ref, other_ref, gain_ref, up_ref, down_ref, top_ref, forced_ref = refs[:7]
    mask_ref = refs[7] if masked else None
    out_ref, values_ref = refs[-2:]
    _, levels, band, channels, _ = own_ref.shape
    ch = lax.axis_index("ch")
    total = 2 * channels

    def step(at, carry):
        level = at // band
        i = lax.rem(at, band)
        mine = pl.ds(pl.multiple_of(ch * channels, channels), channels)
        theirs = pl.ds(pl.multiple_of((1 - ch) * channels, channels), channels)
        for s in range(2):
            lanes = slice(s * LANES, (s + 1) * LANES)
            values_ref[mine, lanes] = own_ref[s, level, i].astype(F32)
            values_ref[theirs, lanes] = other_ref[s, level, i].astype(F32)
        values = values_ref[...]
        center = jnp.sum(values, axis=0, keepdims=True) * (1.0 / total)
        values = values - center
        spread = jnp.sum(values * values, axis=0, keepdims=True) * (1.0 / total)
        normed = (values * lax.rsqrt(spread + 1e-06) * gain_ref[...]).astype(BF16)
        raw = jnp.dot(up_ref[...], normed, preferred_element_type=F32)
        inner = raw * (0.7978845608028654 + 0.035677408136300125 * (raw * raw))
        half = 0.5 * raw
        hidden = (half + half * jnp.tanh(inner)).astype(BF16)
        down = down_ref[mine, :]
        if masked:
            mask = mask_ref[...]
            picked = lax.broadcasted_iota(jnp.int32, mask.shape, 0) == i
            sea = jnp.sum(jnp.where(picked, mask.astype(F32), 0.0), axis=0, keepdims=True)
        update = jnp.dot(down, hidden, preferred_element_type=F32).astype(BF16).astype(F32)
        for s in range(2):
            lanes = slice(s * LANES, (s + 1) * LANES)
            forced = jnp.where(level == 0, top_ref[s, i], forced_ref[s, level, i].astype(F32))
            result = forced + update[:, lanes]
            if masked:
                result = result * sea[:, lanes]
            out_ref[s, level, i] = result.astype(BF16)
        return carry

    lax.fori_loop(0, levels * band, step, 0)


def toeplitz(kernel, levels, name):
    channels = kernel.shape[0]
    taps = jnp.transpose(kernel, (3, 0, 1, 2)).reshape(TAPS * channels, 3 * TAPS)
    return call(
        toeplitz_kernel, jax.ShapeDtypeStruct((channels // 8, levels * 2, 2 * TAPS * 8, 256), BF16),
        [], name, 10**9, 3 * 10**6, taps,
    )


def ring(count, step):
    return [(i, (i + step) % count) for i in range(count)]


def per_device(
    ocean_state, ocean_mask, air_state, surface_temp, air_fluxes, ocean_kernel, ocean_gain, ocean_up,
    ocean_down, air_kernel, air_gain, air_up, air_down, flux_weight, temp_weight,
):
    o_levels, o_ch, band, lats = ocean_state.shape
    a_levels, a_ch = air_state.shape[:2]
    fields = air_fluxes.shape[0]
    shape = jax.ShapeDtypeStruct

    ocean_grid = jnp.transpose(
        ocean_state.reshape(o_levels, o_ch, band, 2, LANES), (3, 0, 2, 1, 4)
    )
    air_grid = jnp.transpose(air_state, (3, 0, 2, 1, 4))
    o_grid = (2, o_levels, band, o_ch, LANES)
    a_grid = (2, a_levels, band, a_ch, LANES)

    rows = fields * band + 2 * band + a_ch
    packed = call(
        pack_kernel, shape((rows, LANES), F32), [], "pack", 10**5, 10**6,
        ocean_mask, surface_temp, air_fluxes, air_grid,
    )
    got = lax.ppermute(packed, "comp", ring(2, 1))
    o_rim = (2 * o_levels * 3, o_ch, LANES)
    a_rim = (2 * a_levels * 3 + 1, a_ch, LANES)
    ocean_top, air_top, ocean_forced, air_forced, edge, o_west, o_east, a_west, a_east = call(
        force_kernel,
        (
            shape((2, band, o_ch, LANES), F32), shape((2, band, a_ch, LANES), F32),
            shape(o_grid, BF16), shape(a_grid, BF16), shape((a_ch, LANES), F32),
            shape(o_rim, BF16), shape(o_rim, BF16), shape(a_rim, BF16), shape(a_rim, BF16),
        ),
        [], "force", 10**6, 4 * 10**6,
        ocean_mask, surface_temp, air_fluxes, got, ocean_grid, air_grid,
        flux_weight.T, temp_weight[:, None],
    )
    bands = lax.axis_size("comp") * lax.axis_size("lon")
    lons = lax.axis_size("lon")
    from_west_o = lax.ppermute(o_east, ("comp", "lon"), ring(bands, 1))
    from_east_o = lax.ppermute(o_west, ("comp", "lon"), ring(bands, -1))
    from_west_a = lax.ppermute(a_east, "lon", ring(lons, 1))
    from_east_a = lax.ppermute(a_west, "lon", ring(lons, -1))

    o_matrix = toeplitz(ocean_kernel, o_levels, "matrix_ocean")
    a_matrix = toeplitz(air_kernel, a_levels, "matrix_air")
    o_conv = convolution(
        conv_ocean_kernel, "conv_ocean", ocean_forced, from_west_o, from_east_o, None, o_matrix
    )
    o_other = lax.ppermute(o_conv, "ch", ring(2, 1))
    a_conv = convolution(
        conv_air_kernel, "conv_air", air_forced, from_west_a, from_east_a, edge, a_matrix
    )
    a_other = lax.ppermute(a_conv, "ch", ring(2, 1))

    o_next = call(
        functools.partial(mlp_kernel, True), shape(o_grid, BF16),
        [pltpu.VMEM((2 * o_ch, 2 * LANES), F32)], "mlp_ocean", 10**9, 3 * 10**6,
        o_conv, o_other, ocean_gain[:, None], ocean_up.T, ocean_down.T, ocean_top, ocean_forced,
        ocean_mask,
    )
    a_next = call(
        functools.partial(mlp_kernel, False), shape(a_grid, BF16),
        [pltpu.VMEM((2 * a_ch, 2 * LANES), F32)], "mlp_air", 10**9, 3 * 10**6,
        a_conv, a_other, air_gain[:, None], air_up.T, air_down.T, air_top, air_forced,
    )
    ocean_next = jnp.transpose(o_next, (1, 3, 2, 0, 4)).reshape(ocean_state.shape)
    air_next = jnp.transpose(a_next, (1, 3, 2, 0, 4))
    return (ocean_next, air_next)


def solution(mesh):
    in_specs = (
        P(None, "ch", ("comp", "lon"), None),
        P(("comp", "lon"), None),
        P(None, "ch", "lon", None, "comp"),
        P(("comp", "lon"), None),
        P(None, "lon", None, "comp"),
        P("ch", None, None, None),
        P(),
        P(),
        P(),
        P("ch", None, None, None),
        P(),
        P(),
        P(),
        P(None, "ch"),
        P("ch"),
    )
    out_specs = (P(None, "ch", ("comp", "lon"), None), P(None, "ch", "lon", None, "comp"))
    return jax.shard_map(
        per_device, mesh=mesh, in_specs=in_specs, out_specs=out_specs, check_vma=False
    )
```

```python
import functools

import jax
import jax.numpy as jnp
from jax import lax
from jax.experimental import pallas as pl
from jax.experimental.pallas import tpu as pltpu
from jax.sharding import PartitionSpec as P

F32 = jnp.float32
BF16 = jnp.bfloat16
LANES = 128
VMEM = pl.BlockSpec(memory_space=pltpu.VMEM)


def lane_ids(rows):
    return lax.broadcasted_iota(jnp.int32, (rows, LANES), 1)


def call(kernel, out_shape, scratch, name, flops, moved, *args):
    return pl.pallas_call(
        kernel,
        out_shape=out_shape,
        in_specs=[VMEM] * len(args),
        out_specs=jax.tree.map(lambda _: VMEM, out_shape),
        scratch_shapes=scratch,
        name=name,
        cost_estimate=pl.CostEstimate(flops=flops, bytes_accessed=moved, transcendentals=0),
    )(*args)


def rows_of(fields, band):
    temp = fields * band * 2
    return temp, temp + 2 * band, temp + 4 * band


def pack_kernel(mask_ref, temp_ref, flux_ref, air_ref, out_ref):
    comp = lax.axis_index("comp")
    fields, band = flux_ref.shape[:2]
    temp_row, sea_row, edge_row = rows_of(fields, band)
    for k in range(fields):
        for j in range(band):
            at = (k * band + j) * 2
            out_ref[at : at + 2, :] = flux_ref[k, j]
    sea = mask_ref[...].astype(F32)
    temp = temp_ref[...] * sea
    for s in range(2):
        lanes = slice(s * LANES, (s + 1) * LANES)
        out_ref[temp_row + s * band : temp_row + (s + 1) * band, :] = temp[:, lanes]
        out_ref[sea_row + s * band : sea_row + (s + 1) * band, :] = sea[:, lanes]
    levels, channels = air_ref.shape[1], air_ref.shape[3]
    start = jnp.where(comp == 0, LANES - 8, 0)
    lane = lane_ids(channels)
    packed = jnp.zeros((channels, LANES), F32)
    for level in range(levels):
        for h in range(2):
            for j in range(band):
                idx = (level * 2 + h) * band + j
                rolled = pltpu.roll(
                    air_ref[h, level, j].astype(F32), lax.rem(8 * idx - start + LANES, LANES), 1
                )
                packed = jnp.where(lane // 8 == idx, rolled, packed)
    out_ref[edge_row : edge_row + channels, :] = packed


def fill_surface(mask_ref, temp_ref, surface_ref):
    band = mask_ref.shape[0]
    sea = mask_ref[...].astype(F32)
    temp = temp_ref[...] * sea
    for s in range(2):
        lanes = slice(s * LANES, (s + 1) * LANES)
        surface_ref[s * band : (s + 1) * band, :] = temp[:, lanes]
        surface_ref[(2 + s) * band : (3 + s) * band, :] = sea[:, lanes]


def inject_of(flux_ref, got_ref, fw_ref, half, s, i):
    comp = lax.axis_index("comp")
    fields, band = flux_ref.shape[:2]
    total = None
    for k in range(fields):
        mine = flux_ref[k, i, pl.ds(half, 1), :]
        theirs = got_ref[pl.ds((k * band + i) * 2 + half, 1), :]
        term = fw_ref[:, k : k + 1] * jnp.where(comp == s, mine, theirs)
        total = term if total is None else total + term
    return total


def temp_of(surface_ref, got_ref, fields, band, h, s, j):
    comp = lax.axis_index("comp")
    temp_row = rows_of(fields, band)[0]
    mine = surface_ref[pl.ds(s * band + j, 1), :]
    theirs = got_ref[pl.ds(temp_row + s * band + j, 1), :]
    return jnp.where(comp == h, mine, theirs)


def force_halo_kernel(
    mask_ref, temp_ref, flux_ref, got_ref, ocean_ref, swapped_ref, air_ref, fw_ref, tw_ref,
    even_ref, odd_ref, edge_ref, surface_ref,
):
    comp = lax.axis_index("comp")
    lon = lax.axis_index("lon")
    parity = lax.rem(lon, 2)
    at_end = (lon == 0) | (lon == lax.axis_size("lon") - 1)
    fields, band = flux_ref.shape[:2]
    o_levels, o_ch = ocean_ref.shape[1], ocean_ref.shape[3]
    a_levels, a_ch = air_ref.shape[1], air_ref.shape[3]
    temp_row, sea_row, edge_row = rows_of(fields, band)
    fill_surface(mask_ref, temp_ref, surface_ref)
    heat = tw_ref[...]

    start = jnp.where(comp == 0, 0, LANES - 8)
    lane = lane_ids(8)
    edge_temp = jnp.zeros((8, LANES), F32)
    for h in range(2):
        for j in range(band):
            idx = h * band + j
            row = temp_of(surface_ref, got_ref, fields, band, h, 1 - comp, j)
            rolled = pltpu.roll(
                jnp.broadcast_to(row, (8, LANES)), lax.rem(8 * idx - start + LANES, LANES), 1
            )
            edge_temp = jnp.where(lane // 8 == idx, rolled, edge_temp)
    edge = got_ref[edge_row : edge_row + a_ch, :] + heat * edge_temp[0:1, :]
    edge_ref[...] = edge

    first_air = 2 * o_levels * 3 * o_ch
    for out_ref, offset, outer in ((even_ref, 1 - parity, None), (odd_ref, parity, at_end)):
        for j in range(3):
            col = j + offset
            half = comp if outer is None else jnp.where(outer, 1 - comp, comp)
            for s in range(2):
                inject = inject_of(flux_ref, got_ref, fw_ref, half, s, col)
                sea = surface_ref[pl.ds((2 + s) * band + col, 1), :]
                if outer is not None:
                    sea = jnp.where(outer, got_ref[pl.ds(sea_row + s * band + col, 1), :], sea)
                for level in range(o_levels):
                    tile = (s * o_levels + level) * 3 + j
                    value = ocean_ref[s, level, col].astype(F32)
                    if outer is not None:
                        value = jnp.where(outer, swapped_ref[tile].astype(F32), value)
                    if level == 0:
                        value = value + inject
                    out_ref[tile * o_ch : (tile + 1) * o_ch, :] = (value * sea).astype(BF16)
            for h in range(2):
                row = temp_of(surface_ref, got_ref, fields, band, h, comp, col)
                for level in range(a_levels):
                    value = air_ref[h, level, col].astype(F32)
                    if level == 0:
                        value = value + heat * row
                    at = first_air + ((h * a_levels + level) * 3 + j) * a_ch
                    out_ref[at : at + a_ch, :] = value.astype(BF16)
        at = first_air + 2 * a_levels * 3 * a_ch
        out_ref[at : at + a_ch, :] = edge.astype(BF16)


def force_own_kernel(
    mask_ref, temp_ref, flux_ref, got_ref, ocean_ref, air_ref, fw_ref, tw_ref,
    fo_ref, fa_ref, ob_ref, ab_ref, surface_ref,
):
    comp = lax.axis_index("comp")
    fields, band = flux_ref.shape[:2]
    o_levels, a_levels = ocean_ref.shape[1], air_ref.shape[1]
    fill_surface(mask_ref, temp_ref, surface_ref)
    heat = tw_ref[...]
    for s in range(2):
        for i in range(band):
            inject = inject_of(flux_ref, got_ref, fw_ref, comp, s, i)
            at = (2 + s) * band + i
            sea = surface_ref[at : at + 1, :]
            row = temp_of(surface_ref, got_ref, fields, band, s, comp, i)
            for level in range(o_levels):
                value = ocean_ref[s, level, i].astype(F32)
                if level == 0:
                    value = (value + inject) * sea
                    fo_ref[s, i] = value
                else:
                    value = value * sea
                ob_ref[s, level, i] = value.astype(BF16)
            for level in range(a_levels):
                value = air_ref[s, level, i].astype(F32)
                if level == 0:
                    value = value + heat * row
                    fa_ref[s, i] = value
                ab_ref[s, level, i] = value.astype(BF16)


def unpack_edge(packed, idx, shift, lane):
    comp = lax.axis_index("comp")
    start = lax.rem(jnp.where(comp == 0, 0, LANES - 8) + shift, LANES)
    rolled = pltpu.roll(packed, lax.rem(start - 8 * idx + 2 * LANES, LANES), 1)
    return jnp.where(lane // 8 == start // 8, rolled, 0.0)


TAPS = 7


def toeplitz_kernel(levels, taps_ref, out_ref):
    groups, _, rows, depth = out_ref.shape
    channels = groups * 8
    pair = pl.program_id(0)
    window = taps_ref.shape[1]
    taps = taps_ref[...].astype(BF16)
    row = lax.broadcasted_iota(jnp.int32, (window, depth), 0)
    lane = lax.broadcasted_iota(jnp.int32, (window, depth), 1)
    from_level = lane // 80
    from_lon = lane // 8 - from_level * 10
    same = (lax.broadcasted_iota(jnp.int32, (8, depth), 1) & 7) == lax.broadcasted_iota(
        jnp.int32, (8, depth), 0
    )
    level = pair // 2
    parts = []
    for side in range(2):
        a = from_level - level + 1
        b = from_lon - (lax.rem(pair, 2) * 2 + side)
        hit = (
            (from_level < levels)
            & (a >= 0) & (a <= 2) & (b >= 0) & (b < TAPS) & (a * TAPS + b == row)
        )
        choose = jnp.where(hit, 1.0, 0.0).astype(BF16)
        parts.append(jnp.dot(taps, choose, preferred_element_type=F32))
    for g in range(groups):
        tiles = [
            jnp.where(same, part[d * channels + g * 8 : d * channels + g * 8 + 8], 0.0)
            for part in parts
            for d in range(TAPS)
        ]
        out_ref[g, 0] = jnp.concatenate(tiles, axis=0).astype(BF16)


def rim_tile(even_ref, odd_ref, at, count):
    rows = pl.ds(pl.multiple_of(at, 16), count)
    return even_ref[rows, :].astype(F32), odd_ref[rows, :].astype(F32)


def conv_ocean_kernel(own_ref, even_ref, odd_ref, matrix_ref, out_ref, product_ref):
    _, levels, band, count, _ = own_ref.shape
    depth = matrix_ref.shape[-1]
    lane = lane_ids(8)
    channels = pl.num_programs(0) * count
    first = pl.program_id(0) * count
    inner = lax.rem(lax.axis_index("lon"), 2) == 1
    columns = []
    for s in range(2):
        tiles = []
        for level in range(levels):
            west, east = [], []
            for i in range(3):
                at = ((s * levels + level) * 3 + i) * channels + first
                even, odd = rim_tile(even_ref, odd_ref, at, count)
                west.append(jnp.where(inner, even, odd))
                east.append(jnp.where(inner, odd, even))
            own = [own_ref[s, level, i].astype(F32) for i in range(band)]
            tiles += west + own + east
        columns.append(tiles)
    for sub in range(count // 8):
        rows = slice(sub * 8, sub * 8 + 8)
        halves = []
        for tiles in columns:
            tiles = [tile[rows] for tile in tiles]
            if depth > len(tiles) * 8:
                tiles.append(jnp.zeros((depth - len(tiles) * 8, LANES), F32))
            halves.append(jnp.concatenate(tiles, axis=0))
        data = jnp.concatenate(halves, axis=1).astype(BF16)
        matrix = matrix_ref[sub].reshape(-1, depth)
        product_ref[...] = jnp.dot(matrix, data, preferred_element_type=F32)
        for level in range(levels):
            for i in range(band):
                base = (level * band + i) * TAPS
                sums = [None, None]
                for d in range(TAPS):
                    at = slice((base + d) * 8, (base + d) * 8 + 8)
                    first = product_ref[at, :LANES]
                    second = product_ref[at, LANES:]
                    off = d - 3
                    if off > 0:
                        first, second = (
                            pltpu.roll(jnp.where(lane < off, second, first), LANES - off, 1),
                            pltpu.roll(jnp.where(lane < off, 0.0, second), LANES - off, 1),
                        )
                    elif off < 0:
                        first, second = (
                            pltpu.roll(jnp.where(lane >= LANES + off, 0.0, first), -off, 1),
                            pltpu.roll(jnp.where(lane >= LANES + off, first, second), -off, 1),
                        )
                    sums = [
                        part if old is None else old + part
                        for old, part in zip(sums, (first, second))
                    ]
                for s in range(2):
                    out_ref[s, level, i, rows] = sums[s].astype(BF16)


def conv_air_kernel(own_ref, even_ref, odd_ref, packed_ref, matrix_ref, out_ref, product_ref):
    _, levels, band, count, _ = own_ref.shape
    depth = matrix_ref.shape[-1]
    lon = lax.axis_index("lon")
    inner = lax.rem(lon, 2) == 1
    swap_west = jnp.where(lon == 0, 1, 0)
    swap_east = jnp.where(lon == lax.axis_size("lon") - 1, 1, 0)
    channels = pl.num_programs(0) * count
    first = pl.program_id(0) * count + even_ref.shape[0] - (2 * levels * 3 + 1) * channels
    lane = lane_ids(8)
    even, odd = rim_tile(even_ref, odd_ref, first + 2 * levels * 3 * channels, count)
    edge_tiles = [packed_ref[...], jnp.where(inner, even, odd), jnp.where(inner, odd, even)]
    all_tiles = []
    beyond = []
    for h in range(2):
        west_h = jnp.abs(h - swap_west)
        east_h = jnp.abs(h - swap_east)
        tiles = []
        for level in range(levels):
            west, east = [], []
            for i in range(3):
                at = first + ((west_h * levels + level) * 3 + i) * channels
                even, odd = rim_tile(even_ref, odd_ref, at, count)
                west.append(jnp.where(inner, even, odd))
                at = first + ((east_h * levels + level) * 3 + i) * channels
                even, odd = rim_tile(even_ref, odd_ref, at, count)
                east.append(jnp.where(inner, odd, even))
            tiles += west + [own_ref[h, level, i].astype(F32) for i in range(band)] + east
            beyond += [(h, 1, (level * 2 + west_h) * band + i + band - 3) for i in range(3)]
            beyond += [(h, 0, (level * 2 + h) * band + i) for i in range(band)]
            beyond += [(h, 2, (level * 2 + east_h) * band + i) for i in range(3)]
        all_tiles.append(tiles)
    for sub in range(count // 8):
        rows = slice(sub * 8, sub * 8 + 8)
        columns = [[tile[rows] for tile in tiles] for tiles in all_tiles]
        packed = [tile[rows] for tile in edge_tiles]
        edges = [
            [unpack_edge(packed[who], idx, h * 64, lane) for at_h, who, idx in beyond if at_h == h]
            for h in range(2)
        ]
        columns.append([one + two for one, two in zip(*edges)])
        pad = depth - len(columns[0]) * 8
        if pad:
            columns = [tiles + [jnp.zeros((pad, LANES), F32)] for tiles in columns]
        data = jnp.concatenate(
            [jnp.concatenate(tiles, axis=0) for tiles in columns], axis=1
        ).astype(BF16)
        matrix = matrix_ref[sub].reshape(-1, depth)
        product_ref[...] = jnp.dot(matrix, data, preferred_element_type=F32)
        for level in range(levels):
            for i in range(band):
                base = (level * band + i) * TAPS
                sums = [None, None]
                for d in range(TAPS):
                    at = slice((base + d) * 8, (base + d) * 8 + 8)
                    off = d - 3
                    edge = product_ref[at, 2 * LANES :] if off else None
                    for h in range(2):
                        part = product_ref[at, h * LANES : (h + 1) * LANES]
                        if off:
                            here = edge if h == 0 else pltpu.roll(edge, 64, 1)
                            inside = lane < off if off > 0 else lane >= LANES + off
                            part = pltpu.roll(jnp.where(inside, here, part), (LANES - off) % LANES, 1)
                        sums[h] = part if sums[h] is None else sums[h] + part
                for h in range(2):
                    out_ref[h, level, i, rows] = sums[h].astype(BF16)


def convolution(kernel, name, own, even, odd, packed, matrix):
    _, levels, band, channels, _ = own.shape
    groups, pairs, rows, depth = matrix.shape
    count = 16
    lane_tiles = 2 if packed is None else 3
    grid_spec = pl.BlockSpec((2, levels, band, count, LANES), lambda g: (0, 0, 0, g, 0))
    rim_spec = pl.BlockSpec(even.shape, lambda g: (0, 0))
    args = [own, even, odd]
    specs = [grid_spec, rim_spec, rim_spec]
    if packed is not None:
        args.append(packed)
        specs.append(pl.BlockSpec((count, LANES), lambda g: (g, 0)))
    args.append(matrix)
    specs.append(pl.BlockSpec((count // 8, pairs, rows, depth), lambda g: (g, 0, 0, 0)))
    return pl.pallas_call(
        kernel,
        grid=(channels // count,),
        out_shape=jax.ShapeDtypeStruct(own.shape, BF16),
        in_specs=specs,
        out_specs=grid_spec,
        scratch_shapes=[pltpu.VMEM((pairs * rows, lane_tiles * LANES), F32)],
        name=name,
        cost_estimate=pl.CostEstimate(flops=2 * 10**9, bytes_accessed=4 * 10**6, transcendentals=0),
    )(*args)


def mlp_kernel(masked, *refs):
    own_ref, other_ref, gain_ref, up_ref, down_ref, top_ref, forced_ref = refs[:7]
    mask_ref = refs[7] if masked else None
    out_ref, values_ref = refs[-2:]
    _, levels, band, channels, _ = own_ref.shape
    ch = lax.axis_index("ch")
    total = 2 * channels

    def row(at, slot):
        level = at // band
        i = lax.rem(at, band)
        mine = pl.ds(pl.multiple_of(ch * channels, channels), channels)
        theirs = pl.ds(pl.multiple_of((1 - ch) * channels, channels), channels)
        for s in range(2):
            lanes = slice(s * LANES, (s + 1) * LANES)
            values_ref[slot, mine, lanes] = own_ref[s, level, i].astype(F32)
            values_ref[slot, theirs, lanes] = other_ref[s, level, i].astype(F32)
        values = values_ref[slot]
        center = jnp.sum(values, axis=0, keepdims=True) * (1.0 / total)
        values = values - center
        spread = jnp.sum(values * values, axis=0, keepdims=True) * (1.0 / total)
        normed = (values * lax.rsqrt(spread + 1e-06) * gain_ref[...]).astype(BF16)
        raw = jnp.dot(up_ref[...], normed, preferred_element_type=F32)
        inner = raw * (0.7978845608028654 + 0.035677408136300125 * (raw * raw))
        doubled = (raw + raw * jnp.tanh(inner)).astype(BF16)
        update = jnp.dot(down_ref[mine, :], doubled, preferred_element_type=F32) * 0.5
        update = update.astype(BF16).astype(F32)
        if masked:
            mask = mask_ref[...]
            picked = lax.broadcasted_iota(jnp.int32, mask.shape, 0) == i
            sea = jnp.sum(jnp.where(picked, mask.astype(F32), 0.0), axis=0, keepdims=True)
        for s in range(2):
            lanes = slice(s * LANES, (s + 1) * LANES)
            forced = jnp.where(level == 0, top_ref[s, i], forced_ref[s, level, i].astype(F32))
            result = forced + update[:, lanes]
            if masked:
                result = result * sea[:, lanes]
            out_ref[s, level, i] = result.astype(BF16)

    def step(at, carry):
        row(at * 2, 0)
        row(at * 2 + 1, 1)
        return carry

    lax.fori_loop(0, levels * band // 2, step, 0)


def taps_of(kernel):
    return jnp.transpose(kernel, (3, 0, 1, 2)).reshape(TAPS * kernel.shape[0], 3 * TAPS)


def toeplitz(taps, levels, name):
    groups = taps.shape[0] // TAPS // 8
    block = (groups, 1, 2 * TAPS * 8, 256)
    return pl.pallas_call(
        functools.partial(toeplitz_kernel, levels),
        grid=(levels * 2,),
        out_shape=jax.ShapeDtypeStruct((groups, levels * 2) + block[2:], BF16),
        in_specs=[pl.BlockSpec(taps.shape, lambda p: (0, 0))],
        out_specs=pl.BlockSpec(block, lambda p: (0, p, 0, 0)),
        name=name,
        cost_estimate=pl.CostEstimate(flops=10**9, bytes_accessed=3 * 10**6, transcendentals=0),
    )(taps)


def pairs_of(count, first):
    pairs = []
    for i in range(first, count + first, 2):
        pairs += [(i % count, (i + 1) % count), ((i + 1) % count, i % count)]
    return pairs


def ring(count, step):
    return [(i, (i + step) % count) for i in range(count)]


def per_device(
    ocean_state, ocean_mask, air_state, surface_temp, air_fluxes, ocean_kernel, ocean_gain, ocean_up,
    ocean_down, air_kernel, air_gain, air_up, air_down, flux_weight, temp_weight,
):
    o_levels, o_ch, band, lats = ocean_state.shape
    a_levels, a_ch = air_state.shape[:2]
    fields = air_fluxes.shape[0]
    shape = jax.ShapeDtypeStruct

    ocean_grid = jnp.transpose(
        ocean_state.reshape(o_levels, o_ch, band, 2, LANES), (3, 0, 2, 1, 4)
    )
    air_grid = jnp.transpose(air_state, (3, 0, 2, 1, 4))
    o_grid = (2, o_levels, band, o_ch, LANES)
    a_grid = (2, a_levels, band, a_ch, LANES)

    lons = lax.axis_size("lon")
    bands = lax.axis_size("comp") * lons
    lon = lax.axis_index("lon")
    outward = lax.dynamic_slice_in_dim(ocean_grid, jnp.where(lon == 0, 0, band - 3), 3, 2)
    swaps = [(i, (i + lons) % bands) for i in (0, lons - 1, lons, bands - 1)]
    rows = rows_of(fields, band)[-1] + a_ch
    packed = call(
        pack_kernel, shape((rows, LANES), F32), [], "pack", 10**5, 10**6,
        ocean_mask, surface_temp, air_fluxes, air_grid,
    )
    got = lax.ppermute(packed, "comp", ring(2, 1))
    o_tiles = 2 * o_levels * 3
    swapped = lax.ppermute(outward.reshape(o_tiles, o_ch, LANES), ("comp", "lon"), swaps)
    rim = (o_tiles * o_ch + (2 * a_levels * 3 + 1) * a_ch, LANES)
    surface = pltpu.VMEM((4 * band, LANES), F32)
    weights = (flux_weight.T, temp_weight[:, None])
    even_out, odd_out, edge = call(
        force_halo_kernel,
        (shape(rim, BF16), shape(rim, BF16), shape((a_ch, LANES), F32)),
        [surface], "force_halo", 10**6, 4 * 10**6,
        ocean_mask, surface_temp, air_fluxes, got, ocean_grid, swapped, air_grid, *weights,
    )
    even = lax.ppermute(even_out, "lon", pairs_of(lons, 0))
    odd = lax.ppermute(odd_out, "lon", pairs_of(lons, 1))
    ocean_top, air_top, ocean_forced, air_forced = call(
        force_own_kernel,
        (
            shape((2, band, o_ch, LANES), F32), shape((2, band, a_ch, LANES), F32),
            shape(o_grid, BF16), shape(a_grid, BF16),
        ),
        [surface], "force_own", 10**6, 4 * 10**6,
        ocean_mask, surface_temp, air_fluxes, got, ocean_grid, air_grid, *weights,
    )

    o_taps, a_taps, o_gain, a_gain, o_up, a_up, o_down, a_down = lax.optimization_barrier(
        (
            taps_of(ocean_kernel), taps_of(air_kernel), ocean_gain[:, None], air_gain[:, None],
            ocean_up.T, air_up.T, ocean_down.T, air_down.T,
        )
    )
    o_matrix = toeplitz(o_taps, o_levels, "matrix_ocean")
    a_matrix = toeplitz(a_taps, a_levels, "matrix_air")
    a_conv = convolution(conv_air_kernel, "conv_air", air_forced, even, odd, edge, a_matrix)
    a_other = lax.ppermute(a_conv, "ch", ring(2, 1))
    o_conv = convolution(conv_ocean_kernel, "conv_ocean", ocean_forced, even, odd, None, o_matrix)
    o_other = lax.ppermute(o_conv, "ch", ring(2, 1))

    a_next = call(
        functools.partial(mlp_kernel, False), shape(a_grid, BF16),
        [pltpu.VMEM((2, 2 * a_ch, 2 * LANES), F32)], "mlp_air", 10**9, 3 * 10**6,
        a_conv, a_other, a_gain, a_up, a_down, air_top, air_forced,
    )
    o_next = call(
        functools.partial(mlp_kernel, True), shape(o_grid, BF16),
        [pltpu.VMEM((2, 2 * o_ch, 2 * LANES), F32)], "mlp_ocean", 10**9, 3 * 10**6,
        o_conv, o_other, o_gain, o_up, o_down, ocean_top, ocean_forced, ocean_mask,
    )
    ocean_next = jnp.transpose(o_next, (1, 3, 2, 0, 4)).reshape(ocean_state.shape)
    air_next = jnp.transpose(a_next, (1, 3, 2, 0, 4))
    return (ocean_next, air_next)


def solution(mesh):
    in_specs = (
        P(None, "ch", ("comp", "lon"), None),
        P(("comp", "lon"), None),
        P(None, "ch", "lon", None, "comp"),
        P(("comp", "lon"), None),
        P(None, "lon", None, "comp"),
        P("ch", None, None, None),
        P(),
        P(),
        P(),
        P("ch", None, None, None),
        P(),
        P(),
        P(),
        P(None, "ch"),
        P("ch"),
    )
    out_specs = (P(None, "ch", ("comp", "lon"), None), P(None, "ch", "lon", None, "comp"))
    return jax.shard_map(
        per_device, mesh=mesh, in_specs=in_specs, out_specs=out_specs, check_vma=False
    )
```

```python
import functools

import jax
import jax.numpy as jnp
from jax import lax
from jax.experimental import pallas as pl
from jax.experimental.pallas import tpu as pltpu
from jax.sharding import PartitionSpec as P

F32 = jnp.float32
BF16 = jnp.bfloat16
LANES = 128
PARAMS = pltpu.CompilerParams(vmem_limit_bytes=24 * 2**20)
VMEM = pl.BlockSpec(memory_space=pltpu.VMEM)


def lane_ids(rows):
    return lax.broadcasted_iota(jnp.int32, (rows, LANES), 1)


def column(row):
    n = row.shape[1]
    same = lax.broadcasted_iota(jnp.int32, (n, n), 0) == lax.broadcasted_iota(jnp.int32, (n, n), 1)
    return jnp.sum(jnp.where(same, row, 0.0), axis=1, keepdims=True)


def call(kernel, out_shape, scratch, name, flops, moved, *args):
    return pl.pallas_call(
        kernel,
        out_shape=out_shape,
        in_specs=[VMEM] * len(args),
        out_specs=jax.tree.map(lambda _: VMEM, out_shape),
        scratch_shapes=scratch,
        name=name,
        compiler_params=PARAMS,
        cost_estimate=pl.CostEstimate(flops=flops, bytes_accessed=moved, transcendentals=0),
    )(*args)


def rows_of(fields, band):
    temp = fields * band * 2
    return temp, temp + 2 * band, temp + 4 * band


def pack_kernel(mask_ref, temp_ref, flux_ref, air_ref, out_ref):
    comp = lax.axis_index("comp")
    fields, band = flux_ref.shape[:2]
    temp_row, sea_row, edge_row = rows_of(fields, band)
    for k in range(fields):
        for j in range(band):
            at = (k * band + j) * 2
            out_ref[at : at + 2, :] = flux_ref[k, j]
    sea = mask_ref[...].astype(F32)
    temp = temp_ref[...] * sea
    for s in range(2):
        lanes = slice(s * LANES, (s + 1) * LANES)
        out_ref[temp_row + s * band : temp_row + (s + 1) * band, :] = temp[:, lanes]
        out_ref[sea_row + s * band : sea_row + (s + 1) * band, :] = sea[:, lanes]
    levels, channels = air_ref.shape[1], air_ref.shape[3]
    start = jnp.where(comp == 0, LANES - 8, 0)
    lane = lane_ids(channels)
    packed = jnp.zeros((channels, LANES), F32)
    for level in range(levels):
        for h in range(2):
            for j in range(band):
                idx = (level * 2 + h) * band + j
                rolled = pltpu.roll(
                    air_ref[h, level, j].astype(F32), (8 * idx - start + LANES) & (LANES - 1), 1
                )
                packed = jnp.where((lane >> 3) == idx, rolled, packed)
    out_ref[edge_row : edge_row + channels, :] = packed


def fill_surface(mask_ref, temp_ref, surface_ref):
    band = mask_ref.shape[0]
    sea = mask_ref[...].astype(F32)
    temp = temp_ref[...] * sea
    for s in range(2):
        lanes = slice(s * LANES, (s + 1) * LANES)
        surface_ref[s * band : (s + 1) * band, :] = temp[:, lanes]
        surface_ref[(2 + s) * band : (3 + s) * band, :] = sea[:, lanes]


def inject_of(flux_ref, got_ref, fw, half, s, i):
    comp = lax.axis_index("comp")
    fields, band = flux_ref.shape[:2]
    total = None
    for k in range(fields):
        mine = flux_ref[k, i, pl.ds(half, 1), :]
        theirs = got_ref[pl.ds((k * band + i) * 2 + half, 1), :]
        term = fw[k] * jnp.where(comp == s, mine, theirs)
        total = term if total is None else total + term
    return total


def temp_of(surface_ref, got_ref, fields, band, h, s, j):
    comp = lax.axis_index("comp")
    temp_row = rows_of(fields, band)[0]
    mine = surface_ref[pl.ds(s * band + j, 1), :]
    theirs = got_ref[pl.ds(temp_row + s * band + j, 1), :]
    return jnp.where(comp == h, mine, theirs)


def force_halo_kernel(
    mask_ref, temp_ref, flux_ref, got_ref, ocean_ref, swapped_ref, air_ref, fw_ref, tw_ref,
    even_ref, odd_ref, edge_ref, surface_ref,
):
    comp = lax.axis_index("comp")
    lon = lax.axis_index("lon")
    parity = (lon & 1)
    at_end = (lon == 0) | (lon == lax.axis_size("lon") - 1)
    fields, band = flux_ref.shape[:2]
    o_levels, o_ch = ocean_ref.shape[1], ocean_ref.shape[3]
    a_levels, a_ch = air_ref.shape[1], air_ref.shape[3]
    temp_row, sea_row, edge_row = rows_of(fields, band)
    fill_surface(mask_ref, temp_ref, surface_ref)
    heat = column(tw_ref[...])
    fw = [column(fw_ref[k : k + 1, :]) for k in range(fields)]

    start = jnp.where(comp == 0, 0, LANES - 8)
    lane = lane_ids(8)
    edge_temp = jnp.zeros((8, LANES), F32)
    for h in range(2):
        for j in range(band):
            idx = h * band + j
            row = temp_of(surface_ref, got_ref, fields, band, h, 1 - comp, j)
            rolled = pltpu.roll(
                jnp.broadcast_to(row, (8, LANES)), (8 * idx - start + LANES) & (LANES - 1), 1
            )
            edge_temp = jnp.where((lane >> 3) == idx, rolled, edge_temp)
    edge = got_ref[edge_row : edge_row + a_ch, :] + heat * edge_temp[0:1, :]
    edge_ref[...] = edge

    first_air = 2 * o_levels * 3 * o_ch
    for out_ref, offset, outer in ((even_ref, 1 - parity, None), (odd_ref, parity, at_end)):
        for j in range(3):
            col = j + offset
            half = comp if outer is None else jnp.where(outer, 1 - comp, comp)
            for s in range(2):
                inject = inject_of(flux_ref, got_ref, fw, half, s, col)
                sea = surface_ref[pl.ds((2 + s) * band + col, 1), :]
                if outer is not None:
                    sea = jnp.where(outer, got_ref[pl.ds(sea_row + s * band + col, 1), :], sea)
                for level in range(o_levels):
                    tile = (s * o_levels + level) * 3 + j
                    value = ocean_ref[s, level, col].astype(F32)
                    if outer is not None:
                        value = jnp.where(outer, swapped_ref[tile].astype(F32), value)
                    if level == 0:
                        value = value + inject
                    out_ref[tile * o_ch : (tile + 1) * o_ch, :] = (value * sea).astype(BF16)
            for h in range(2):
                row = temp_of(surface_ref, got_ref, fields, band, h, comp, col)
                for level in range(a_levels):
                    value = air_ref[h, level, col].astype(F32)
                    if level == 0:
                        value = value + heat * row
                    at = first_air + ((h * a_levels + level) * 3 + j) * a_ch
                    out_ref[at : at + a_ch, :] = value.astype(BF16)
        at = first_air + 2 * a_levels * 3 * a_ch
        out_ref[at : at + a_ch, :] = edge.astype(BF16)


def force_own_kernel(
    mask_ref, temp_ref, flux_ref, got_ref, ocean_ref, air_ref, fw_ref, tw_ref,
    fo_ref, fa_ref, ob_ref, ab_ref, surface_ref,
):
    comp = lax.axis_index("comp")
    fields, band = flux_ref.shape[:2]
    o_levels, a_levels = ocean_ref.shape[1], air_ref.shape[1]
    fill_surface(mask_ref, temp_ref, surface_ref)
    heat = column(tw_ref[...])
    fw = [column(fw_ref[k : k + 1, :]) for k in range(fields)]
    for s in range(2):
        for i in range(band):
            inject = inject_of(flux_ref, got_ref, fw, comp, s, i)
            at = (2 + s) * band + i
            sea = surface_ref[at : at + 1, :]
            row = temp_of(surface_ref, got_ref, fields, band, s, comp, i)
            for level in range(o_levels):
                value = ocean_ref[s, level, i].astype(F32)
                if level == 0:
                    value = (value + inject) * sea
                    fo_ref[s, i] = value
                else:
                    value = value * sea
                ob_ref[s, level, i] = value.astype(BF16)
            for level in range(a_levels):
                value = air_ref[s, level, i].astype(F32)
                if level == 0:
                    value = value + heat * row
                    fa_ref[s, i] = value
                ab_ref[s, level, i] = value.astype(BF16)


def unpack_edge(packed, idx, shift, lane):
    comp = lax.axis_index("comp")
    start = (jnp.where(comp == 0, 0, LANES - 8) + shift) & (LANES - 1)
    rolled = pltpu.roll(packed, (start - 8 * idx + 2 * LANES) & (LANES - 1), 1)
    return jnp.where((lane >> 3) == (start >> 3), rolled, 0.0)


TAPS = 7


def toeplitz_kernel(taps_ref, out_ref, rows_ref):
    groups, levels, _, depth = out_ref.shape
    channels = groups * 8
    for d in range(TAPS):
        rows_ref[d] = jnp.zeros(rows_ref.shape[1:], F32)
        for a in range(3):
            for b in range(TAPS):
                at = a * TAPS + b
                rows_ref[d, at : at + 1, :channels] = taps_ref[a, b, d : d + 1, :]
    window = rows_ref.shape[1]
    taps = [rows_ref[d].T[:channels].astype(BF16) for d in range(TAPS)]
    taps = jnp.concatenate(taps, axis=0)
    row = lax.broadcasted_iota(jnp.int32, (window, depth), 0)
    lane = lax.broadcasted_iota(jnp.int32, (window, depth), 1)
    from_level = lane // 80
    from_lon = (lane >> 3) - from_level * 10
    same = (lax.broadcasted_iota(jnp.int32, (8, depth), 1) & 7) == lax.broadcasted_iota(
        jnp.int32, (8, depth), 0
    )
    for level in range(levels):
        parts = []
        for side in range(2):
            a = from_level - level + 1
            b = from_lon - (pl.program_id(0) * 2 + side)
            hit = (
                (from_level < levels)
                & (a >= 0) & (a <= 2) & (b >= 0) & (b < TAPS) & (a * TAPS + b == row)
            )
            choose = jnp.where(hit, 1.0, 0.0).astype(BF16)
            parts.append(jnp.dot(taps, choose, preferred_element_type=F32))
        for g in range(groups):
            tiles = [
                jnp.where(same, part[d * channels + g * 8 : d * channels + g * 8 + 8], 0.0)
                for part in parts
                for d in range(TAPS)
            ]
            out_ref[g, level] = jnp.concatenate(tiles, axis=0).astype(BF16)


def both_toeplitz_kernel(o_ref, a_ref, o_out, a_out, o_rows, a_rows):
    toeplitz_kernel(a_ref, a_out, a_rows)
    toeplitz_kernel(o_ref, o_out, o_rows)


def rim_tile(even_ref, odd_ref, at, count):
    rows = pl.ds(pl.multiple_of(at, 16), count)
    return even_ref[rows, :].astype(F32), odd_ref[rows, :].astype(F32)


def conv_ocean_kernel(own_ref, even_ref, odd_ref, matrix_ref, out_ref, product_ref):
    _, levels, band, count, _ = own_ref.shape
    depth = matrix_ref.shape[-1]
    lane = lane_ids(8)
    channels = pl.num_programs(0) * count
    first = pl.program_id(0) * count
    inner = (lax.axis_index("lon") & 1) == 1
    columns = []
    for s in range(2):
        tiles = []
        for level in range(levels):
            west, east = [], []
            for i in range(3):
                at = ((s * levels + level) * 3 + i) * channels + first
                even, odd = rim_tile(even_ref, odd_ref, at, count)
                west.append(jnp.where(inner, even, odd))
                east.append(jnp.where(inner, odd, even))
            own = [own_ref[s, level, i].astype(F32) for i in range(band)]
            tiles += west + own + east
        columns.append(tiles)
    for sub in range(count // 8):
        rows = slice(sub * 8, sub * 8 + 8)
        halves = []
        for tiles in columns:
            tiles = [tile[rows] for tile in tiles]
            if depth > len(tiles) * 8:
                tiles.append(jnp.zeros((depth - len(tiles) * 8, LANES), F32))
            halves.append(jnp.concatenate(tiles, axis=0))
        data = jnp.concatenate(halves, axis=1).astype(BF16)
        matrix = matrix_ref[sub].reshape(-1, depth)
        product_ref[...] = jnp.dot(matrix, data, preferred_element_type=F32)
        for level in range(levels):
            for i in range(band):
                base = ((i // 2 * levels + level) * 2 + i % 2) * TAPS
                sums = [None, None]
                for d in range(TAPS):
                    at = slice((base + d) * 8, (base + d) * 8 + 8)
                    first = product_ref[at, :LANES]
                    second = product_ref[at, LANES:]
                    off = d - 3
                    if off > 0:
                        first, second = (
                            pltpu.roll(jnp.where(lane < off, second, first), LANES - off, 1),
                            pltpu.roll(jnp.where(lane < off, 0.0, second), LANES - off, 1),
                        )
                    elif off < 0:
                        first, second = (
                            pltpu.roll(jnp.where(lane >= LANES + off, 0.0, first), -off, 1),
                            pltpu.roll(jnp.where(lane >= LANES + off, first, second), -off, 1),
                        )
                    sums = [
                        part if old is None else old + part
                        for old, part in zip(sums, (first, second))
                    ]
                for s in range(2):
                    out_ref[s, level, i, rows] = sums[s].astype(BF16)


def conv_air_kernel(own_ref, even_ref, odd_ref, packed_ref, matrix_ref, out_ref, product_ref):
    _, levels, band, count, _ = own_ref.shape
    depth = matrix_ref.shape[-1]
    lon = lax.axis_index("lon")
    inner = (lon & 1) == 1
    swap_west = jnp.where(lon == 0, 1, 0)
    swap_east = jnp.where(lon == lax.axis_size("lon") - 1, 1, 0)
    channels = pl.num_programs(0) * count
    first = pl.program_id(0) * count + even_ref.shape[0] - (2 * levels * 3 + 1) * channels
    lane = lane_ids(8)
    even, odd = rim_tile(even_ref, odd_ref, first + 2 * levels * 3 * channels, count)
    edge_tiles = [packed_ref[...], jnp.where(inner, even, odd), jnp.where(inner, odd, even)]
    all_tiles = []
    beyond = []
    for h in range(2):
        west_h = jnp.abs(h - swap_west)
        east_h = jnp.abs(h - swap_east)
        tiles = []
        for level in range(levels):
            west, east = [], []
            for i in range(3):
                at = first + ((west_h * levels + level) * 3 + i) * channels
                even, odd = rim_tile(even_ref, odd_ref, at, count)
                west.append(jnp.where(inner, even, odd))
                at = first + ((east_h * levels + level) * 3 + i) * channels
                even, odd = rim_tile(even_ref, odd_ref, at, count)
                east.append(jnp.where(inner, odd, even))
            tiles += west + [own_ref[h, level, i].astype(F32) for i in range(band)] + east
            beyond += [(h, 1, (level * 2 + west_h) * band + i + band - 3) for i in range(3)]
            beyond += [(h, 0, (level * 2 + h) * band + i) for i in range(band)]
            beyond += [(h, 2, (level * 2 + east_h) * band + i) for i in range(3)]
        all_tiles.append(tiles)
    for sub in range(count // 8):
        rows = slice(sub * 8, sub * 8 + 8)
        columns = [[tile[rows] for tile in tiles] for tiles in all_tiles]
        packed = [tile[rows] for tile in edge_tiles]
        edges = [
            [unpack_edge(packed[who], idx, h * 64, lane) for at_h, who, idx in beyond if at_h == h]
            for h in range(2)
        ]
        columns.append([one + two for one, two in zip(*edges)])
        pad = depth - len(columns[0]) * 8
        if pad:
            columns = [tiles + [jnp.zeros((pad, LANES), F32)] for tiles in columns]
        data = jnp.concatenate(
            [jnp.concatenate(tiles, axis=0) for tiles in columns], axis=1
        ).astype(BF16)
        matrix = matrix_ref[sub].reshape(-1, depth)
        product_ref[...] = jnp.dot(matrix, data, preferred_element_type=F32)
        for level in range(levels):
            for i in range(band):
                base = ((i // 2 * levels + level) * 2 + i % 2) * TAPS
                sums = [None, None]
                for d in range(TAPS):
                    at = slice((base + d) * 8, (base + d) * 8 + 8)
                    off = d - 3
                    edge = product_ref[at, 2 * LANES :] if off else None
                    for h in range(2):
                        part = product_ref[at, h * LANES : (h + 1) * LANES]
                        if off:
                            here = edge if h == 0 else pltpu.roll(edge, 64, 1)
                            inside = lane < off if off > 0 else lane >= LANES + off
                            part = pltpu.roll(jnp.where(inside, here, part), (LANES - off) % LANES, 1)
                        sums[h] = part if sums[h] is None else sums[h] + part
                for h in range(2):
                    out_ref[h, level, i, rows] = sums[h].astype(BF16)


def convolution(kernel, name, own, even, odd, packed, matrix):
    _, levels, band, channels, _ = own.shape
    groups, pairs, rows, depth = matrix.shape
    count = 16
    lane_tiles = 2 if packed is None else 3
    grid_spec = pl.BlockSpec((2, levels, band, count, LANES), lambda g: (0, 0, 0, g, 0))
    rim_spec = pl.BlockSpec(even.shape, lambda g: (0, 0))
    args = [own, even, odd]
    specs = [grid_spec, rim_spec, rim_spec]
    if packed is not None:
        args.append(packed)
        specs.append(pl.BlockSpec((count, LANES), lambda g: (g, 0)))
    args.append(matrix)
    specs.append(pl.BlockSpec((count // 8, pairs, rows, depth), lambda g: (g, 0, 0, 0)))
    return pl.pallas_call(
        kernel,
        grid=(channels // count,),
        out_shape=jax.ShapeDtypeStruct(own.shape, BF16),
        in_specs=specs,
        out_specs=grid_spec,
        scratch_shapes=[pltpu.VMEM((pairs * rows, lane_tiles * LANES), F32)],
        name=name,
        compiler_params=PARAMS,
        cost_estimate=pl.CostEstimate(flops=2 * 10**9, bytes_accessed=4 * 10**6, transcendentals=0),
    )(*args)


def mlp_kernel(masked, *refs):
    own_ref, other_ref, gain_ref, up_ref, down_ref, top_ref, forced_ref = refs[:7]
    mask_ref = refs[7] if masked else None
    out_ref, values_ref, wide_ref, narrow_ref = refs[-4:]
    _, levels, band, channels, _ = own_ref.shape
    ch = lax.axis_index("ch")
    total = 2 * channels
    gain = column(gain_ref[...])
    wide_ref[...] = up_ref[...].astype(F32).T.astype(BF16)
    mine = pl.ds(pl.multiple_of(ch * channels, channels), channels)
    if masked:
        narrow_ref[...] = down_ref[...].astype(F32).T.astype(BF16)
    else:
        narrow_ref[: channels] = down_ref[mine, :]
    down_rows = mine if masked else slice(0, channels)

    def row(at, slot):
        level = at // band
        i = lax.rem(at, band)
        mine = pl.ds(pl.multiple_of(ch * channels, channels), channels)
        theirs = pl.ds(pl.multiple_of((1 - ch) * channels, channels), channels)
        for s in range(2):
            lanes = slice(s * LANES, (s + 1) * LANES)
            values_ref[slot, mine, lanes] = own_ref[s, level, i].astype(F32)
            values_ref[slot, theirs, lanes] = other_ref[s, level, i].astype(F32)
        values = values_ref[slot]
        center = jnp.sum(values, axis=0, keepdims=True) * (1.0 / total)
        values = values - center
        spread = jnp.sum(values * values, axis=0, keepdims=True) * (1.0 / total)
        normed = (values * lax.rsqrt(spread + 1e-06) * gain).astype(BF16)
        raw = jnp.dot(wide_ref[...], normed, preferred_element_type=F32)
        inner = raw * (0.7978845608028654 + 0.035677408136300125 * (raw * raw))
        doubled = (raw + raw * jnp.tanh(inner)).astype(BF16)
        update = jnp.dot(narrow_ref[down_rows, :], doubled, preferred_element_type=F32) * 0.5
        update = update.astype(BF16).astype(F32)
        if masked:
            mask = mask_ref[...]
            picked = lax.broadcasted_iota(jnp.int32, mask.shape, 0) == i
            sea = jnp.sum(jnp.where(picked, mask.astype(F32), 0.0), axis=0, keepdims=True)
        for s in range(2):
            lanes = slice(s * LANES, (s + 1) * LANES)
            forced = jnp.where(level == 0, top_ref[s, i], forced_ref[s, level, i].astype(F32))
            result = forced + update[:, lanes]
            if masked:
                result = result * sea[:, lanes]
            out_ref[s, level, i] = result.astype(BF16)

    def step(at, carry):
        row(at * 2, 0)
        row(at * 2 + 1, 1)
        return carry

    lax.fori_loop(0, levels * band // 2, step, 0)


def toeplitz(ocean_kernel, air_kernel, o_levels, a_levels):
    taps = [jnp.transpose(kernel, (1, 2, 3, 0)) for kernel in (ocean_kernel, air_kernel)]
    shapes = [
        (part.shape[-1] // 8, levels, 2 * TAPS * 8, 256)
        for part, levels in zip(taps, (o_levels, a_levels))
    ]
    return pl.pallas_call(
        both_toeplitz_kernel,
        grid=(2,),
        out_shape=[
            jax.ShapeDtypeStruct((g, 2 * levels, rows, depth), BF16)
            for g, levels, rows, depth in shapes
        ],
        in_specs=[pl.BlockSpec(part.shape, lambda p: (0, 0, 0, 0)) for part in taps],
        out_specs=[pl.BlockSpec(block, lambda p: (0, p, 0, 0)) for block in shapes],
        scratch_shapes=[pltpu.VMEM((TAPS, LANES, LANES), F32)] * 2,
        name="matrix",
        compiler_params=PARAMS,
        cost_estimate=pl.CostEstimate(flops=2 * 10**9, bytes_accessed=6 * 10**6, transcendentals=0),
    )(*taps)


def pairs_of(count, first):
    pairs = []
    for i in range(first, count + first, 2):
        pairs += [(i % count, (i + 1) % count), ((i + 1) % count, i % count)]
    return pairs


def ring(count, step):
    return [(i, (i + step) % count) for i in range(count)]


def per_device(
    ocean_state, ocean_mask, air_state, surface_temp, air_fluxes, ocean_kernel, ocean_gain, ocean_up,
    ocean_down, air_kernel, air_gain, air_up, air_down, flux_weight, temp_weight,
):
    o_levels, o_ch, band, lats = ocean_state.shape
    a_levels, a_ch = air_state.shape[:2]
    fields = air_fluxes.shape[0]
    shape = jax.ShapeDtypeStruct

    ocean_grid = jnp.transpose(
        ocean_state.reshape(o_levels, o_ch, band, 2, LANES), (3, 0, 2, 1, 4)
    )
    air_grid = jnp.transpose(air_state, (3, 0, 2, 1, 4))
    o_grid = (2, o_levels, band, o_ch, LANES)
    a_grid = (2, a_levels, band, a_ch, LANES)

    lons = lax.axis_size("lon")
    bands = lax.axis_size("comp") * lons
    lon = lax.axis_index("lon")
    outward = lax.dynamic_slice_in_dim(ocean_grid, jnp.where(lon == 0, 0, band - 3), 3, 2)
    swaps = [(i, (i + lons) % bands) for i in (0, lons - 1, lons, bands - 1)]
    rows = rows_of(fields, band)[-1] + a_ch
    packed = call(
        pack_kernel, shape((rows, LANES), F32), [], "pack", 10**5, 10**6,
        ocean_mask, surface_temp, air_fluxes, air_grid,
    )
    got = lax.ppermute(packed, "comp", ring(2, 1))
    o_tiles = 2 * o_levels * 3
    outward, _ = lax.optimization_barrier((outward, packed))
    swapped = lax.ppermute(outward.reshape(o_tiles, o_ch, LANES), ("comp", "lon"), swaps)
    o_matrix, a_matrix = toeplitz(ocean_kernel, air_kernel, o_levels, a_levels)
    o_matrix, a_matrix, got, swapped = lax.optimization_barrier((o_matrix, a_matrix, got, swapped))
    rim = (o_tiles * o_ch + (2 * a_levels * 3 + 1) * a_ch, LANES)
    surface = pltpu.VMEM((4 * band, LANES), F32)
    weights = (flux_weight, temp_weight.reshape(1, a_ch))
    even_out, odd_out, edge = call(
        force_halo_kernel,
        (shape(rim, BF16), shape(rim, BF16), shape((a_ch, LANES), F32)),
        [surface], "force_halo", 10**6, 4 * 10**6,
        ocean_mask, surface_temp, air_fluxes, got, ocean_grid, swapped, air_grid, *weights,
    )
    even = lax.ppermute(even_out, "lon", pairs_of(lons, 0))
    odd = lax.ppermute(odd_out, "lon", pairs_of(lons, 1))
    ocean_top, air_top, ocean_forced, air_forced = call(
        force_own_kernel,
        (
            shape((2, band, o_ch, LANES), F32), shape((2, band, a_ch, LANES), F32),
            shape(o_grid, BF16), shape(a_grid, BF16),
        ),
        [surface], "force_own", 10**6, 4 * 10**6,
        ocean_mask, surface_temp, air_fluxes, got, ocean_grid, air_grid, *weights,
    )

    a_conv = convolution(conv_air_kernel, "conv_air", air_forced, even, odd, edge, a_matrix)
    a_other = lax.ppermute(a_conv, "ch", ring(2, 1))
    o_conv = convolution(conv_ocean_kernel, "conv_ocean", ocean_forced, even, odd, None, o_matrix)
    o_other = lax.ppermute(o_conv, "ch", ring(2, 1))

    a_hid, o_hid = air_up.shape[1], ocean_up.shape[1]
    a_next = call(
        functools.partial(mlp_kernel, False), shape(a_grid, BF16),
        [
            pltpu.VMEM((2, 2 * a_ch, 2 * LANES), F32), pltpu.VMEM((a_hid, 2 * a_ch), BF16),
            pltpu.VMEM((2 * a_ch, a_hid), BF16),
        ],
        "mlp_air", 10**9, 3 * 10**6,
        a_conv, a_other, air_gain.reshape(1, -1), air_up, air_down.T, air_top, air_forced,
    )
    o_next = call(
        functools.partial(mlp_kernel, True), shape(o_grid, BF16),
        [
            pltpu.VMEM((2, 2 * o_ch, 2 * LANES), F32), pltpu.VMEM((o_hid, 2 * o_ch), BF16),
            pltpu.VMEM((2 * o_ch, o_hid), BF16),
        ],
        "mlp_ocean", 10**9, 3 * 10**6,
        o_conv, o_other, ocean_gain.reshape(1, -1), ocean_up, ocean_down, ocean_top, ocean_forced,
        ocean_mask,
    )
    ocean_next = jnp.transpose(o_next, (1, 3, 2, 0, 4)).reshape(ocean_state.shape)
    air_next = jnp.transpose(a_next, (1, 3, 2, 0, 4))
    return (ocean_next, air_next)


def solution(mesh):
    in_specs = (
        P(None, "ch", ("comp", "lon"), None),
        P(("comp", "lon"), None),
        P(None, "ch", "lon", None, "comp"),
        P(("comp", "lon"), None),
        P(None, "lon", None, "comp"),
        P("ch", None, None, None),
        P(),
        P(),
        P(),
        P("ch", None, None, None),
        P(),
        P(),
        P(),
        P(None, "ch"),
        P("ch"),
    )
    out_specs = (P(None, "ch", ("comp", "lon"), None), P(None, "ch", "lon", None, "comp"))
    return jax.shard_map(
        per_device, mesh=mesh, in_specs=in_specs, out_specs=out_specs, check_vma=False
    )
```

```python
import functools

import jax
import jax.numpy as jnp
from jax import lax
from jax.experimental import pallas as pl
from jax.experimental.pallas import tpu as pltpu
from jax.sharding import PartitionSpec as P

F32 = jnp.float32
BF16 = jnp.bfloat16
LANES = 128
PARAMS = pltpu.CompilerParams(vmem_limit_bytes=24 * 2**20)
VMEM = pl.BlockSpec(memory_space=pltpu.VMEM)


def lane_ids(rows):
    return lax.broadcasted_iota(jnp.int32, (rows, LANES), 1)


def column(row):
    n = row.shape[1]
    same = lax.broadcasted_iota(jnp.int32, (n, n), 0) == lax.broadcasted_iota(jnp.int32, (n, n), 1)
    return jnp.sum(jnp.where(same, row, 0.0), axis=1, keepdims=True)


def call(kernel, out_shape, scratch, name, flops, moved, *args):
    return pl.pallas_call(
        kernel,
        out_shape=out_shape,
        in_specs=[VMEM] * len(args),
        out_specs=jax.tree.map(lambda _: VMEM, out_shape),
        scratch_shapes=scratch,
        name=name,
        compiler_params=PARAMS,
        cost_estimate=pl.CostEstimate(flops=flops, bytes_accessed=moved, transcendentals=0),
    )(*args)


def rows_of(fields, band):
    temp = fields * band
    return temp, temp + 2 * band


def pack_kernel(mask_hbm, temp_hbm, flux_hbm, air_ref, out_ref, mask_ref, temp_ref, flux_ref, sems):
    copies = [
        pltpu.make_async_copy(mask_hbm, mask_ref, sems.at[0]),
        pltpu.make_async_copy(temp_hbm, temp_ref, sems.at[1]),
        pltpu.make_async_copy(flux_hbm, flux_ref, sems.at[2]),
    ]
    for copy in copies:
        copy.start()
    comp = lax.axis_index("comp")
    fields, band = flux_ref.shape[:2]
    temp_row, edge_row = rows_of(fields, band)
    levels, channels = air_ref.shape[1], air_ref.shape[3]
    start = jnp.where(comp == 0, LANES - 8, 0)
    lane = lane_ids(channels)
    packed = jnp.zeros((channels, LANES), F32)
    for level in range(levels):
        for h in range(2):
            for j in range(band):
                idx = (level * 2 + h) * band + j
                rolled = pltpu.roll(
                    air_ref[h, level, j].astype(F32), (8 * idx - start + LANES) & (LANES - 1), 1
                )
                packed = jnp.where((lane >> 3) == idx, rolled, packed)
    out_ref[edge_row : edge_row + channels, :] = packed
    for copy in copies:
        copy.wait()
    for k in range(fields):
        for j in range(band):
            at = k * band + j
            out_ref[at : at + 1, :] = flux_ref[k, j, pl.ds(1 - comp, 1), :]
    temp = temp_ref[...] * mask_ref[...].astype(F32)
    for s in range(2):
        lanes = slice(s * LANES, (s + 1) * LANES)
        out_ref[temp_row + s * band : temp_row + (s + 1) * band, :] = temp[:, lanes]


def fill_surface(mask_ref, temp_ref, surface_ref):
    band = mask_ref.shape[0]
    sea = mask_ref[...].astype(F32)
    temp = temp_ref[...] * sea
    for s in range(2):
        lanes = slice(s * LANES, (s + 1) * LANES)
        surface_ref[s * band : (s + 1) * band, :] = temp[:, lanes]
        surface_ref[(2 + s) * band : (3 + s) * band, :] = sea[:, lanes]


def inject_of(flux_ref, got_ref, fw, s, i):
    comp = lax.axis_index("comp")
    fields, band = flux_ref.shape[:2]
    total = None
    for k in range(fields):
        mine = flux_ref[k, i, pl.ds(comp, 1), :]
        theirs = got_ref[pl.ds(k * band + i, 1), :]
        term = fw[k] * jnp.where(comp == s, mine, theirs)
        total = term if total is None else total + term
    return total


def temp_of(surface_ref, got_ref, fields, band, h, s, j):
    comp = lax.axis_index("comp")
    temp_row = rows_of(fields, band)[0]
    mine = surface_ref[pl.ds(s * band + j, 1), :]
    theirs = got_ref[pl.ds(temp_row + s * band + j, 1), :]
    return jnp.where(comp == h, mine, theirs)


def force_halo_kernel(
    mask_ref, temp_ref, flux_ref, got_ref, ocean_ref, air_ref, fw_ref, tw_ref,
    even_ref, odd_ocean_ref, odd_air_ref, edge_ref, surface_ref,
):
    comp = lax.axis_index("comp")
    parity = lax.axis_index("lon") & 1
    fields, band = flux_ref.shape[:2]
    o_levels, o_ch = ocean_ref.shape[1], ocean_ref.shape[3]
    a_levels, a_ch = air_ref.shape[1], air_ref.shape[3]
    edge_row = rows_of(fields, band)[1]
    fill_surface(mask_ref, temp_ref, surface_ref)
    heat = column(tw_ref[...])
    fw = [column(fw_ref[k : k + 1, :]) for k in range(fields)]

    start = jnp.where(comp == 0, 0, LANES - 8)
    lane = lane_ids(8)
    edge_temp = jnp.zeros((8, LANES), F32)
    for h in range(2):
        for j in range(band):
            idx = h * band + j
            row = temp_of(surface_ref, got_ref, fields, band, h, 1 - comp, j)
            rolled = pltpu.roll(
                jnp.broadcast_to(row, (8, LANES)), (8 * idx - start + LANES) & (LANES - 1), 1
            )
            edge_temp = jnp.where((lane >> 3) == idx, rolled, edge_temp)
    edge = got_ref[edge_row : edge_row + a_ch, :] + heat * edge_temp[0:1, :]
    edge_ref[...] = edge

    first_air = 2 * o_levels * 3 * o_ch
    for ocean_out, air_out, base, offset in (
        (even_ref, even_ref, first_air, 1 - parity), (odd_ocean_ref, odd_air_ref, 0, parity)
    ):
        for j in range(3):
            col = j + offset
            for s in range(2):
                inject = inject_of(flux_ref, got_ref, fw, s, col)
                sea = surface_ref[pl.ds((2 + s) * band + col, 1), :]
                for level in range(o_levels):
                    tile = (s * o_levels + level) * 3 + j
                    value = ocean_ref[s, level, col].astype(F32)
                    if level == 0:
                        value = value + inject
                    ocean_out[tile * o_ch : (tile + 1) * o_ch, :] = (value * sea).astype(BF16)
            for h in range(2):
                row = temp_of(surface_ref, got_ref, fields, band, h, comp, col)
                for level in range(a_levels):
                    value = air_ref[h, level, col].astype(F32)
                    if level == 0:
                        value = value + heat * row
                    at = base + ((h * a_levels + level) * 3 + j) * a_ch
                    air_out[at : at + a_ch, :] = value.astype(BF16)
        at = base + 2 * a_levels * 3 * a_ch
        air_out[at : at + a_ch, :] = edge.astype(BF16)


def force_own_kernel(
    mask_ref, temp_ref, flux_ref, got_ref, ocean_ref, air_ref, fw_ref, tw_ref,
    fo_ref, fa_ref, ob_ref, ab_ref, surface_ref,
):
    comp = lax.axis_index("comp")
    fields, band = flux_ref.shape[:2]
    o_levels, a_levels = ocean_ref.shape[1], air_ref.shape[1]
    fill_surface(mask_ref, temp_ref, surface_ref)
    heat = column(tw_ref[...])
    fw = [column(fw_ref[k : k + 1, :]) for k in range(fields)]
    for s in range(2):
        for i in range(band):
            inject = inject_of(flux_ref, got_ref, fw, s, i)
            at = (2 + s) * band + i
            sea = surface_ref[at : at + 1, :]
            row = temp_of(surface_ref, got_ref, fields, band, s, comp, i)
            for level in range(o_levels):
                value = ocean_ref[s, level, i].astype(F32)
                if level == 0:
                    value = (value + inject) * sea
                    fo_ref[s, i] = value
                else:
                    value = value * sea
                ob_ref[s, level, i] = value.astype(BF16)
            for level in range(a_levels):
                value = air_ref[s, level, i].astype(F32)
                if level == 0:
                    value = value + heat * row
                    fa_ref[s, i] = value
                ab_ref[s, level, i] = value.astype(BF16)


TAPS = 7


def toeplitz_kernel(taps_ref, out_ref, rows_ref):
    groups, levels, _, depth = out_ref.shape
    channels = groups * 8
    for d in range(TAPS):
        rows_ref[d] = jnp.zeros(rows_ref.shape[1:], F32)
        for a in range(3):
            for b in range(TAPS):
                at = a * TAPS + b
                rows_ref[d, at : at + 1, :channels] = taps_ref[a, b, d : d + 1, :]
    window = rows_ref.shape[1]
    taps = [rows_ref[d].T[:channels].astype(BF16) for d in range(TAPS)]
    taps = jnp.concatenate(taps, axis=0)
    row = lax.broadcasted_iota(jnp.int32, (window, depth), 0)
    lane = lax.broadcasted_iota(jnp.int32, (window, depth), 1)
    from_level = lane // 80
    from_lon = (lane >> 3) - from_level * 10
    same = (lax.broadcasted_iota(jnp.int32, (8, depth), 1) & 7) == lax.broadcasted_iota(
        jnp.int32, (8, depth), 0
    )
    for level in range(levels):
        parts = []
        for side in range(2):
            a = from_level - level + 1
            b = from_lon - (pl.program_id(0) * 2 + side)
            hit = (
                (from_level < levels)
                & (a >= 0) & (a <= 2) & (b >= 0) & (b < TAPS) & (a * TAPS + b == row)
            )
            choose = jnp.where(hit, 1.0, 0.0).astype(BF16)
            parts.append(jnp.dot(taps, choose, preferred_element_type=F32))
        for g in range(groups):
            tiles = [
                jnp.where(same, part[d * channels + g * 8 : d * channels + g * 8 + 8], 0.0)
                for part in parts
                for d in range(TAPS)
            ]
            out_ref[g, level] = jnp.concatenate(tiles, axis=0).astype(BF16)


def both_toeplitz_kernel(o_ref, a_ref, o_out, a_out, o_rows, a_rows):
    toeplitz_kernel(a_ref, a_out, a_rows)
    toeplitz_kernel(o_ref, o_out, o_rows)


def rim_tile(even_ref, odd_ref, even_at, odd_at, count):
    even = even_ref[pl.ds(pl.multiple_of(even_at, 16), count), :]
    odd = odd_ref[pl.ds(pl.multiple_of(odd_at, 16), count), :]
    return even.astype(F32), odd.astype(F32)


def conv_ocean_kernel(own_ref, even_ref, odd_ref, matrix_ref, out_ref, product_ref):
    _, levels, band, count, _ = own_ref.shape
    depth = matrix_ref.shape[-1]
    lane = lane_ids(8)
    channels = pl.num_programs(0) * count
    first = pl.program_id(0) * count
    inner = (lax.axis_index("lon") & 1) == 1
    columns = []
    for s in range(2):
        tiles = []
        for level in range(levels):
            west, east = [], []
            for i in range(3):
                at = ((s * levels + level) * 3 + i) * channels + first
                even, odd = rim_tile(even_ref, odd_ref, at, at, count)
                west.append(jnp.where(inner, even, odd))
                east.append(jnp.where(inner, odd, even))
            own = [own_ref[s, level, i].astype(F32) for i in range(band)]
            tiles += west + own + east
        columns.append(tiles)
    for sub in range(count // 8):
        rows = slice(sub * 8, sub * 8 + 8)
        halves = []
        for tiles in columns:
            tiles = [tile[rows] for tile in tiles]
            if depth > len(tiles) * 8:
                tiles.append(jnp.zeros((depth - len(tiles) * 8, LANES), F32))
            halves.append(jnp.concatenate(tiles, axis=0))
        data = jnp.concatenate(halves, axis=1).astype(BF16)
        matrix = matrix_ref[sub].reshape(-1, depth)
        product_ref[...] = jnp.dot(matrix, data, preferred_element_type=F32)
        for level in range(levels):
            for i in range(band):
                base = ((i // 2 * levels + level) * 2 + i % 2) * TAPS
                sums = [None, None]
                for d in range(TAPS):
                    at = slice((base + d) * 8, (base + d) * 8 + 8)
                    first = product_ref[at, :LANES]
                    second = product_ref[at, LANES:]
                    off = d - 3
                    if off > 0:
                        first, second = (
                            pltpu.roll(jnp.where(lane < off, second, first), LANES - off, 1),
                            pltpu.roll(jnp.where(lane < off, 0.0, second), LANES - off, 1),
                        )
                    elif off < 0:
                        first, second = (
                            pltpu.roll(jnp.where(lane >= LANES + off, 0.0, first), -off, 1),
                            pltpu.roll(jnp.where(lane >= LANES + off, first, second), -off, 1),
                        )
                    sums = [
                        part if old is None else old + part
                        for old, part in zip(sums, (first, second))
                    ]
                for s in range(2):
                    out_ref[s, level, i, rows] = sums[s].astype(BF16)


def conv_air_kernel(own_ref, even_ref, odd_ref, packed_ref, matrix_ref, *refs):
    out_refs, product_ref = refs[:-1], refs[-1]
    _, levels, band, count, _ = own_ref.shape
    depth = matrix_ref.shape[-1]
    lon = lax.axis_index("lon")
    inner = (lon & 1) == 1
    swap_west = jnp.where(lon == 0, 1, 0)
    swap_east = jnp.where(lon == lax.axis_size("lon") - 1, 1, 0)
    channels = pl.num_programs(0) * count
    first_odd = pl.program_id(0) * count
    first_even = first_odd + even_ref.shape[0] - odd_ref.shape[0]

    def tiles_at(tile):
        at = tile * channels
        return rim_tile(even_ref, odd_ref, first_even + at, first_odd + at, count)

    start = jnp.where(lax.axis_index("comp") == 0, 0, LANES - 8)
    wide = lane_ids(count)
    even, odd = tiles_at(2 * levels * 3)
    edge_tiles = []
    for tile, swap in (
        (packed_ref[...], None),
        (jnp.where(inner, even, odd), swap_west),
        (jnp.where(inner, odd, even), swap_east),
    ):
        if swap is not None:
            span = 8 * band
            other = jnp.where(
                (wide & span) == 0, pltpu.roll(tile, LANES - span, 1), pltpu.roll(tile, span, 1)
            )
            tile = jnp.where(swap == 1, other, tile)
        edge_tiles.append(pltpu.roll(tile, start, 1))
    lane = lane_ids(8)
    block = ((lane - start + LANES) & (LANES - 1)) >> 3
    adjoining = (block == 0) | (block == band)
    all_tiles = []
    for h in range(2):
        west_h = jnp.abs(h - swap_west)
        east_h = jnp.abs(h - swap_east)
        tiles = []
        for level in range(levels):
            west, east = [], []
            for i in range(3):
                even, odd = tiles_at((west_h * levels + level) * 3 + i)
                west.append(jnp.where(inner, even, odd))
                even, odd = tiles_at((east_h * levels + level) * 3 + i)
                east.append(jnp.where(inner, odd, even))
            tiles += west + [own_ref[h, level, i].astype(F32) for i in range(band)] + east
        all_tiles.append(tiles)
    beyond = []
    for level in range(levels):
        first = level * 2 * band
        beyond += [(1, first + i + band - 3) for i in range(3)]
        beyond += [(0, first + i) for i in range(band)]
        beyond += [(2, first + i) for i in range(3)]
    for sub in range(count // 8):
        rows = slice(sub * 8, sub * 8 + 8)
        columns = [[tile[rows] for tile in tiles] for tiles in all_tiles]
        packed = [tile[rows] for tile in edge_tiles]
        columns.append(
            [
                jnp.where(adjoining, pltpu.roll(packed[who], -8 * idx % LANES, 1), 0.0)
                for who, idx in beyond
            ]
        )
        pad = depth - len(columns[0]) * 8
        if pad:
            columns = [tiles + [jnp.zeros((pad, LANES), F32)] for tiles in columns]
        data = jnp.concatenate(
            [jnp.concatenate(tiles, axis=0) for tiles in columns], axis=1
        ).astype(BF16)
        matrix = matrix_ref[sub].reshape(-1, depth)
        product_ref[...] = jnp.dot(matrix, data, preferred_element_type=F32)
        for level in range(levels):
            for i in range(band):
                base = ((i // 2 * levels + level) * 2 + i % 2) * TAPS
                sums = [None, None]
                for d in range(TAPS):
                    at = slice((base + d) * 8, (base + d) * 8 + 8)
                    off = d - 3
                    edge = product_ref[at, 2 * LANES :] if off else None
                    for h in range(2):
                        part = product_ref[at, h * LANES : (h + 1) * LANES]
                        if off:
                            here = edge if h == 0 else pltpu.roll(edge, LANES - 8 * band, 1)
                            inside = lane < off if off > 0 else lane >= LANES + off
                            part = pltpu.roll(jnp.where(inside, here, part), (LANES - off) % LANES, 1)
                        sums[h] = part if sums[h] is None else sums[h] + part
                for h in range(2):
                    out_refs[level][h, 0, i, rows] = sums[h].astype(BF16)


def convolution(kernel, name, own, even, odd, packed, matrix):
    _, levels, band, channels, _ = own.shape
    groups, pairs, rows, depth = matrix.shape
    count = 16
    lane_tiles = 2 if packed is None else 3
    grid_spec = pl.BlockSpec((2, levels, band, count, LANES), lambda g: (0, 0, 0, g, 0))
    args = [own, even, odd]
    specs = [grid_spec] + [pl.BlockSpec(rim.shape, lambda g: (0, 0)) for rim in (even, odd)]
    outs = [levels] if packed is None else [1] * levels
    if packed is not None:
        args.append(packed)
        specs.append(pl.BlockSpec((count, LANES), lambda g: (g, 0)))
    args.append(matrix)
    specs.append(pl.BlockSpec((count // 8, pairs, rows, depth), lambda g: (g, 0, 0, 0)))
    return pl.pallas_call(
        kernel,
        grid=(channels // count,),
        out_shape=[jax.ShapeDtypeStruct((2, part) + own.shape[2:], BF16) for part in outs],
        in_specs=specs,
        out_specs=[
            pl.BlockSpec((2, part, band, count, LANES), lambda g: (0, 0, 0, g, 0)) for part in outs
        ],
        scratch_shapes=[pltpu.VMEM((pairs * rows, lane_tiles * LANES), F32)],
        name=name,
        compiler_params=PARAMS,
        cost_estimate=pl.CostEstimate(flops=2 * 10**9, bytes_accessed=4 * 10**6, transcendentals=0),
    )(*args)


def mlp_kernel(masked, first_level, *refs):
    own_ref, other_ref, gain_ref, up_ref, down_ref, top_ref, forced_ref = refs[:7]
    extra_ref = refs[7] if len(refs) > 11 else None
    out_ref, values_ref, wide_ref, narrow_ref = refs[-4:]
    _, levels, band, channels, _ = own_ref.shape
    ch = lax.axis_index("ch")
    total = 2 * channels
    gain = column(gain_ref[...])
    wide_ref[...] = up_ref[...].astype(F32).T.astype(BF16)
    mine = pl.ds(pl.multiple_of(ch * channels, channels), channels)
    if masked:
        narrow_ref[...] = down_ref[...].astype(F32).T.astype(BF16)
    else:
        narrow_ref[: channels] = down_ref[mine, :]
    down_rows = mine if masked else slice(0, channels)

    if not masked and extra_ref is not None:
        out_ref[:, :first_level] = extra_ref[...]

    def row(at, slot):
        level = at // band
        i = lax.rem(at, band)
        mine = pl.ds(pl.multiple_of(ch * channels, channels), channels)
        theirs = pl.ds(pl.multiple_of((1 - ch) * channels, channels), channels)
        for s in range(2):
            lanes = slice(s * LANES, (s + 1) * LANES)
            values_ref[slot, mine, lanes] = own_ref[s, level, i].astype(F32)
            values_ref[slot, theirs, lanes] = other_ref[s, level, i].astype(F32)
        values = values_ref[slot]
        center = jnp.sum(values, axis=0, keepdims=True) * (1.0 / total)
        values = values - center
        spread = jnp.sum(values * values, axis=0, keepdims=True) * (1.0 / total)
        normed = (values * lax.rsqrt(spread + 1e-06) * gain).astype(BF16)
        raw = jnp.dot(wide_ref[...], normed, preferred_element_type=F32)
        inner = raw * (0.7978845608028654 + 0.035677408136300125 * (raw * raw))
        doubled = (raw + raw * jnp.tanh(inner)).astype(BF16)
        update = jnp.dot(narrow_ref[down_rows, :], doubled, preferred_element_type=F32) * 0.5
        update = update.astype(BF16).astype(F32)
        if masked:
            mask = extra_ref[...]
            picked = lax.broadcasted_iota(jnp.int32, mask.shape, 0) == i
            sea = jnp.sum(jnp.where(picked, mask.astype(F32), 0.0), axis=0, keepdims=True)
        for s in range(2):
            lanes = slice(s * LANES, (s + 1) * LANES)
            if first_level:
                forced = forced_ref[s, first_level + level, i].astype(F32)
            else:
                forced = jnp.where(level == 0, top_ref[s, i], forced_ref[s, level, i].astype(F32))
            result = forced + update[:, lanes]
            if masked:
                result = result * sea[:, lanes]
            out_ref[s, first_level + level, i] = result.astype(BF16)

    def step(at, carry):
        row(at * 2, 0)
        row(at * 2 + 1, 1)
        return carry

    lax.fori_loop(0, levels * band // 2, step, 0)


def toeplitz(ocean_kernel, air_kernel, o_levels, a_levels):
    taps = [jnp.transpose(kernel, (1, 2, 3, 0)) for kernel in (ocean_kernel, air_kernel)]
    shapes = [
        (part.shape[-1] // 8, levels, 2 * TAPS * 8, 256)
        for part, levels in zip(taps, (o_levels, a_levels))
    ]
    return pl.pallas_call(
        both_toeplitz_kernel,
        grid=(2,),
        out_shape=[
            jax.ShapeDtypeStruct((g, 2 * levels, rows, depth), BF16)
            for g, levels, rows, depth in shapes
        ],
        in_specs=[pl.BlockSpec(part.shape, lambda p: (0, 0, 0, 0)) for part in taps],
        out_specs=[pl.BlockSpec(block, lambda p: (0, p, 0, 0)) for block in shapes],
        scratch_shapes=[pltpu.VMEM((TAPS, LANES, LANES), F32)] * 2,
        name="matrix",
        compiler_params=PARAMS,
        cost_estimate=pl.CostEstimate(flops=2 * 10**9, bytes_accessed=6 * 10**6, transcendentals=0),
    )(*taps)


def pairs_of(count, first):
    pairs = []
    for i in range(first, count + first, 2):
        pairs += [(i % count, (i + 1) % count), ((i + 1) % count, i % count)]
    return pairs


def ring(count, step):
    return [(i, (i + step) % count) for i in range(count)]


def per_device(
    ocean_state, ocean_mask, air_state, surface_temp, air_fluxes, ocean_kernel, ocean_gain, ocean_up,
    ocean_down, air_kernel, air_gain, air_up, air_down, flux_weight, temp_weight,
):
    o_levels, o_ch, band, lats = ocean_state.shape
    a_levels, a_ch = air_state.shape[:2]
    fields = air_fluxes.shape[0]
    shape = jax.ShapeDtypeStruct

    air_grid = jnp.transpose(air_state, (3, 0, 2, 1, 4))
    o_grid = (2, o_levels, band, o_ch, LANES)
    a_grid = (2, a_levels, band, a_ch, LANES)

    lons = lax.axis_size("lon")
    bands = lax.axis_size("comp") * lons
    rows = rows_of(fields, band)[-1] + a_ch
    hbm = pl.BlockSpec(memory_space=pltpu.HBM)
    surface_args = (ocean_mask, surface_temp, air_fluxes)
    packed = pl.pallas_call(
        pack_kernel,
        out_shape=shape((rows, LANES), F32),
        in_specs=[hbm, hbm, hbm, VMEM],
        out_specs=VMEM,
        scratch_shapes=[pltpu.VMEM(arg.shape, arg.dtype) for arg in surface_args]
        + [pltpu.SemaphoreType.DMA((3,))],
        name="pack",
        compiler_params=PARAMS,
    )(*surface_args, air_grid)
    got = lax.ppermute(packed, "comp", ring(2, 1))
    later_ocean, _ = lax.optimization_barrier((ocean_state, packed))
    ocean_grid = jnp.transpose(
        later_ocean.reshape(o_levels, o_ch, band, 2, LANES), (3, 0, 2, 1, 4)
    )
    ocean_grid, ocean_kernel = lax.optimization_barrier((ocean_grid, ocean_kernel))
    o_matrix, a_matrix = toeplitz(ocean_kernel, air_kernel, o_levels, a_levels)
    o_matrix, a_matrix, got = lax.optimization_barrier((o_matrix, a_matrix, got))
    o_rows = 2 * o_levels * 3 * o_ch
    a_rows = (2 * a_levels * 3 + 1) * a_ch
    surface = pltpu.VMEM((4 * band, LANES), F32)
    weights = (flux_weight, temp_weight.reshape(1, a_ch))
    even_out, odd_out_o, odd_out_a, edge = call(
        force_halo_kernel,
        (
            shape((o_rows + a_rows, LANES), BF16), shape((o_rows, LANES), BF16),
            shape((a_rows, LANES), BF16), shape((a_ch, LANES), F32),
        ),
        [surface], "force_halo", 10**6, 4 * 10**6,
        *surface_args, got, ocean_grid, air_grid, *weights,
    )
    even = lax.ppermute(even_out, "lon", pairs_of(lons, 0))
    odd_o = lax.ppermute(odd_out_o, ("comp", "lon"), pairs_of(bands, 1))
    odd_a = lax.ppermute(odd_out_a, "lon", pairs_of(lons, 1))
    ocean_top, air_top, ocean_forced, air_forced = call(
        force_own_kernel,
        (
            shape((2, band, o_ch, LANES), F32), shape((2, band, a_ch, LANES), F32),
            shape(o_grid, BF16), shape(a_grid, BF16),
        ),
        [surface], "force_own", 10**6, 4 * 10**6,
        *surface_args, got, ocean_grid, air_grid, *weights,
    )

    (o_conv,) = convolution(conv_ocean_kernel, "conv_ocean", ocean_forced, even, odd_o, None, o_matrix)
    o_other = lax.ppermute(o_conv, "ch", ring(2, 1))
    a_convs = convolution(conv_air_kernel, "conv_air", air_forced, even, odd_a, edge, a_matrix)
    a_others = [lax.ppermute(part, "ch", ring(2, 1)) for part in a_convs]

    a_hid, o_hid = air_up.shape[1], ocean_up.shape[1]
    o_next = call(
        functools.partial(mlp_kernel, True, 0), shape(o_grid, BF16),
        [
            pltpu.VMEM((2, 2 * o_ch, 2 * LANES), F32), pltpu.VMEM((o_hid, 2 * o_ch), BF16),
            pltpu.VMEM((2 * o_ch, o_hid), BF16),
        ],
        "mlp_ocean", 10**9, 3 * 10**6,
        o_conv, o_other, ocean_gain.reshape(1, -1), ocean_up, ocean_down, ocean_top, ocean_forced,
        ocean_mask,
    )
    done = []
    a_convs, o_next = lax.optimization_barrier((a_convs, o_next))
    for level, (part, other) in enumerate(zip(a_convs, a_others)):
        a_next = call(
            functools.partial(mlp_kernel, False, level),
            shape((2, level + 1) + a_grid[2:], BF16),
            [
                pltpu.VMEM((2, 2 * a_ch, 2 * LANES), F32), pltpu.VMEM((a_hid, 2 * a_ch), BF16),
                pltpu.VMEM((2 * a_ch, a_hid), BF16),
            ],
            f"mlp_air{level}", 10**9, 3 * 10**6,
            part, other, air_gain.reshape(1, -1), air_up, air_down.T, air_top, air_forced, *done,
        )
        done = [a_next]
    ocean_next = jnp.transpose(o_next, (1, 3, 2, 0, 4)).reshape(ocean_state.shape)
    air_next = jnp.transpose(a_next, (1, 3, 2, 0, 4))
    return (ocean_next, air_next)


def solution(mesh):
    in_specs = (
        P(None, "ch", ("comp", "lon"), None),
        P(("comp", "lon"), None),
        P(None, "ch", "lon", None, "comp"),
        P(("comp", "lon"), None),
        P(None, "lon", None, "comp"),
        P("ch", None, None, None),
        P(),
        P(),
        P(),
        P("ch", None, None, None),
        P(),
        P(),
        P(),
        P(None, "ch"),
        P("ch"),
    )
    out_specs = (P(None, "ch", ("comp", "lon"), None), P(None, "ch", "lon", None, "comp"))
    return jax.shard_map(
        per_device, mesh=mesh, in_specs=in_specs, out_specs=out_specs, check_vma=False
    )
```

```python
import functools

import jax
import jax.numpy as jnp
from jax import lax
from jax.experimental import pallas as pl
from jax.experimental.pallas import tpu as pltpu
from jax.sharding import PartitionSpec as P

F32 = jnp.float32
BF16 = jnp.bfloat16
LANES = 128
TOGETHER = 4
PARAMS = pltpu.CompilerParams(vmem_limit_bytes=24 * 2**20)
VMEM = pl.BlockSpec(memory_space=pltpu.VMEM)


def lane_ids(rows):
    return lax.broadcasted_iota(jnp.int32, (rows, LANES), 1)


def column(row):
    n = row.shape[1]
    same = lax.broadcasted_iota(jnp.int32, (n, n), 0) == lax.broadcasted_iota(jnp.int32, (n, n), 1)
    return jnp.sum(jnp.where(same, row, 0.0), axis=1, keepdims=True)


def call(kernel, out_shape, scratch, name, flops, moved, *args):
    return pl.pallas_call(
        kernel,
        out_shape=out_shape,
        in_specs=[VMEM] * len(args),
        out_specs=jax.tree.map(lambda _: VMEM, out_shape),
        scratch_shapes=scratch,
        name=name,
        compiler_params=PARAMS,
        cost_estimate=pl.CostEstimate(flops=flops, bytes_accessed=moved, transcendentals=0),
    )(*args)


def rows_of(fields, band):
    temp = fields * band
    return temp, temp + 2 * band


def pack_kernel(mask_hbm, temp_hbm, flux_hbm, air_ref, out_ref, mask_ref, temp_ref, flux_ref, sems):
    copies = [
        pltpu.make_async_copy(mask_hbm, mask_ref, sems.at[0]),
        pltpu.make_async_copy(temp_hbm, temp_ref, sems.at[1]),
        pltpu.make_async_copy(flux_hbm, flux_ref, sems.at[2]),
    ]
    for copy in copies:
        copy.start()
    comp = lax.axis_index("comp")
    fields, band = flux_ref.shape[:2]
    temp_row, edge_row = rows_of(fields, band)
    levels, channels = air_ref.shape[1], air_ref.shape[3]
    start = jnp.where(comp == 0, LANES - 8, 0)
    lane = lane_ids(channels)
    packed = jnp.zeros((channels, LANES), F32)
    for level in range(levels):
        for h in range(2):
            for j in range(band):
                idx = (level * 2 + h) * band + j
                rolled = pltpu.roll(
                    air_ref[h, level, j].astype(F32), (8 * idx - start + LANES) & (LANES - 1), 1
                )
                packed = jnp.where((lane >> 3) == idx, rolled, packed)
    out_ref[edge_row : edge_row + channels, :] = packed
    for copy in copies:
        copy.wait()
    for k in range(fields):
        for j in range(band):
            at = k * band + j
            out_ref[at : at + 1, :] = flux_ref[k, j, pl.ds(1 - comp, 1), :]
    temp = temp_ref[...] * mask_ref[...].astype(F32)
    for s in range(2):
        lanes = slice(s * LANES, (s + 1) * LANES)
        out_ref[temp_row + s * band : temp_row + (s + 1) * band, :] = temp[:, lanes]


def fill_surface(mask_ref, temp_ref, surface_ref):
    band = mask_ref.shape[0]
    sea = mask_ref[...].astype(F32)
    temp = temp_ref[...] * sea
    for s in range(2):
        lanes = slice(s * LANES, (s + 1) * LANES)
        surface_ref[s * band : (s + 1) * band, :] = temp[:, lanes]
        surface_ref[(2 + s) * band : (3 + s) * band, :] = sea[:, lanes]


def inject_of(flux_ref, got_ref, fw, s, i):
    comp = lax.axis_index("comp")
    fields, band = flux_ref.shape[:2]
    total = None
    for k in range(fields):
        mine = flux_ref[k, i, pl.ds(comp, 1), :]
        theirs = got_ref[pl.ds(k * band + i, 1), :]
        term = fw[k] * jnp.where(comp == s, mine, theirs)
        total = term if total is None else total + term
    return total


def temp_of(surface_ref, got_ref, fields, band, h, s, j):
    comp = lax.axis_index("comp")
    temp_row = rows_of(fields, band)[0]
    mine = surface_ref[pl.ds(s * band + j, 1), :]
    theirs = got_ref[pl.ds(temp_row + s * band + j, 1), :]
    return jnp.where(comp == h, mine, theirs)


def force_halo_kernel(
    mask_ref, temp_ref, flux_ref, got_ref, ocean_ref, air_ref, fw_ref, tw_ref,
    even_ref, odd_ocean_ref, odd_air_ref, edge_ref, surface_ref,
):
    comp = lax.axis_index("comp")
    parity = lax.axis_index("lon") & 1
    fields, band = flux_ref.shape[:2]
    o_levels, o_ch = ocean_ref.shape[1], ocean_ref.shape[3]
    a_levels, a_ch = air_ref.shape[1], air_ref.shape[3]
    edge_row = rows_of(fields, band)[1]
    fill_surface(mask_ref, temp_ref, surface_ref)
    heat = column(tw_ref[...])
    fw = [column(fw_ref[k : k + 1, :]) for k in range(fields)]

    start = jnp.where(comp == 0, 0, LANES - 8)
    lane = lane_ids(8)
    edge_temp = jnp.zeros((8, LANES), F32)
    for h in range(2):
        for j in range(band):
            idx = h * band + j
            row = temp_of(surface_ref, got_ref, fields, band, h, 1 - comp, j)
            rolled = pltpu.roll(
                jnp.broadcast_to(row, (8, LANES)), (8 * idx - start + LANES) & (LANES - 1), 1
            )
            edge_temp = jnp.where((lane >> 3) == idx, rolled, edge_temp)
    edge = got_ref[edge_row : edge_row + a_ch, :] + heat * edge_temp[0:1, :]
    edge_ref[...] = edge

    first_air = 2 * o_levels * 3 * o_ch
    for ocean_out, air_out, base, offset in (
        (even_ref, even_ref, first_air, 1 - parity), (odd_ocean_ref, odd_air_ref, 0, parity)
    ):
        for j in range(3):
            col = j + offset
            for s in range(2):
                inject = inject_of(flux_ref, got_ref, fw, s, col)
                sea = surface_ref[pl.ds((2 + s) * band + col, 1), :]
                for level in range(o_levels):
                    tile = (s * o_levels + level) * 3 + j
                    value = ocean_ref[s, level, col].astype(F32)
                    if level == 0:
                        value = value + inject
                    ocean_out[tile * o_ch : (tile + 1) * o_ch, :] = (value * sea).astype(BF16)
            for h in range(2):
                row = temp_of(surface_ref, got_ref, fields, band, h, comp, col)
                for level in range(a_levels):
                    value = air_ref[h, level, col].astype(F32)
                    if level == 0:
                        value = value + heat * row
                    at = base + ((h * a_levels + level) * 3 + j) * a_ch
                    air_out[at : at + a_ch, :] = value.astype(BF16)
        at = base + 2 * a_levels * 3 * a_ch
        air_out[at : at + a_ch, :] = edge.astype(BF16)


def force_own_kernel(
    mask_ref, temp_ref, flux_ref, got_ref, ocean_ref, air_ref, fw_ref, tw_ref,
    fo_ref, fa_ref, ob_ref, ab_ref, surface_ref,
):
    comp = lax.axis_index("comp")
    fields, band = flux_ref.shape[:2]
    o_levels, a_levels = ocean_ref.shape[1], air_ref.shape[1]
    fill_surface(mask_ref, temp_ref, surface_ref)
    heat = column(tw_ref[...])
    fw = [column(fw_ref[k : k + 1, :]) for k in range(fields)]
    for s in range(2):
        for i in range(band):
            inject = inject_of(flux_ref, got_ref, fw, s, i)
            at = (2 + s) * band + i
            sea = surface_ref[at : at + 1, :]
            row = temp_of(surface_ref, got_ref, fields, band, s, comp, i)
            for level in range(o_levels):
                value = ocean_ref[s, level, i].astype(F32)
                if level == 0:
                    value = (value + inject) * sea
                    fo_ref[s, i] = value
                else:
                    value = value * sea
                ob_ref[s, level, i] = value.astype(BF16)
            for level in range(a_levels):
                value = air_ref[s, level, i].astype(F32)
                if level == 0:
                    value = value + heat * row
                    fa_ref[s, i] = value
                ab_ref[s, level, i] = value.astype(BF16)


TAPS = 7


def toeplitz_kernel(taps_ref, out_ref, rows_ref):
    groups, levels, _, depth = out_ref.shape
    channels = groups * 8
    for d in range(TAPS):
        rows_ref[d] = jnp.zeros(rows_ref.shape[1:], F32)
        for a in range(3):
            for b in range(TAPS):
                at = a * TAPS + b
                rows_ref[d, at : at + 1, :channels] = taps_ref[a, b, d : d + 1, :]
    window = rows_ref.shape[1]
    taps = [rows_ref[d].T[:channels].astype(BF16) for d in range(TAPS)]
    taps = jnp.concatenate(taps, axis=0)
    row = lax.broadcasted_iota(jnp.int32, (window, depth), 0)
    lane = lax.broadcasted_iota(jnp.int32, (window, depth), 1)
    from_level = lane // 80
    from_lon = (lane >> 3) - from_level * 10
    same = (lax.broadcasted_iota(jnp.int32, (8, depth), 1) & 7) == lax.broadcasted_iota(
        jnp.int32, (8, depth), 0
    )
    for level in range(levels):
        parts = []
        for side in range(2):
            a = from_level - level + 1
            b = from_lon - (pl.program_id(0) * 2 + side)
            hit = (
                (from_level < levels)
                & (a >= 0) & (a <= 2) & (b >= 0) & (b < TAPS) & (a * TAPS + b == row)
            )
            choose = jnp.where(hit, 1.0, 0.0).astype(BF16)
            parts.append(jnp.dot(taps, choose, preferred_element_type=F32))
        for g in range(groups):
            tiles = [
                jnp.where(same, part[d * channels + g * 8 : d * channels + g * 8 + 8], 0.0)
                for part in parts
                for d in range(TAPS)
            ]
            out_ref[g, level] = jnp.concatenate(tiles, axis=0).astype(BF16)


def both_toeplitz_kernel(o_ref, a_ref, o_out, a_out, o_rows, a_rows):
    toeplitz_kernel(a_ref, a_out, a_rows)
    toeplitz_kernel(o_ref, o_out, o_rows)


def rim_tile(even_ref, odd_ref, even_at, odd_at, count):
    even = even_ref[pl.ds(pl.multiple_of(even_at, 16), count), :]
    odd = odd_ref[pl.ds(pl.multiple_of(odd_at, 16), count), :]
    return even.astype(F32), odd.astype(F32)


def conv_ocean_kernel(own_ref, even_ref, odd_ref, matrix_ref, out_ref, product_ref):
    _, levels, band, count, _ = own_ref.shape
    depth = matrix_ref.shape[-1]
    lane = lane_ids(8)
    channels = pl.num_programs(0) * count
    first = pl.program_id(0) * count
    inner = (lax.axis_index("lon") & 1) == 1
    columns = []
    for s in range(2):
        tiles = []
        for level in range(levels):
            west, east = [], []
            for i in range(3):
                at = ((s * levels + level) * 3 + i) * channels + first
                even, odd = rim_tile(even_ref, odd_ref, at, at, count)
                west.append(jnp.where(inner, even, odd))
                east.append(jnp.where(inner, odd, even))
            own = [own_ref[s, level, i].astype(F32) for i in range(band)]
            tiles += west + own + east
        columns.append(tiles)
    for sub in range(count // 8):
        rows = slice(sub * 8, sub * 8 + 8)
        halves = []
        for tiles in columns:
            tiles = [tile[rows] for tile in tiles]
            if depth > len(tiles) * 8:
                tiles.append(jnp.zeros((depth - len(tiles) * 8, LANES), F32))
            halves.append(jnp.concatenate(tiles, axis=0))
        data = jnp.concatenate(halves, axis=1).astype(BF16)
        matrix = matrix_ref[sub].reshape(-1, depth)
        product_ref[...] = jnp.dot(matrix, data, preferred_element_type=F32)
        for level in range(levels):
            for i in range(band):
                base = ((i // 2 * levels + level) * 2 + i % 2) * TAPS
                sums = [None, None]
                for d in range(TAPS):
                    at = slice((base + d) * 8, (base + d) * 8 + 8)
                    first = product_ref[at, :LANES]
                    second = product_ref[at, LANES:]
                    off = d - 3
                    if off > 0:
                        first, second = (
                            pltpu.roll(jnp.where(lane < off, second, first), LANES - off, 1),
                            pltpu.roll(jnp.where(lane < off, 0.0, second), LANES - off, 1),
                        )
                    elif off < 0:
                        first, second = (
                            pltpu.roll(jnp.where(lane >= LANES + off, 0.0, first), -off, 1),
                            pltpu.roll(jnp.where(lane >= LANES + off, first, second), -off, 1),
                        )
                    sums = [
                        part if old is None else old + part
                        for old, part in zip(sums, (first, second))
                    ]
                for s in range(2):
                    out_ref[s, level, i, rows] = sums[s].astype(BF16)


def conv_air_kernel(own_ref, even_ref, odd_ref, packed_ref, matrix_ref, *refs):
    out_refs, product_ref = refs[:-1], refs[-1]
    _, levels, band, count, _ = own_ref.shape
    depth = matrix_ref.shape[-1]
    lon = lax.axis_index("lon")
    inner = (lon & 1) == 1
    swap_west = jnp.where(lon == 0, 1, 0)
    swap_east = jnp.where(lon == lax.axis_size("lon") - 1, 1, 0)
    first_odd = pl.program_id(0) * count
    first_even = first_odd + even_ref.shape[0] - odd_ref.shape[0]

    stride = 3 * levels * out_refs[0].shape[3] * pl.num_programs(0)

    def tiles_at(half, tile):
        at = tile * (stride // (3 * levels))
        moved = half * stride
        return rim_tile(even_ref, odd_ref, first_even + moved + at, first_odd + moved + at, count)

    start = jnp.where(lax.axis_index("comp") == 0, 0, LANES - 8)
    wide = lane_ids(count)
    even, odd = tiles_at(0, 2 * levels * 3)
    edge_tiles = []
    for tile, swap in (
        (packed_ref[...], None),
        (jnp.where(inner, even, odd), swap_west),
        (jnp.where(inner, odd, even), swap_east),
    ):
        if swap is not None:
            span = 8 * band
            other = jnp.where(
                (wide & span) == 0, pltpu.roll(tile, LANES - span, 1), pltpu.roll(tile, span, 1)
            )
            tile = jnp.where(swap == 1, other, tile)
        edge_tiles.append(pltpu.roll(tile, start, 1))
    lane = lane_ids(8)
    block = ((lane - start + LANES) & (LANES - 1)) >> 3
    adjoining = (block == 0) | (block == band)
    all_tiles = []
    for h in range(2):
        west_h = jnp.abs(h - swap_west)
        east_h = jnp.abs(h - swap_east)
        tiles = []
        for level in range(levels):
            west, east = [], []
            for i in range(3):
                even, odd = tiles_at(west_h, level * 3 + i)
                west.append(jnp.where(inner, even, odd))
                even, odd = tiles_at(east_h, level * 3 + i)
                east.append(jnp.where(inner, odd, even))
            tiles += west + [own_ref[h, level, i].astype(F32) for i in range(band)] + east
        all_tiles.append(tiles)
    beyond = []
    for level in range(levels):
        first = level * 2 * band
        beyond += [(1, first + i + band - 3) for i in range(3)]
        beyond += [(0, first + i) for i in range(band)]
        beyond += [(2, first + i) for i in range(3)]
    for sub in range(count // 8):
        rows = slice(sub * 8, sub * 8 + 8)
        columns = [[tile[rows] for tile in tiles] for tiles in all_tiles]
        packed = [tile[rows] for tile in edge_tiles]
        columns.append(
            [
                jnp.where(adjoining, pltpu.roll(packed[who], -8 * idx % LANES, 1), 0.0)
                for who, idx in beyond
            ]
        )
        pad = depth - len(columns[0]) * 8
        if pad:
            columns = [tiles + [jnp.zeros((pad, LANES), F32)] for tiles in columns]
        data = jnp.concatenate(
            [jnp.concatenate(tiles, axis=0) for tiles in columns], axis=1
        ).astype(BF16)
        matrix = matrix_ref[sub].reshape(-1, depth)
        product_ref[...] = jnp.dot(matrix, data, preferred_element_type=F32)
        for level in range(levels):
            for i in range(band):
                base = ((i // 2 * levels + level) * 2 + i % 2) * TAPS
                sums = [None, None]
                for d in range(TAPS):
                    at = slice((base + d) * 8, (base + d) * 8 + 8)
                    off = d - 3
                    edge = product_ref[at, 2 * LANES :] if off else None
                    for h in range(2):
                        part = product_ref[at, h * LANES : (h + 1) * LANES]
                        if off:
                            here = edge if h == 0 else pltpu.roll(edge, LANES - 8 * band, 1)
                            inside = lane < off if off > 0 else lane >= LANES + off
                            part = pltpu.roll(jnp.where(inside, here, part), (LANES - off) % LANES, 1)
                        sums[h] = part if sums[h] is None else sums[h] + part
                for h in range(2):
                    out_refs[level][h, 0, i, rows] = sums[h].astype(BF16)


def convolution(kernel, name, own, even, odd, packed, matrix):
    _, levels, band, channels, _ = own.shape
    groups, pairs, rows, depth = matrix.shape
    count = 16
    lane_tiles = 2 if packed is None else 3
    grid_spec = pl.BlockSpec((2, levels, band, count, LANES), lambda g: (0, 0, 0, g, 0))
    args = [own, even, odd]
    specs = [grid_spec] + [pl.BlockSpec(rim.shape, lambda g: (0, 0)) for rim in (even, odd)]
    outs = [levels] if packed is None else [1] * levels
    if packed is not None:
        args.append(packed)
        specs.append(pl.BlockSpec((count, LANES), lambda g: (g, 0)))
    args.append(matrix)
    specs.append(pl.BlockSpec((count // 8, pairs, rows, depth), lambda g: (g, 0, 0, 0)))
    return pl.pallas_call(
        kernel,
        grid=(channels // count,),
        out_shape=[jax.ShapeDtypeStruct((2, part) + own.shape[2:], BF16) for part in outs],
        in_specs=specs,
        out_specs=[
            pl.BlockSpec((2, part, band, count, LANES), lambda g: (0, 0, 0, g, 0)) for part in outs
        ],
        scratch_shapes=[pltpu.VMEM((pairs * rows, lane_tiles * LANES), F32)],
        name=name,
        compiler_params=PARAMS,
        cost_estimate=pl.CostEstimate(flops=2 * 10**9, bytes_accessed=4 * 10**6, transcendentals=0),
    )(*args)


def mlp_kernel(masked, first_level, *refs):
    own_ref, other_ref, gain_ref, up_ref, down_ref, top_ref, forced_ref = refs[:7]
    extra_ref = refs[7] if len(refs) > 11 else None
    out_ref, values_ref, wide_ref, narrow_ref = refs[-4:]
    _, levels, band, channels, _ = own_ref.shape
    ch = lax.axis_index("ch")
    total = 2 * channels
    gain = column(gain_ref[...])
    wide_ref[...] = up_ref[...].astype(F32).T.astype(BF16)
    mine = pl.ds(pl.multiple_of(ch * channels, channels), channels)
    if masked:
        narrow_ref[...] = down_ref[...].astype(F32).T.astype(BF16)
    else:
        narrow_ref[: channels] = down_ref[mine, :]
    down_rows = mine if masked else slice(0, channels)

    if not masked and extra_ref is not None:
        out_ref[:, :first_level] = extra_ref[...]
    theirs = pl.ds(pl.multiple_of((1 - ch) * channels, channels), channels)
    together = values_ref.shape[1] // (2 * LANES)
    if masked:
        sea = extra_ref[...].astype(F32)

    def step(at, carry):
        level = at // (band // together)
        first = lax.rem(at, band // together) * together
        blocks = [
            (s, n, slice((n * 2 + s) * LANES, (n * 2 + s + 1) * LANES))
            for n in range(together)
            for s in range(2)
        ]
        for s, n, lanes in blocks:
            values_ref[mine, lanes] = own_ref[s, level, first + n].astype(F32)
            values_ref[theirs, lanes] = other_ref[s, level, first + n].astype(F32)
        values = values_ref[...]
        center = jnp.sum(values, axis=0, keepdims=True) * (1.0 / total)
        values = values - center
        spread = jnp.sum(values * values, axis=0, keepdims=True) * (1.0 / total)
        normed = (values * lax.rsqrt(spread + 1e-06) * gain).astype(BF16)
        raw = jnp.dot(wide_ref[...], normed, preferred_element_type=F32)
        inner = raw * (0.7978845608028654 + 0.035677408136300125 * (raw * raw))
        doubled = (raw + raw * jnp.tanh(inner)).astype(BF16)
        update = jnp.dot(narrow_ref[down_rows, :], doubled, preferred_element_type=F32) * 0.5
        update = update.astype(BF16).astype(F32)
        for s, n, lanes in blocks:
            i = first + n
            if first_level:
                forced = forced_ref[s, first_level + level, i].astype(F32)
            else:
                forced = jnp.where(level == 0, top_ref[s, i], forced_ref[s, level, i].astype(F32))
            result = forced + update[:, lanes]
            if masked:
                half = sea[:, s * LANES : (s + 1) * LANES]
                picked = lax.broadcasted_iota(jnp.int32, half.shape, 0) == i
                result = result * jnp.sum(jnp.where(picked, half, 0.0), axis=0, keepdims=True)
            out_ref[s, first_level + level, i] = result.astype(BF16)
        return carry

    lax.fori_loop(0, levels * band // together, step, 0)


def toeplitz(ocean_kernel, air_kernel, o_levels, a_levels):
    taps = [jnp.transpose(kernel, (1, 2, 3, 0)) for kernel in (ocean_kernel, air_kernel)]
    shapes = [
        (part.shape[-1] // 8, levels, 2 * TAPS * 8, 256)
        for part, levels in zip(taps, (o_levels, a_levels))
    ]
    return pl.pallas_call(
        both_toeplitz_kernel,
        grid=(2,),
        out_shape=[
            jax.ShapeDtypeStruct((g, 2 * levels, rows, depth), BF16)
            for g, levels, rows, depth in shapes
        ],
        in_specs=[pl.BlockSpec(part.shape, lambda p: (0, 0, 0, 0)) for part in taps],
        out_specs=[pl.BlockSpec(block, lambda p: (0, p, 0, 0)) for block in shapes],
        scratch_shapes=[pltpu.VMEM((TAPS, LANES, LANES), F32)] * 2,
        name="matrix",
        compiler_params=PARAMS,
        cost_estimate=pl.CostEstimate(flops=2 * 10**9, bytes_accessed=6 * 10**6, transcendentals=0),
    )(*taps)


def pairs_of(count, first):
    pairs = []
    for i in range(first, count + first, 2):
        pairs += [(i % count, (i + 1) % count), ((i + 1) % count, i % count)]
    return pairs


def ring(count, step):
    return [(i, (i + step) % count) for i in range(count)]


def per_device(
    ocean_state, ocean_mask, air_state, surface_temp, air_fluxes, ocean_kernel, ocean_gain, ocean_up,
    ocean_down, air_kernel, air_gain, air_up, air_down, flux_weight, temp_weight,
):
    o_levels, o_ch, band, lats = ocean_state.shape
    a_levels, a_ch = air_state.shape[:2]
    fields = air_fluxes.shape[0]
    shape = jax.ShapeDtypeStruct

    air_grid = jnp.transpose(air_state, (3, 0, 2, 1, 4))
    o_grid = (2, o_levels, band, o_ch, LANES)
    a_grid = (2, a_levels, band, a_ch, LANES)

    lons = lax.axis_size("lon")
    bands = lax.axis_size("comp") * lons
    rows = rows_of(fields, band)[-1] + a_ch
    hbm = pl.BlockSpec(memory_space=pltpu.HBM)
    surface_args = (ocean_mask, surface_temp, air_fluxes)
    packed = pl.pallas_call(
        pack_kernel,
        out_shape=shape((rows, LANES), F32),
        in_specs=[hbm, hbm, hbm, VMEM],
        out_specs=VMEM,
        scratch_shapes=[pltpu.VMEM(arg.shape, arg.dtype) for arg in surface_args]
        + [pltpu.SemaphoreType.DMA((3,))],
        name="pack",
        compiler_params=pltpu.CompilerParams(vmem_limit_bytes=60 * 2**20),
    )(*surface_args, air_grid)
    got = lax.ppermute(packed, "comp", ring(2, 1))
    later_ocean, _ = lax.optimization_barrier((ocean_state, packed))
    ocean_grid = jnp.transpose(
        later_ocean.reshape(o_levels, o_ch, band, 2, LANES), (3, 0, 2, 1, 4)
    )
    ocean_grid, ocean_kernel = lax.optimization_barrier((ocean_grid, ocean_kernel))
    o_matrix, a_matrix = toeplitz(ocean_kernel, air_kernel, o_levels, a_levels)
    o_matrix, a_matrix, got = lax.optimization_barrier((o_matrix, a_matrix, got))
    o_rows = 2 * o_levels * 3 * o_ch
    a_rows = (2 * a_levels * 3 + 1) * a_ch
    surface = pltpu.VMEM((4 * band, LANES), F32)
    weights = (flux_weight, temp_weight.reshape(1, a_ch))
    even_out, odd_out_o, odd_out_a, edge = call(
        force_halo_kernel,
        (
            shape((o_rows + a_rows, LANES), BF16), shape((o_rows, LANES), BF16),
            shape((a_rows, LANES), BF16), shape((a_ch, LANES), F32),
        ),
        [surface], "force_halo", 10**6, 4 * 10**6,
        *surface_args, got, ocean_grid, air_grid, *weights,
    )
    even = lax.ppermute(even_out, "lon", pairs_of(lons, 0))
    odd_o = lax.ppermute(odd_out_o, ("comp", "lon"), pairs_of(bands, 1))
    odd_a = lax.ppermute(odd_out_a, "lon", pairs_of(lons, 1))
    ocean_top, air_top, ocean_forced, air_forced = call(
        force_own_kernel,
        (
            shape((2, band, o_ch, LANES), F32), shape((2, band, a_ch, LANES), F32),
            shape(o_grid, BF16), shape(a_grid, BF16),
        ),
        [surface], "force_own", 10**6, 4 * 10**6,
        *surface_args, got, ocean_grid, air_grid, *weights,
    )

    (o_conv,) = convolution(conv_ocean_kernel, "conv_ocean", ocean_forced, even, odd_o, None, o_matrix)
    o_other = lax.ppermute(o_conv, "ch", ring(2, 1))
    a_convs = convolution(conv_air_kernel, "conv_air", air_forced, even, odd_a, edge, a_matrix)
    a_others = [lax.ppermute(part, "ch", ring(2, 1)) for part in a_convs]

    a_hid, o_hid = air_up.shape[1], ocean_up.shape[1]
    o_next = call(
        functools.partial(mlp_kernel, True, 0), shape(o_grid, BF16),
        [
            pltpu.VMEM((2 * o_ch, TOGETHER * 2 * LANES), F32), pltpu.VMEM((o_hid, 2 * o_ch), BF16),
            pltpu.VMEM((2 * o_ch, o_hid), BF16),
        ],
        "mlp_ocean", 10**9, 3 * 10**6,
        o_conv, o_other, ocean_gain.reshape(1, -1), ocean_up, ocean_down, ocean_top, ocean_forced,
        ocean_mask,
    )
    done = []
    a_convs, o_next = lax.optimization_barrier((a_convs, o_next))
    for level, (part, other) in enumerate(zip(a_convs, a_others)):
        a_next = call(
            functools.partial(mlp_kernel, False, level),
            shape((2, level + 1) + a_grid[2:], BF16),
            [
                pltpu.VMEM((2 * a_ch, TOGETHER * 2 * LANES), F32), pltpu.VMEM((a_hid, 2 * a_ch), BF16),
                pltpu.VMEM((2 * a_ch, a_hid), BF16),
            ],
            f"mlp_air{level}", 10**9, 3 * 10**6,
            part, other, air_gain.reshape(1, -1), air_up, air_down.T, air_top, air_forced, *done,
        )
        done = [a_next]
    ocean_next = jnp.transpose(o_next, (1, 3, 2, 0, 4)).reshape(ocean_state.shape)
    air_next = jnp.transpose(a_next, (1, 3, 2, 0, 4))
    return (ocean_next, air_next)


def solution(mesh):
    in_specs = (
        P(None, "ch", ("comp", "lon"), None),
        P(("comp", "lon"), None),
        P(None, "ch", "lon", None, "comp"),
        P(("comp", "lon"), None),
        P(None, "lon", None, "comp"),
        P("ch", None, None, None),
        P(),
        P(),
        P(),
        P("ch", None, None, None),
        P(),
        P(),
        P(),
        P(None, "ch"),
        P("ch"),
    )
    out_specs = (P(None, "ch", ("comp", "lon"), None), P(None, "ch", "lon", None, "comp"))
    return jax.shard_map(
        per_device, mesh=mesh, in_specs=in_specs, out_specs=out_specs, check_vma=False
    )
```

```python
import functools

import jax
import jax.numpy as jnp
from jax import lax
from jax.experimental import pallas as pl
from jax.experimental.pallas import tpu as pltpu
from jax.sharding import PartitionSpec as P

F32 = jnp.float32
BF16 = jnp.bfloat16
LANES = 128
TOGETHER = 4
PARAMS = pltpu.CompilerParams(vmem_limit_bytes=24 * 2**20)
VMEM = pl.BlockSpec(memory_space=pltpu.VMEM)


def lane_ids(rows):
    return lax.broadcasted_iota(jnp.int32, (rows, LANES), 1)


def column(row):
    n = row.shape[1]
    same = lax.broadcasted_iota(jnp.int32, (n, n), 0) == lax.broadcasted_iota(jnp.int32, (n, n), 1)
    return jnp.sum(jnp.where(same, row, 0.0), axis=1, keepdims=True)


def call(kernel, out_shape, scratch, name, flops, moved, *args):
    return pl.pallas_call(
        kernel,
        out_shape=out_shape,
        in_specs=[VMEM] * len(args),
        out_specs=jax.tree.map(lambda _: VMEM, out_shape),
        scratch_shapes=scratch,
        name=name,
        compiler_params=PARAMS,
        cost_estimate=pl.CostEstimate(flops=flops, bytes_accessed=moved, transcendentals=0),
    )(*args)


def rows_of(fields, band):
    temp = fields * band
    return temp, temp + 2 * band


def pack_kernel(small_ref, air_ref, out_ref):
    comp = lax.axis_index("comp")
    edge_row = small_ref.shape[0]
    out_ref[:edge_row, :] = small_ref[...]
    _, levels, band, channels, _ = air_ref.shape
    start = jnp.where(comp == 0, LANES - 8, 0)
    lane = lane_ids(channels)
    packed = jnp.zeros((channels, LANES), F32)
    for level in range(levels):
        for h in range(2):
            for j in range(band):
                idx = (level * 2 + h) * band + j
                rolled = pltpu.roll(
                    air_ref[h, level, j].astype(F32), (8 * idx - start + LANES) & (LANES - 1), 1
                )
                packed = jnp.where((lane >> 3) == idx, rolled, packed)
    out_ref[edge_row:, :] = packed


def fill_surface(mask_ref, temp_ref, surface_ref):
    band = mask_ref.shape[0]
    sea = mask_ref[...].astype(F32)
    temp = temp_ref[...] * sea
    for s in range(2):
        lanes = slice(s * LANES, (s + 1) * LANES)
        surface_ref[s * band : (s + 1) * band, :] = temp[:, lanes]
        surface_ref[(2 + s) * band : (3 + s) * band, :] = sea[:, lanes]


def inject_of(flux_ref, got_ref, fw, s, i):
    comp = lax.axis_index("comp")
    fields, band = flux_ref.shape[:2]
    total = None
    for k in range(fields):
        mine = flux_ref[k, i, pl.ds(comp, 1), :]
        theirs = got_ref[pl.ds(k * band + i, 1), :]
        term = fw[k] * jnp.where(comp == s, mine, theirs)
        total = term if total is None else total + term
    return total


def temp_of(surface_ref, got_ref, fields, band, h, s, j):
    comp = lax.axis_index("comp")
    temp_row = rows_of(fields, band)[0]
    mine = surface_ref[pl.ds(s * band + j, 1), :]
    theirs = got_ref[pl.ds(temp_row + s * band + j, 1), :]
    return jnp.where(comp == h, mine, theirs)


def force_halo_kernel(
    mask_ref, temp_ref, flux_ref, got_ref, ocean_ref, air_ref, fw_ref, tw_ref,
    even_ref, odd_ocean_ref, odd_air_ref, edge_ref, surface_ref,
):
    comp = lax.axis_index("comp")
    parity = lax.axis_index("lon") & 1
    fields, band = flux_ref.shape[:2]
    o_levels, o_ch = ocean_ref.shape[1], ocean_ref.shape[3]
    a_levels, a_ch = air_ref.shape[1], air_ref.shape[3]
    edge_row = rows_of(fields, band)[1]
    fill_surface(mask_ref, temp_ref, surface_ref)
    heat = column(tw_ref[...])
    fw = [column(fw_ref[k : k + 1, :]) for k in range(fields)]

    start = jnp.where(comp == 0, 0, LANES - 8)
    lane = lane_ids(8)
    edge_temp = jnp.zeros((8, LANES), F32)
    for h in range(2):
        for j in range(band):
            idx = h * band + j
            row = temp_of(surface_ref, got_ref, fields, band, h, 1 - comp, j)
            rolled = pltpu.roll(
                jnp.broadcast_to(row, (8, LANES)), (8 * idx - start + LANES) & (LANES - 1), 1
            )
            edge_temp = jnp.where((lane >> 3) == idx, rolled, edge_temp)
    edge = got_ref[edge_row : edge_row + a_ch, :] + heat * edge_temp[0:1, :]
    edge_ref[...] = edge

    first_air = 2 * o_levels * 3 * o_ch
    for ocean_out, air_out, base, offset in (
        (even_ref, even_ref, first_air, 1 - parity), (odd_ocean_ref, odd_air_ref, 0, parity)
    ):
        for j in range(3):
            col = j + offset
            for s in range(2):
                inject = inject_of(flux_ref, got_ref, fw, s, col)
                sea = surface_ref[pl.ds((2 + s) * band + col, 1), :]
                for level in range(o_levels):
                    tile = (s * o_levels + level) * 3 + j
                    value = ocean_ref[s, level, col].astype(F32)
                    if level == 0:
                        value = value + inject
                    ocean_out[tile * o_ch : (tile + 1) * o_ch, :] = (value * sea).astype(BF16)
            for h in range(2):
                row = temp_of(surface_ref, got_ref, fields, band, h, comp, col)
                for level in range(a_levels):
                    value = air_ref[h, level, col].astype(F32)
                    if level == 0:
                        value = value + heat * row
                    at = base + ((h * a_levels + level) * 3 + j) * a_ch
                    air_out[at : at + a_ch, :] = value.astype(BF16)
        at = base + 2 * a_levels * 3 * a_ch
        air_out[at : at + a_ch, :] = edge.astype(BF16)


def force_own_kernel(
    mask_ref, temp_ref, flux_ref, got_ref, ocean_ref, air_ref, fw_ref, tw_ref,
    fo_ref, fa_ref, ob_ref, ab_ref, surface_ref,
):
    comp = lax.axis_index("comp")
    fields, band = flux_ref.shape[:2]
    o_levels, a_levels = ocean_ref.shape[1], air_ref.shape[1]
    fill_surface(mask_ref, temp_ref, surface_ref)
    heat = column(tw_ref[...])
    fw = [column(fw_ref[k : k + 1, :]) for k in range(fields)]
    for s in range(2):
        for i in range(band):
            inject = inject_of(flux_ref, got_ref, fw, s, i)
            at = (2 + s) * band + i
            sea = surface_ref[at : at + 1, :]
            row = temp_of(surface_ref, got_ref, fields, band, s, comp, i)
            for level in range(o_levels):
                value = ocean_ref[s, level, i].astype(F32)
                if level == 0:
                    value = (value + inject) * sea
                    fo_ref[s, i] = value
                else:
                    value = value * sea
                ob_ref[s, level, i] = value.astype(BF16)
            for level in range(a_levels):
                value = air_ref[s, level, i].astype(F32)
                if level == 0:
                    value = value + heat * row
                    fa_ref[s, i] = value
                ab_ref[s, level, i] = value.astype(BF16)


TAPS = 7


def toeplitz_kernel(taps_ref, out_ref, rows_ref):
    groups, levels, _, depth = out_ref.shape
    channels = groups * 8
    for d in range(TAPS):
        rows_ref[d] = jnp.zeros(rows_ref.shape[1:], F32)
        for a in range(3):
            for b in range(TAPS):
                at = a * TAPS + b
                rows_ref[d, at : at + 1, :channels] = taps_ref[a, b, d : d + 1, :]
    window = rows_ref.shape[1]
    taps = [rows_ref[d].T[:channels].astype(BF16) for d in range(TAPS)]
    taps = jnp.concatenate(taps, axis=0)
    row = lax.broadcasted_iota(jnp.int32, (window, depth), 0)
    lane = lax.broadcasted_iota(jnp.int32, (window, depth), 1)
    from_level = lane // 80
    from_lon = (lane >> 3) - from_level * 10
    same = (lax.broadcasted_iota(jnp.int32, (8, depth), 1) & 7) == lax.broadcasted_iota(
        jnp.int32, (8, depth), 0
    )
    for level in range(levels):
        parts = []
        for side in range(2):
            a = from_level - level + 1
            b = from_lon - (pl.program_id(0) * 2 + side)
            hit = (
                (from_level < levels)
                & (a >= 0) & (a <= 2) & (b >= 0) & (b < TAPS) & (a * TAPS + b == row)
            )
            choose = jnp.where(hit, 1.0, 0.0).astype(BF16)
            parts.append(jnp.dot(taps, choose, preferred_element_type=F32))
        for g in range(groups):
            tiles = [
                jnp.where(same, part[d * channels + g * 8 : d * channels + g * 8 + 8], 0.0)
                for part in parts
                for d in range(TAPS)
            ]
            out_ref[g, level] = jnp.concatenate(tiles, axis=0).astype(BF16)


def both_toeplitz_kernel(o_ref, a_ref, o_out, a_out, o_rows, a_rows):
    toeplitz_kernel(a_ref, a_out, a_rows)
    toeplitz_kernel(o_ref, o_out, o_rows)


def rim_tile(even_ref, odd_ref, even_at, odd_at, count):
    even = even_ref[pl.ds(pl.multiple_of(even_at, 16), count), :]
    odd = odd_ref[pl.ds(pl.multiple_of(odd_at, 16), count), :]
    return even.astype(F32), odd.astype(F32)


def conv_ocean_kernel(own_ref, even_ref, odd_ref, matrix_ref, out_ref, product_ref):
    _, levels, band, count, _ = own_ref.shape
    depth = matrix_ref.shape[-1]
    lane = lane_ids(8)
    channels = pl.num_programs(0) * count
    first = pl.program_id(0) * count
    inner = (lax.axis_index("lon") & 1) == 1
    columns = []
    for s in range(2):
        tiles = []
        for level in range(levels):
            west, east = [], []
            for i in range(3):
                at = ((s * levels + level) * 3 + i) * channels + first
                even, odd = rim_tile(even_ref, odd_ref, at, at, count)
                west.append(jnp.where(inner, even, odd))
                east.append(jnp.where(inner, odd, even))
            own = [own_ref[s, level, i].astype(F32) for i in range(band)]
            tiles += west + own + east
        columns.append(tiles)
    for sub in range(count // 8):
        rows = slice(sub * 8, sub * 8 + 8)
        halves = []
        for tiles in columns:
            tiles = [tile[rows] for tile in tiles]
            if depth > len(tiles) * 8:
                tiles.append(jnp.zeros((depth - len(tiles) * 8, LANES), F32))
            halves.append(jnp.concatenate(tiles, axis=0))
        data = jnp.concatenate(halves, axis=1).astype(BF16)
        matrix = matrix_ref[sub].reshape(-1, depth)
        product_ref[sub % 2] = jnp.dot(matrix, data, preferred_element_type=F32)
        for level in range(levels):
            for i in range(band):
                base = ((i // 2 * levels + level) * 2 + i % 2) * TAPS
                sums = [None, None]
                for d in range(TAPS):
                    at = slice((base + d) * 8, (base + d) * 8 + 8)
                    first = product_ref[sub % 2, at, :LANES]
                    second = product_ref[sub % 2, at, LANES:]
                    off = d - 3
                    if off > 0:
                        first, second = (
                            pltpu.roll(jnp.where(lane < off, second, first), LANES - off, 1),
                            pltpu.roll(jnp.where(lane < off, 0.0, second), LANES - off, 1),
                        )
                    elif off < 0:
                        first, second = (
                            pltpu.roll(jnp.where(lane >= LANES + off, 0.0, first), -off, 1),
                            pltpu.roll(jnp.where(lane >= LANES + off, first, second), -off, 1),
                        )
                    sums = [
                        part if old is None else old + part
                        for old, part in zip(sums, (first, second))
                    ]
                for s in range(2):
                    out_ref[s, level, i, rows] = sums[s].astype(BF16)


def conv_air_kernel(own_ref, even_ref, odd_ref, packed_ref, matrix_ref, *refs):
    out_refs, product_ref = refs[:-1], refs[-1]
    _, levels, band, count, _ = own_ref.shape
    depth = matrix_ref.shape[-1]
    lon = lax.axis_index("lon")
    inner = (lon & 1) == 1
    swap_west = jnp.where(lon == 0, 1, 0)
    swap_east = jnp.where(lon == lax.axis_size("lon") - 1, 1, 0)
    first_odd = pl.program_id(0) * count
    first_even = first_odd + even_ref.shape[0] - odd_ref.shape[0]

    stride = 3 * levels * out_refs[0].shape[3] * pl.num_programs(0)

    def tiles_at(half, tile):
        at = tile * (stride // (3 * levels))
        moved = half * stride
        return rim_tile(even_ref, odd_ref, first_even + moved + at, first_odd + moved + at, count)

    start = jnp.where(lax.axis_index("comp") == 0, 0, LANES - 8)
    wide = lane_ids(count)
    even, odd = tiles_at(0, 2 * levels * 3)
    edge_tiles = []
    for tile, swap in (
        (packed_ref[...], None),
        (jnp.where(inner, even, odd), swap_west),
        (jnp.where(inner, odd, even), swap_east),
    ):
        if swap is not None:
            span = 8 * band
            other = jnp.where(
                (wide & span) == 0, pltpu.roll(tile, LANES - span, 1), pltpu.roll(tile, span, 1)
            )
            tile = jnp.where(swap == 1, other, tile)
        edge_tiles.append(pltpu.roll(tile, start, 1))
    lane = lane_ids(8)
    block = ((lane - start + LANES) & (LANES - 1)) >> 3
    adjoining = (block == 0) | (block == band)
    all_tiles = []
    for h in range(2):
        west_h = jnp.abs(h - swap_west)
        east_h = jnp.abs(h - swap_east)
        tiles = []
        for level in range(levels):
            west, east = [], []
            for i in range(3):
                even, odd = tiles_at(west_h, level * 3 + i)
                west.append(jnp.where(inner, even, odd))
                even, odd = tiles_at(east_h, level * 3 + i)
                east.append(jnp.where(inner, odd, even))
            tiles += west + [own_ref[h, level, i].astype(F32) for i in range(band)] + east
        all_tiles.append(tiles)
    beyond = []
    for level in range(levels):
        first = level * 2 * band
        beyond += [(1, first + i + band - 3) for i in range(3)]
        beyond += [(0, first + i) for i in range(band)]
        beyond += [(2, first + i) for i in range(3)]
    for sub in range(count // 8):
        rows = slice(sub * 8, sub * 8 + 8)
        columns = [[tile[rows] for tile in tiles] for tiles in all_tiles]
        packed = [tile[rows] for tile in edge_tiles]
        columns.append(
            [
                jnp.where(adjoining, pltpu.roll(packed[who], -8 * idx % LANES, 1), 0.0)
                for who, idx in beyond
            ]
        )
        pad = depth - len(columns[0]) * 8
        if pad:
            columns = [tiles + [jnp.zeros((pad, LANES), F32)] for tiles in columns]
        data = jnp.concatenate(
            [jnp.concatenate(tiles, axis=0) for tiles in columns], axis=1
        ).astype(BF16)
        matrix = matrix_ref[sub].reshape(-1, depth)
        product_ref[sub % 2] = jnp.dot(matrix, data, preferred_element_type=F32)
        for level in range(levels):
            for i in range(band):
                base = ((i // 2 * levels + level) * 2 + i % 2) * TAPS
                sums = [None, None]
                for d in range(TAPS):
                    at = slice((base + d) * 8, (base + d) * 8 + 8)
                    off = d - 3
                    edge = product_ref[sub % 2, at, 2 * LANES :] if off else None
                    for h in range(2):
                        part = product_ref[sub % 2, at, h * LANES : (h + 1) * LANES]
                        if off:
                            here = edge if h == 0 else pltpu.roll(edge, LANES - 8 * band, 1)
                            inside = lane < off if off > 0 else lane >= LANES + off
                            part = pltpu.roll(jnp.where(inside, here, part), (LANES - off) % LANES, 1)
                        sums[h] = part if sums[h] is None else sums[h] + part
                for h in range(2):
                    out_refs[level][h, 0, i, rows] = sums[h].astype(BF16)


def convolution(kernel, name, own, even, odd, packed, matrix):
    _, levels, band, channels, _ = own.shape
    groups, pairs, rows, depth = matrix.shape
    count = 32
    lane_tiles = 2 if packed is None else 3
    grid_spec = pl.BlockSpec((2, levels, band, count, LANES), lambda g: (0, 0, 0, g, 0))
    args = [own, even, odd]
    specs = [grid_spec] + [pl.BlockSpec(rim.shape, lambda g: (0, 0)) for rim in (even, odd)]
    outs = [levels] if packed is None else [1] * levels
    if packed is not None:
        args.append(packed)
        specs.append(pl.BlockSpec((count, LANES), lambda g: (g, 0)))
    args.append(matrix)
    specs.append(pl.BlockSpec((count // 8, pairs, rows, depth), lambda g: (g, 0, 0, 0)))
    return pl.pallas_call(
        kernel,
        grid=(channels // count,),
        out_shape=[jax.ShapeDtypeStruct((2, part) + own.shape[2:], BF16) for part in outs],
        in_specs=specs,
        out_specs=[
            pl.BlockSpec((2, part, band, count, LANES), lambda g: (0, 0, 0, g, 0)) for part in outs
        ],
        scratch_shapes=[pltpu.VMEM((2, pairs * rows, lane_tiles * LANES), F32)],
        name=name,
        compiler_params=PARAMS,
        cost_estimate=pl.CostEstimate(flops=2 * 10**9, bytes_accessed=4 * 10**6, transcendentals=0),
    )(*args)


def mlp_kernel(masked, first_level, *refs):
    own_ref, other_ref, gain_ref, up_ref, down_ref, top_ref, forced_ref = refs[:7]
    extra_ref = refs[7] if len(refs) > 11 else None
    out_ref, values_ref, wide_ref, narrow_ref = refs[-4:]
    _, levels, band, channels, _ = own_ref.shape
    ch = lax.axis_index("ch")
    total = 2 * channels
    gain = column(gain_ref[...])
    wide_ref[...] = up_ref[...].astype(F32).T.astype(BF16)
    mine = pl.ds(pl.multiple_of(ch * channels, channels), channels)
    if masked:
        narrow_ref[...] = down_ref[...].astype(F32).T.astype(BF16)
    else:
        narrow_ref[: channels] = down_ref[mine, :]
    down_rows = mine if masked else slice(0, channels)

    if not masked and extra_ref is not None:
        out_ref[:, :first_level] = extra_ref[...]
    theirs = pl.ds(pl.multiple_of((1 - ch) * channels, channels), channels)
    together = values_ref.shape[1] // (2 * LANES)
    if masked:
        sea = extra_ref[...].astype(F32)

    def step(at, carry):
        level = at // (band // together)
        first = lax.rem(at, band // together) * together
        blocks = [
            (s, n, slice((n * 2 + s) * LANES, (n * 2 + s + 1) * LANES))
            for n in range(together)
            for s in range(2)
        ]
        for s, n, lanes in blocks:
            values_ref[mine, lanes] = own_ref[s, level, first + n].astype(F32)
            values_ref[theirs, lanes] = other_ref[s, level, first + n].astype(F32)
        values = values_ref[...]
        center = jnp.sum(values, axis=0, keepdims=True) * (1.0 / total)
        values = values - center
        spread = jnp.sum(values * values, axis=0, keepdims=True) * (1.0 / total)
        normed = (values * lax.rsqrt(spread + 1e-06) * gain).astype(BF16)
        raw = jnp.dot(wide_ref[...], normed, preferred_element_type=F32)
        inner = raw * (0.7978845608028654 + 0.035677408136300125 * (raw * raw))
        doubled = (raw + raw * jnp.tanh(inner)).astype(BF16)
        update = jnp.dot(narrow_ref[down_rows, :], doubled, preferred_element_type=F32) * 0.5
        update = update.astype(BF16).astype(F32)
        for s, n, lanes in blocks:
            i = first + n
            if first_level:
                forced = forced_ref[s, first_level + level, i].astype(F32)
            else:
                forced = jnp.where(level == 0, top_ref[s, i], forced_ref[s, level, i].astype(F32))
            result = forced + update[:, lanes]
            if masked:
                half = sea[:, s * LANES : (s + 1) * LANES]
                picked = lax.broadcasted_iota(jnp.int32, half.shape, 0) == i
                result = result * jnp.sum(jnp.where(picked, half, 0.0), axis=0, keepdims=True)
            if masked:
                out_ref[level, i, :, s * LANES : (s + 1) * LANES] = result.astype(BF16)
            else:
                out_ref[s, first_level + level, i] = result.astype(BF16)
        return carry

    lax.fori_loop(0, levels * band // together, step, 0)


def toeplitz(ocean_kernel, air_kernel, o_levels, a_levels):
    taps = [jnp.transpose(kernel, (1, 2, 3, 0)) for kernel in (ocean_kernel, air_kernel)]
    shapes = [
        (part.shape[-1] // 8, levels, 2 * TAPS * 8, 256)
        for part, levels in zip(taps, (o_levels, a_levels))
    ]
    return pl.pallas_call(
        both_toeplitz_kernel,
        grid=(2,),
        out_shape=[
            jax.ShapeDtypeStruct((g, 2 * levels, rows, depth), BF16)
            for g, levels, rows, depth in shapes
        ],
        in_specs=[pl.BlockSpec(part.shape, lambda p: (0, 0, 0, 0)) for part in taps],
        out_specs=[pl.BlockSpec(block, lambda p: (0, p, 0, 0)) for block in shapes],
        scratch_shapes=[pltpu.VMEM((TAPS, LANES, LANES), F32)] * 2,
        name="matrix",
        compiler_params=PARAMS,
        cost_estimate=pl.CostEstimate(flops=2 * 10**9, bytes_accessed=6 * 10**6, transcendentals=0),
    )(*taps)


def pairs_of(count, first):
    pairs = []
    for i in range(first, count + first, 2):
        pairs += [(i % count, (i + 1) % count), ((i + 1) % count, i % count)]
    return pairs


def ring(count, step):
    return [(i, (i + step) % count) for i in range(count)]


def per_device(
    ocean_state, ocean_mask, air_state, surface_temp, air_fluxes, ocean_kernel, ocean_gain, ocean_up,
    ocean_down, air_kernel, air_gain, air_up, air_down, flux_weight, temp_weight,
):
    o_levels, o_ch, band, lats = ocean_state.shape
    a_levels, a_ch = air_state.shape[:2]
    fields = air_fluxes.shape[0]
    shape = jax.ShapeDtypeStruct

    air_grid = jnp.transpose(air_state, (3, 0, 2, 1, 4))
    o_grid = (2, o_levels, band, o_ch, LANES)
    a_grid = (2, a_levels, band, a_ch, LANES)

    lons = lax.axis_size("lon")
    bands = lax.axis_size("comp") * lons
    rows = rows_of(fields, band)[-1] + a_ch
    surface_args = (ocean_mask, surface_temp, air_fluxes)
    partner = 1 - lax.axis_index("comp")
    temp_rows = (surface_temp * ocean_mask.astype(F32)).reshape(band, 2, LANES)
    small = jnp.concatenate(
        [
            lax.dynamic_index_in_dim(air_fluxes, partner, 2, False).reshape(-1, LANES),
            jnp.transpose(temp_rows, (1, 0, 2)).reshape(-1, LANES),
        ]
    )
    packed = call(
        pack_kernel, shape((rows, LANES), F32), [], "pack", 10**5, 10**6, small, air_grid
    )
    got = lax.ppermute(packed, "comp", ring(2, 1))
    later_ocean, _ = lax.optimization_barrier((ocean_state, packed))
    ocean_grid = jnp.transpose(
        later_ocean.reshape(o_levels, o_ch, band, 2, LANES), (3, 0, 2, 1, 4)
    )
    ocean_grid, ocean_kernel = lax.optimization_barrier((ocean_grid, ocean_kernel))
    o_matrix, a_matrix = toeplitz(ocean_kernel, air_kernel, o_levels, a_levels)
    o_matrix, a_matrix, got = lax.optimization_barrier((o_matrix, a_matrix, got))
    o_rows = 2 * o_levels * 3 * o_ch
    a_rows = (2 * a_levels * 3 + 1) * a_ch
    surface = pltpu.VMEM((4 * band, LANES), F32)
    weights = (flux_weight, temp_weight.reshape(1, a_ch))
    even_out, odd_out_o, odd_out_a, edge = call(
        force_halo_kernel,
        (
            shape((o_rows + a_rows, LANES), BF16), shape((o_rows, LANES), BF16),
            shape((a_rows, LANES), BF16), shape((a_ch, LANES), F32),
        ),
        [surface], "force_halo", 10**6, 4 * 10**6,
        *surface_args, got, ocean_grid, air_grid, *weights,
    )
    even = lax.ppermute(even_out, "lon", pairs_of(lons, 0))
    odd_o = lax.ppermute(odd_out_o, ("comp", "lon"), pairs_of(bands, 1))
    odd_a = lax.ppermute(odd_out_a, "lon", pairs_of(lons, 1))
    ocean_top, air_top, ocean_forced, air_forced = call(
        force_own_kernel,
        (
            shape((2, band, o_ch, LANES), F32), shape((2, band, a_ch, LANES), F32),
            shape(o_grid, BF16), shape(a_grid, BF16),
        ),
        [surface], "force_own", 10**6, 4 * 10**6,
        *surface_args, got, ocean_grid, air_grid, *weights,
    )

    (o_conv,) = convolution(conv_ocean_kernel, "conv_ocean", ocean_forced, even, odd_o, None, o_matrix)
    o_other = lax.ppermute(o_conv, "ch", ring(2, 1))
    a_convs = convolution(conv_air_kernel, "conv_air", air_forced, even, odd_a, edge, a_matrix)
    a_others = [lax.ppermute(part, "ch", ring(2, 1)) for part in a_convs]

    a_hid, o_hid = air_up.shape[1], ocean_up.shape[1]
    o_next = call(
        functools.partial(mlp_kernel, True, 0), shape((o_levels, band, o_ch, lats), BF16),
        [
            pltpu.VMEM((2 * o_ch, TOGETHER * 2 * LANES), F32), pltpu.VMEM((o_hid, 2 * o_ch), BF16),
            pltpu.VMEM((2 * o_ch, o_hid), BF16),
        ],
        "mlp_ocean", 10**9, 3 * 10**6,
        o_conv, o_other, ocean_gain.reshape(1, -1), ocean_up, ocean_down, ocean_top, ocean_forced,
        ocean_mask,
    )
    done = []
    a_convs, o_next = lax.optimization_barrier((a_convs, o_next))
    for level, (part, other) in enumerate(zip(a_convs, a_others)):
        a_next = call(
            functools.partial(mlp_kernel, False, level),
            shape((2, level + 1) + a_grid[2:], BF16),
            [
                pltpu.VMEM((2 * a_ch, TOGETHER * 2 * LANES), F32), pltpu.VMEM((a_hid, 2 * a_ch), BF16),
                pltpu.VMEM((2 * a_ch, a_hid), BF16),
            ],
            f"mlp_air{level}", 10**9, 3 * 10**6,
            part, other, air_gain.reshape(1, -1), air_up, air_down.T, air_top, air_forced, *done,
        )
        done = [a_next]
    ocean_next = jnp.transpose(o_next, (0, 2, 1, 3))
    air_next = jnp.transpose(a_next, (1, 3, 2, 0, 4))
    return (ocean_next, air_next)


def solution(mesh):
    in_specs = (
        P(None, "ch", ("comp", "lon"), None),
        P(("comp", "lon"), None),
        P(None, "ch", "lon", None, "comp"),
        P(("comp", "lon"), None),
        P(None, "lon", None, "comp"),
        P("ch", None, None, None),
        P(),
        P(),
        P(),
        P("ch", None, None, None),
        P(),
        P(),
        P(),
        P(None, "ch"),
        P("ch"),
    )
    out_specs = (P(None, "ch", ("comp", "lon"), None), P(None, "ch", "lon", None, "comp"))
    return jax.shard_map(
        per_device, mesh=mesh, in_specs=in_specs, out_specs=out_specs, check_vma=False
    )
```

```python
import functools

import jax
import jax.numpy as jnp
from jax import lax
from jax.experimental import pallas as pl
from jax.experimental.pallas import tpu as pltpu
from jax.sharding import PartitionSpec as P

F32 = jnp.float32
BF16 = jnp.bfloat16
LANES = 128
OCEAN_TOGETHER = 12
TOGETHER = 4
PARAMS = pltpu.CompilerParams(vmem_limit_bytes=24 * 2**20)
VMEM = pl.BlockSpec(memory_space=pltpu.VMEM)


def lane_ids(rows):
    return lax.broadcasted_iota(jnp.int32, (rows, LANES), 1)


def column(row):
    n = row.shape[1]
    same = lax.broadcasted_iota(jnp.int32, (n, n), 0) == lax.broadcasted_iota(jnp.int32, (n, n), 1)
    return jnp.sum(jnp.where(same, row, 0.0), axis=1, keepdims=True)


def call(kernel, out_shape, scratch, name, flops, moved, *args):
    return pl.pallas_call(
        kernel,
        out_shape=out_shape,
        in_specs=[VMEM] * len(args),
        out_specs=jax.tree.map(lambda _: VMEM, out_shape),
        scratch_shapes=scratch,
        name=name,
        compiler_params=PARAMS,
        cost_estimate=pl.CostEstimate(flops=flops, bytes_accessed=moved, transcendentals=0),
    )(*args)


def rows_of(fields, band):
    temp = fields * band
    return temp, temp + 2 * band


def pack_kernel(small_ref, air_ref, out_ref):
    comp = lax.axis_index("comp")
    edge_row = small_ref.shape[0]
    out_ref[:edge_row, :] = small_ref[...]
    _, levels, band, channels, _ = air_ref.shape
    start = jnp.where(comp == 0, LANES - 8, 0)
    lane = lane_ids(channels)
    packed = jnp.zeros((channels, LANES), F32)
    for level in range(levels):
        for h in range(2):
            for j in range(band):
                idx = (level * 2 + h) * band + j
                rolled = pltpu.roll(
                    air_ref[h, level, j].astype(F32), (8 * idx - start + LANES) & (LANES - 1), 1
                )
                packed = jnp.where((lane >> 3) == idx, rolled, packed)
    out_ref[edge_row:, :] = packed


def fill_surface(mask_ref, temp_ref, surface_ref):
    band = mask_ref.shape[0]
    sea = mask_ref[...].astype(F32)
    temp = temp_ref[...] * sea
    for s in range(2):
        lanes = slice(s * LANES, (s + 1) * LANES)
        surface_ref[s * band : (s + 1) * band, :] = temp[:, lanes]
        surface_ref[(2 + s) * band : (3 + s) * band, :] = sea[:, lanes]


def inject_of(flux_ref, got_ref, fw, s, i):
    comp = lax.axis_index("comp")
    fields, band = flux_ref.shape[:2]
    total = None
    for k in range(fields):
        mine = flux_ref[k, i, pl.ds(comp, 1), :]
        theirs = got_ref[pl.ds(k * band + i, 1), :]
        term = fw[k] * jnp.where(comp == s, mine, theirs)
        total = term if total is None else total + term
    return total


def temp_of(surface_ref, got_ref, fields, band, h, s, j):
    comp = lax.axis_index("comp")
    temp_row = rows_of(fields, band)[0]
    mine = surface_ref[pl.ds(s * band + j, 1), :]
    theirs = got_ref[pl.ds(temp_row + s * band + j, 1), :]
    return jnp.where(comp == h, mine, theirs)


def force_halo_kernel(
    mask_ref, temp_ref, flux_ref, got_ref, ocean_ref, air_ref, fw_ref, tw_ref,
    even_ref, odd_ocean_ref, odd_air_ref, edge_ref, surface_ref,
):
    comp = lax.axis_index("comp")
    parity = lax.axis_index("lon") & 1
    fields, band = flux_ref.shape[:2]
    o_levels, o_ch = ocean_ref.shape[1], ocean_ref.shape[3]
    a_levels, a_ch = air_ref.shape[1], air_ref.shape[3]
    edge_row = rows_of(fields, band)[1]
    fill_surface(mask_ref, temp_ref, surface_ref)
    heat = column(tw_ref[...])
    fw = [column(fw_ref[k : k + 1, :]) for k in range(fields)]

    start = jnp.where(comp == 0, 0, LANES - 8)
    lane = lane_ids(8)
    edge_temp = jnp.zeros((8, LANES), F32)
    for h in range(2):
        for j in range(band):
            idx = h * band + j
            row = temp_of(surface_ref, got_ref, fields, band, h, 1 - comp, j)
            rolled = pltpu.roll(
                jnp.broadcast_to(row, (8, LANES)), (8 * idx - start + LANES) & (LANES - 1), 1
            )
            edge_temp = jnp.where((lane >> 3) == idx, rolled, edge_temp)
    edge = got_ref[edge_row : edge_row + a_ch, :] + heat * edge_temp[0:1, :]
    edge_ref[...] = edge

    first_air = 2 * o_levels * 3 * o_ch
    for ocean_out, air_out, base, offset in (
        (even_ref, even_ref, first_air, 1 - parity), (odd_ocean_ref, odd_air_ref, 0, parity)
    ):
        for j in range(3):
            col = j + offset
            for s in range(2):
                inject = inject_of(flux_ref, got_ref, fw, s, col)
                sea = surface_ref[pl.ds((2 + s) * band + col, 1), :]
                for level in range(o_levels):
                    tile = (s * o_levels + level) * 3 + j
                    value = ocean_ref[s, level, col].astype(F32)
                    if level == 0:
                        value = value + inject
                    ocean_out[tile * o_ch : (tile + 1) * o_ch, :] = (value * sea).astype(BF16)
            for h in range(2):
                row = temp_of(surface_ref, got_ref, fields, band, h, comp, col)
                for level in range(a_levels):
                    value = air_ref[h, level, col].astype(F32)
                    if level == 0:
                        value = value + heat * row
                    at = base + ((h * a_levels + level) * 3 + j) * a_ch
                    air_out[at : at + a_ch, :] = value.astype(BF16)
        at = base + 2 * a_levels * 3 * a_ch
        air_out[at : at + a_ch, :] = edge.astype(BF16)


def force_own_kernel(
    mask_ref, temp_ref, flux_ref, got_ref, ocean_ref, air_ref, fw_ref, tw_ref,
    fo_ref, fa_ref, ob_ref, ab_ref, surface_ref,
):
    comp = lax.axis_index("comp")
    fields, band = flux_ref.shape[:2]
    o_levels, a_levels = ocean_ref.shape[1], air_ref.shape[1]
    fill_surface(mask_ref, temp_ref, surface_ref)
    heat = column(tw_ref[...])
    fw = [column(fw_ref[k : k + 1, :]) for k in range(fields)]
    for s in range(2):
        for i in range(band):
            inject = inject_of(flux_ref, got_ref, fw, s, i)
            at = (2 + s) * band + i
            sea = surface_ref[at : at + 1, :]
            row = temp_of(surface_ref, got_ref, fields, band, s, comp, i)
            for level in range(o_levels):
                value = ocean_ref[s, level, i].astype(F32)
                if level == 0:
                    value = (value + inject) * sea
                    fo_ref[s, i] = value
                else:
                    value = value * sea
                ob_ref[s, level, i] = value.astype(BF16)
            for level in range(a_levels):
                value = air_ref[s, level, i].astype(F32)
                if level == 0:
                    value = value + heat * row
                    fa_ref[s, i] = value
                ab_ref[s, level, i] = value.astype(BF16)


TAPS = 7


def toeplitz_kernel(taps_ref, out_ref, rows_ref):
    groups, levels, _, depth = out_ref.shape
    channels = groups * 8
    for d in range(TAPS):
        rows_ref[d] = jnp.zeros(rows_ref.shape[1:], F32)
        for a in range(3):
            for b in range(TAPS):
                at = a * TAPS + b
                rows_ref[d, at : at + 1, :channels] = taps_ref[a, b, d : d + 1, :]
    window = rows_ref.shape[1]
    taps = [rows_ref[d].T[:channels].astype(BF16) for d in range(TAPS)]
    taps = jnp.concatenate(taps, axis=0)
    row = lax.broadcasted_iota(jnp.int32, (window, depth), 0)
    lane = lax.broadcasted_iota(jnp.int32, (window, depth), 1)
    from_level = lane // 80
    from_lon = (lane >> 3) - from_level * 10
    same = (lax.broadcasted_iota(jnp.int32, (8, depth), 1) & 7) == lax.broadcasted_iota(
        jnp.int32, (8, depth), 0
    )
    for level in range(levels):
        parts = []
        for side in range(2):
            a = from_level - level + 1
            b = from_lon - (pl.program_id(0) * 2 + side)
            hit = (
                (from_level < levels)
                & (a >= 0) & (a <= 2) & (b >= 0) & (b < TAPS) & (a * TAPS + b == row)
            )
            choose = jnp.where(hit, 1.0, 0.0).astype(BF16)
            parts.append(jnp.dot(taps, choose, preferred_element_type=F32))
        for g in range(groups):
            tiles = [
                jnp.where(same, part[d * channels + g * 8 : d * channels + g * 8 + 8], 0.0)
                for part in parts
                for d in range(TAPS)
            ]
            out_ref[g, level] = jnp.concatenate(tiles, axis=0).astype(BF16)


def both_toeplitz_kernel(o_ref, a_ref, o_out, a_out, o_rows, a_rows):
    toeplitz_kernel(a_ref, a_out, a_rows)
    toeplitz_kernel(o_ref, o_out, o_rows)


def rim_tile(even_ref, odd_ref, even_at, odd_at, count):
    even = even_ref[pl.ds(pl.multiple_of(even_at, 16), count), :]
    odd = odd_ref[pl.ds(pl.multiple_of(odd_at, 16), count), :]
    return even.astype(F32), odd.astype(F32)


def conv_ocean_kernel(own_ref, even_ref, odd_ref, matrix_ref, out_ref, product_ref):
    _, levels, band, count, _ = own_ref.shape
    depth = matrix_ref.shape[-1]
    lane = lane_ids(8)
    channels = pl.num_programs(0) * count
    first = pl.program_id(0) * count
    inner = (lax.axis_index("lon") & 1) == 1
    columns = []
    for s in range(2):
        tiles = []
        for level in range(levels):
            west, east = [], []
            for i in range(3):
                at = ((s * levels + level) * 3 + i) * channels + first
                even, odd = rim_tile(even_ref, odd_ref, at, at, count)
                west.append(jnp.where(inner, even, odd))
                east.append(jnp.where(inner, odd, even))
            own = [own_ref[s, level, i].astype(F32) for i in range(band)]
            tiles += west + own + east
        columns.append(tiles)
    for sub in range(count // 8):
        rows = slice(sub * 8, sub * 8 + 8)
        halves = []
        for tiles in columns:
            tiles = [tile[rows] for tile in tiles]
            if depth > len(tiles) * 8:
                tiles.append(jnp.zeros((depth - len(tiles) * 8, LANES), F32))
            halves.append(jnp.concatenate(tiles, axis=0))
        data = jnp.concatenate(halves, axis=1).astype(BF16)
        matrix = matrix_ref[sub].reshape(-1, depth)
        product_ref[sub % 2] = jnp.dot(matrix, data, preferred_element_type=F32)
        for level in range(levels):
            for i in range(band):
                base = ((i // 2 * levels + level) * 2 + i % 2) * TAPS
                sums = [None, None]
                for d in range(TAPS):
                    at = slice((base + d) * 8, (base + d) * 8 + 8)
                    first = product_ref[sub % 2, at, :LANES]
                    second = product_ref[sub % 2, at, LANES:]
                    off = d - 3
                    if off > 0:
                        first, second = (
                            pltpu.roll(jnp.where(lane < off, second, first), LANES - off, 1),
                            pltpu.roll(jnp.where(lane < off, 0.0, second), LANES - off, 1),
                        )
                    elif off < 0:
                        first, second = (
                            pltpu.roll(jnp.where(lane >= LANES + off, 0.0, first), -off, 1),
                            pltpu.roll(jnp.where(lane >= LANES + off, first, second), -off, 1),
                        )
                    sums = [
                        part if old is None else old + part
                        for old, part in zip(sums, (first, second))
                    ]
                for s in range(2):
                    out_ref[s, level, i, rows] = sums[s].astype(BF16)


def conv_air_kernel(own_ref, even_ref, odd_ref, packed_ref, matrix_ref, *refs):
    out_refs, product_ref = refs[:-1], refs[-1]
    _, levels, band, count, _ = own_ref.shape
    depth = matrix_ref.shape[-1]
    lon = lax.axis_index("lon")
    inner = (lon & 1) == 1
    swap_west = jnp.where(lon == 0, 1, 0)
    swap_east = jnp.where(lon == lax.axis_size("lon") - 1, 1, 0)
    first_odd = pl.program_id(0) * count
    first_even = first_odd + even_ref.shape[0] - odd_ref.shape[0]

    stride = 3 * levels * out_refs[0].shape[3] * pl.num_programs(0)

    def tiles_at(half, tile):
        at = tile * (stride // (3 * levels))
        moved = half * stride
        return rim_tile(even_ref, odd_ref, first_even + moved + at, first_odd + moved + at, count)

    start = jnp.where(lax.axis_index("comp") == 0, 0, LANES - 8)
    wide = lane_ids(count)
    even, odd = tiles_at(0, 2 * levels * 3)
    edge_tiles = []
    for tile, swap in (
        (packed_ref[...], None),
        (jnp.where(inner, even, odd), swap_west),
        (jnp.where(inner, odd, even), swap_east),
    ):
        if swap is not None:
            span = 8 * band
            other = jnp.where(
                (wide & span) == 0, pltpu.roll(tile, LANES - span, 1), pltpu.roll(tile, span, 1)
            )
            tile = jnp.where(swap == 1, other, tile)
        edge_tiles.append(pltpu.roll(tile, start, 1))
    lane = lane_ids(8)
    block = ((lane - start + LANES) & (LANES - 1)) >> 3
    adjoining = (block == 0) | (block == band)
    all_tiles = []
    for h in range(2):
        west_h = jnp.abs(h - swap_west)
        east_h = jnp.abs(h - swap_east)
        tiles = []
        for level in range(levels):
            west, east = [], []
            for i in range(3):
                even, odd = tiles_at(west_h, level * 3 + i)
                west.append(jnp.where(inner, even, odd))
                even, odd = tiles_at(east_h, level * 3 + i)
                east.append(jnp.where(inner, odd, even))
            tiles += west + [own_ref[h, level, i].astype(F32) for i in range(band)] + east
        all_tiles.append(tiles)
    beyond = []
    for level in range(levels):
        first = level * 2 * band
        beyond += [(1, first + i + band - 3) for i in range(3)]
        beyond += [(0, first + i) for i in range(band)]
        beyond += [(2, first + i) for i in range(3)]
    for sub in range(count // 8):
        rows = slice(sub * 8, sub * 8 + 8)
        columns = [[tile[rows] for tile in tiles] for tiles in all_tiles]
        packed = [tile[rows] for tile in edge_tiles]
        columns.append(
            [
                jnp.where(adjoining, pltpu.roll(packed[who], -8 * idx % LANES, 1), 0.0)
                for who, idx in beyond
            ]
        )
        pad = depth - len(columns[0]) * 8
        if pad:
            columns = [tiles + [jnp.zeros((pad, LANES), F32)] for tiles in columns]
        data = jnp.concatenate(
            [jnp.concatenate(tiles, axis=0) for tiles in columns], axis=1
        ).astype(BF16)
        matrix = matrix_ref[sub].reshape(-1, depth)
        product_ref[sub % 2] = jnp.dot(matrix, data, preferred_element_type=F32)
        for level in range(levels):
            for i in range(band):
                base = ((i // 2 * levels + level) * 2 + i % 2) * TAPS
                sums = [None, None]
                for d in range(TAPS):
                    at = slice((base + d) * 8, (base + d) * 8 + 8)
                    off = d - 3
                    edge = product_ref[sub % 2, at, 2 * LANES :] if off else None
                    for h in range(2):
                        part = product_ref[sub % 2, at, h * LANES : (h + 1) * LANES]
                        if off:
                            here = edge if h == 0 else pltpu.roll(edge, LANES - 8 * band, 1)
                            inside = lane < off if off > 0 else lane >= LANES + off
                            part = pltpu.roll(jnp.where(inside, here, part), (LANES - off) % LANES, 1)
                        sums[h] = part if sums[h] is None else sums[h] + part
                for h in range(2):
                    out_refs[level][h, 0, i, rows] = sums[h].astype(BF16)


def convolution(kernel, name, own, even, odd, packed, matrix):
    _, levels, band, channels, _ = own.shape
    groups, pairs, rows, depth = matrix.shape
    count = 32
    lane_tiles = 2 if packed is None else 3
    grid_spec = pl.BlockSpec((2, levels, band, count, LANES), lambda g: (0, 0, 0, g, 0))
    args = [own, even, odd]
    specs = [grid_spec] + [pl.BlockSpec(rim.shape, lambda g: (0, 0)) for rim in (even, odd)]
    outs = [levels] if packed is None else [1] * levels
    if packed is not None:
        args.append(packed)
        specs.append(pl.BlockSpec((count, LANES), lambda g: (g, 0)))
    args.append(matrix)
    specs.append(pl.BlockSpec((count // 8, pairs, rows, depth), lambda g: (g, 0, 0, 0)))
    return pl.pallas_call(
        kernel,
        grid=(channels // count,),
        out_shape=[jax.ShapeDtypeStruct((2, part) + own.shape[2:], BF16) for part in outs],
        in_specs=specs,
        out_specs=[
            pl.BlockSpec((2, part, band, count, LANES), lambda g: (0, 0, 0, g, 0)) for part in outs
        ],
        scratch_shapes=[pltpu.VMEM((2, pairs * rows, lane_tiles * LANES), F32)],
        name=name,
        compiler_params=PARAMS,
        cost_estimate=pl.CostEstimate(flops=2 * 10**9, bytes_accessed=4 * 10**6, transcendentals=0),
    )(*args)


def flip_kernel(*refs):
    count = len(refs) // 2
    for source, target in zip(refs[:count], refs[count:]):
        target[...] = source[...].astype(F32).T.astype(BF16)


def mlp_kernel(masked, first_level, *refs):
    own_ref, other_ref, gain_ref, up_ref, down_ref, top_ref, forced_ref = refs[:7]
    extra_ref = refs[7] if len(refs) > 9 else None
    out_ref, values_ref = refs[-2:]
    _, levels, band, channels, _ = own_ref.shape
    ch = lax.axis_index("ch")
    total = 2 * channels
    gain = column(gain_ref[...])
    mine = pl.ds(pl.multiple_of(ch * channels, channels), channels)
    if not masked and extra_ref is not None:
        out_ref[:, :first_level] = extra_ref[...]
    theirs = pl.ds(pl.multiple_of((1 - ch) * channels, channels), channels)
    together = values_ref.shape[1] // (2 * LANES)
    if masked:
        sea = extra_ref[...].astype(F32)

    def step(at, carry):
        blocks = []
        for n in range(together):
            index = at * together + n
            spot = (index // band, lax.rem(index, band))
            if together % band == 0:
                spot = (at * (together // band) + n // band, n % band)
            for s in range(2):
                at_lane = (n * 2 + s) * LANES
                blocks.append((s, *spot, slice(at_lane, at_lane + LANES)))
        for s, level, i, lanes in blocks:
            values_ref[mine, lanes] = own_ref[s, level, i].astype(F32)
            values_ref[theirs, lanes] = other_ref[s, level, i].astype(F32)
        values = values_ref[...]
        center = jnp.sum(values, axis=0, keepdims=True) * (1.0 / total)
        values = values - center
        spread = jnp.sum(values * values, axis=0, keepdims=True) * (1.0 / total)
        normed = (values * lax.rsqrt(spread + 1e-06) * gain).astype(BF16)
        raw = jnp.dot(up_ref[...], normed, preferred_element_type=F32)
        inner = raw * (0.7978845608028654 + 0.035677408136300125 * (raw * raw))
        doubled = (raw + raw * jnp.tanh(inner)).astype(BF16)
        update = jnp.dot(down_ref[mine, :], doubled, preferred_element_type=F32) * 0.5
        update = update.astype(BF16).astype(F32)
        for s, level, i, lanes in blocks:
            if first_level:
                forced = forced_ref[s, first_level + level, i].astype(F32)
            else:
                forced = jnp.where(level == 0, top_ref[s, i], forced_ref[s, level, i].astype(F32))
            result = forced + update[:, lanes]
            if masked:
                half = sea[:, s * LANES : (s + 1) * LANES]
                picked = lax.broadcasted_iota(jnp.int32, half.shape, 0) == i
                result = result * jnp.sum(jnp.where(picked, half, 0.0), axis=0, keepdims=True)
            if masked:
                out_ref[level, i, :, s * LANES : (s + 1) * LANES] = result.astype(BF16)
            else:
                out_ref[s, first_level + level, i] = result.astype(BF16)
        return carry

    lax.fori_loop(0, levels * band // together, step, 0)


def toeplitz(ocean_kernel, air_kernel, o_levels, a_levels):
    taps = [jnp.transpose(kernel, (1, 2, 3, 0)) for kernel in (ocean_kernel, air_kernel)]
    shapes = [
        (part.shape[-1] // 8, levels, 2 * TAPS * 8, 256)
        for part, levels in zip(taps, (o_levels, a_levels))
    ]
    return pl.pallas_call(
        both_toeplitz_kernel,
        grid=(2,),
        out_shape=[
            jax.ShapeDtypeStruct((g, 2 * levels, rows, depth), BF16)
            for g, levels, rows, depth in shapes
        ],
        in_specs=[pl.BlockSpec(part.shape, lambda p: (0, 0, 0, 0)) for part in taps],
        out_specs=[pl.BlockSpec(block, lambda p: (0, p, 0, 0)) for block in shapes],
        scratch_shapes=[pltpu.VMEM((TAPS, LANES, LANES), F32)] * 2,
        name="matrix",
        compiler_params=PARAMS,
        cost_estimate=pl.CostEstimate(flops=2 * 10**9, bytes_accessed=6 * 10**6, transcendentals=0),
    )(*taps)


def pairs_of(count, first):
    pairs = []
    for i in range(first, count + first, 2):
        pairs += [(i % count, (i + 1) % count), ((i + 1) % count, i % count)]
    return pairs


def ring(count, step):
    return [(i, (i + step) % count) for i in range(count)]


def per_device(
    ocean_state, ocean_mask, air_state, surface_temp, air_fluxes, ocean_kernel, ocean_gain, ocean_up,
    ocean_down, air_kernel, air_gain, air_up, air_down, flux_weight, temp_weight,
):
    o_levels, o_ch, band, lats = ocean_state.shape
    a_levels, a_ch = air_state.shape[:2]
    fields = air_fluxes.shape[0]
    shape = jax.ShapeDtypeStruct

    air_grid = jnp.transpose(air_state, (3, 0, 2, 1, 4))
    o_grid = (2, o_levels, band, o_ch, LANES)
    a_grid = (2, a_levels, band, a_ch, LANES)

    lons = lax.axis_size("lon")
    bands = lax.axis_size("comp") * lons
    rows = rows_of(fields, band)[-1] + a_ch
    surface_args = (ocean_mask, surface_temp, air_fluxes)
    partner = 1 - lax.axis_index("comp")
    temp_rows = (surface_temp * ocean_mask.astype(F32)).reshape(band, 2, LANES)
    small = jnp.concatenate(
        [
            lax.dynamic_index_in_dim(air_fluxes, partner, 2, False).reshape(-1, LANES),
            jnp.transpose(temp_rows, (1, 0, 2)).reshape(-1, LANES),
        ]
    )
    packed = call(
        pack_kernel, shape((rows, LANES), F32), [], "pack", 10**5, 10**6, small, air_grid
    )
    got = lax.ppermute(packed, "comp", ring(2, 1))
    later_ocean, _ = lax.optimization_barrier((ocean_state, packed))
    ocean_grid = jnp.transpose(
        later_ocean.reshape(o_levels, o_ch, band, 2, LANES), (3, 0, 2, 1, 4)
    )
    ocean_grid, ocean_kernel = lax.optimization_barrier((ocean_grid, ocean_kernel))
    o_matrix, a_matrix = toeplitz(ocean_kernel, air_kernel, o_levels, a_levels)
    o_matrix, a_matrix, got = lax.optimization_barrier((o_matrix, a_matrix, got))
    o_rows = 2 * o_levels * 3 * o_ch
    a_rows = (2 * a_levels * 3 + 1) * a_ch
    surface = pltpu.VMEM((4 * band, LANES), F32)
    weights = (flux_weight, temp_weight.reshape(1, a_ch))
    even_out, odd_out_o, odd_out_a, edge = call(
        force_halo_kernel,
        (
            shape((o_rows + a_rows, LANES), BF16), shape((o_rows, LANES), BF16),
            shape((a_rows, LANES), BF16), shape((a_ch, LANES), F32),
        ),
        [surface], "force_halo", 10**6, 4 * 10**6,
        *surface_args, got, ocean_grid, air_grid, *weights,
    )
    even = lax.ppermute(even_out, "lon", pairs_of(lons, 0))
    odd_o = lax.ppermute(odd_out_o, ("comp", "lon"), pairs_of(bands, 1))
    odd_a = lax.ppermute(odd_out_a, "lon", pairs_of(lons, 1))
    ocean_top, air_top, ocean_forced, air_forced = call(
        force_own_kernel,
        (
            shape((2, band, o_ch, LANES), F32), shape((2, band, a_ch, LANES), F32),
            shape(o_grid, BF16), shape(a_grid, BF16),
        ),
        [surface], "force_own", 10**6, 4 * 10**6,
        *surface_args, got, ocean_grid, air_grid, *weights,
    )

    sources = (ocean_up, ocean_down, air_up)
    *sources, ocean_forced = lax.optimization_barrier((*sources, ocean_forced))
    o_wide, o_narrow, a_wide = call(
        flip_kernel, tuple(shape(part.shape[::-1], BF16) for part in sources), [], "flip",
        10**6, 10**6, *sources,
    )
    o_wide, o_narrow, a_wide, ocean_forced = lax.optimization_barrier(
        (o_wide, o_narrow, a_wide, ocean_forced)
    )
    (o_conv,) = convolution(conv_ocean_kernel, "conv_ocean", ocean_forced, even, odd_o, None, o_matrix)
    o_other = lax.ppermute(o_conv, "ch", ring(2, 1))
    a_convs = convolution(conv_air_kernel, "conv_air", air_forced, even, odd_a, edge, a_matrix)
    a_others = [lax.ppermute(part, "ch", ring(2, 1)) for part in a_convs]

    o_next = call(
        functools.partial(mlp_kernel, True, 0), shape((o_levels, band, o_ch, lats), BF16),
        [pltpu.VMEM((2 * o_ch, OCEAN_TOGETHER * 2 * LANES), F32)],
        "mlp_ocean", 10**9, 3 * 10**6,
        o_conv, o_other, ocean_gain.reshape(1, -1), o_wide, o_narrow, ocean_top, ocean_forced,
        ocean_mask,
    )
    done = []
    a_convs, o_next = lax.optimization_barrier((a_convs, o_next))
    for level, (part, other) in enumerate(zip(a_convs, a_others)):
        a_next = call(
            functools.partial(mlp_kernel, False, level),
            shape((2, level + 1) + a_grid[2:], BF16),
            [pltpu.VMEM((2 * a_ch, TOGETHER * 2 * LANES), F32)],
            f"mlp_air{level}", 10**9, 3 * 10**6,
            part, other, air_gain.reshape(1, -1), a_wide, air_down.T, air_top, air_forced, *done,
        )
        done = [a_next]
    ocean_next = jnp.transpose(o_next, (0, 2, 1, 3))
    air_next = jnp.transpose(a_next, (1, 3, 2, 0, 4))
    return (ocean_next, air_next)


def solution(mesh):
    in_specs = (
        P(None, "ch", ("comp", "lon"), None),
        P(("comp", "lon"), None),
        P(None, "ch", "lon", None, "comp"),
        P(("comp", "lon"), None),
        P(None, "lon", None, "comp"),
        P("ch", None, None, None),
        P(),
        P(),
        P(),
        P("ch", None, None, None),
        P(),
        P(),
        P(),
        P(None, "ch"),
        P("ch"),
    )
    out_specs = (P(None, "ch", ("comp", "lon"), None), P(None, "ch", "lon", None, "comp"))
    return jax.shard_map(
        per_device, mesh=mesh, in_specs=in_specs, out_specs=out_specs, check_vma=False
    )
```
